32 devices in a mesh: dp: 32 (over z, y, x, core).
Axes of the slice: x: 2, y: 2, z: 4, core: 2. Of those that a mesh axis runs over, the one named last changes fastest.
Arguments:
- tokens: bfloat16 [32768, 768], P('dp'), may hold values from -6 to 6
- segment_ids: int32 [32768], P('dp'), may hold values from 0 to 10, as said below
- random_blocks: int32 [12, 6, 3], replicated, may hold values from 1 to 6, as said below
- clip_limit: int32 [1], replicated, may hold values from 6 to 12
- query_weight: bfloat16 [768, 768], P('dp'), may hold values from -1 to 1
- query_bias: bfloat16 [768], P('dp'), may hold values from -1 to 1
- key_weight: bfloat16 [768, 768], P('dp'), may hold values from -0.21875 to 0.21875
- value_weight: bfloat16 [768, 768], P('dp'), may hold values from -0.21875 to 0.21875
- value_bias: bfloat16 [768], P('dp'), may hold values from -1 to 1
- output_weight: bfloat16 [768, 768], P('dp'), may hold values from -1.25 to 1.25
- output_bias: bfloat16 [768], P('dp'), may hold values from -1 to 1
- attn_gain: bfloat16 [768], P('dp'), may hold values from 0.5 to 1.5
- attn_shift: bfloat16 [768], P('dp'), may hold values from -1 to 1
- inner_weight: bfloat16 [768, 3072], P('dp'), may hold values from -0.21875 to 0.21875
- inner_bias: bfloat16 [3072], P('dp'), may hold values from -1 to 1
- outer_weight: bfloat16 [3072, 768], P('dp'), may hold values from -0.15625 to 0.15625
- outer_bias: bfloat16 [768], P('dp'), may hold values from -1 to 1
- final_gain: bfloat16 [768], P('dp'), may hold values from 0.5 to 1.5
- final_shift: bfloat16 [768], P('dp'), may hold values from -1 to 1
- out_cotangent: bfloat16 [32768, 768], P('dp'), may hold values from -6 to 6
Outputs:
- layer_out: bfloat16 [32768, 768], P('dp')
- token_gradient: float32 [32768, 768], P('dp')
- query_weight_gradient: float32 [768, 768], P('dp')
- query_bias_gradient: float32 [768], P('dp')
- key_weight_gradient: float32 [768, 768], P('dp')
- value_weight_gradient: float32 [768, 768], P('dp')
- value_bias_gradient: float32 [768], P('dp')
- output_weight_gradient: float32 [768, 768], P('dp')
- output_bias_gradient: float32 [768], P('dp')
- attn_gain_gradient: float32 [768], P('dp')
- attn_shift_gradient: float32 [768], P('dp')
- inner_weight_gradient: float32 [768, 3072], P('dp')
- inner_bias_gradient: float32 [3072], P('dp')
- outer_weight_gradient: float32 [3072, 768], P('dp')
- outer_bias_gradient: float32 [768], P('dp')
- final_gain_gradient: float32 [768], P('dp')
- final_shift_gradient: float32 [768], P('dp')
- clipped_query: bfloat16 [768, 768], P('dp')
- clipped_key: bfloat16 [768, 768], P('dp')
- head_maxima: float32 [12], replicated
The draws below stay inside these ranges and needn't reach their ends.
Inputs may be any that keep to these rules, and one draw needn't show every extreme that they name: `segment_ids`: within each sequence of 512 tokens the numbers never fall up to a final run of 1 to 128 tokens with number 0; every other number covers 60 to 480 consecutive tokens, except the last one before the final run, which may be shorter and always has the number 512 // 60 + 2; consecutive documents have consecutive numbers. `random_blocks`: row i - 1 of a head lists 3 different blocks for middle query block i, none of them 0, 7, i - 1, i or i + 1.
All inputs are finite; a program needn't handle non-finite values.
Results may differ from the reference program's by a relative error of at most 0.015.
The reference program's roundings to bfloat16 on the way count: a program that leaves them out, or rounds other values in their place, can miss the bound.
Values may be sent and summed in bfloat16 or wider, within the bound.
A program may use at most 384 MiB of HBM per device.

```python
import math
import jax
import jax.numpy as jnp
from jax import lax

D = 768
H = 12
HD = 64
FF = 3072
BLOCK = 64
RAND = 3
SEQ = 512
DOC_LOW = 60
DOC_HIGH = 480
TOKENS = 32768


def draw_segment_ids(key, part):
    seq_count = TOKENS // SEQ
    doc_slots = SEQ // DOC_LOW + 1
    lengths = jax.random.randint(jax.random.fold_in(key, 11), (seq_count, doc_slots), DOC_LOW, DOC_HIGH + 1, dtype=jnp.int32)
    doc_ends = jnp.cumsum(lengths, axis=1)
    places = jnp.arange(SEQ, dtype=jnp.int32)
    numbers = 1 + jnp.sum((places[None, :, None] >= doc_ends[:, None, :]).astype(jnp.int32), axis=2)
    tail_size = jax.random.randint(jax.random.fold_in(key, 12), (seq_count, 1), 1, 2 * BLOCK + 1, dtype=jnp.int32)
    live = places[None, :] < SEQ - tail_size
    last_number = jnp.max(jnp.where(live, numbers, 0), axis=1, keepdims=True)
    top_number = SEQ // DOC_LOW + 2
    numbers = jnp.where(live, numbers + (top_number - last_number), 0)
    return numbers.reshape(TOKENS).astype(jnp.int32)


def draw_random_blocks(key, part):
    block_total = SEQ // BLOCK
    row_blocks = jnp.arange(1, block_total - 1, dtype=jnp.int32)[:, None]
    blocks = jnp.arange(block_total, dtype=jnp.int32)[None, :]
    scores = jax.random.randint(jax.random.fold_in(key, 21), (H, block_total - 2, block_total), 0, 4096, dtype=jnp.int32) * block_total + blocks
    barred = (blocks == 0) | (blocks == block_total - 1) | (jnp.abs(blocks - row_blocks) <= 1)
    scores = jnp.where(barred[None], -1 - blocks[None], scores)
    return lax.top_k(scores, RAND)[1].astype(jnp.int32)


def draw_query_weight(key, part):
    base_draw = jnp.clip(jax.random.normal(jax.random.fold_in(key, 31), (D, D), jnp.float32), -4.0, 4.0)
    head_order = jax.random.permutation(jax.random.fold_in(key, 32), H).astype(jnp.float32)
    ladder = 3.0 ** (head_order / (H - 1))
    return (base_draw * jnp.repeat(ladder, HD)[None, :] * D ** (-0.5)).astype(jnp.bfloat16)


def with_spikes(values, key, source, target, blocks, factor):
    def block_of(axis_at):
        return (jnp.arange(values.shape[axis_at]) // (values.shape[axis_at] // blocks)).reshape((-1,) + (1,) * (values.ndim - 1 - axis_at))

    first = jax.random.permutation(key, blocks)[block_of(target)]
    far = (block_of(target) + blocks // 2) % blocks
    return jnp.where((block_of(source) == first) | (block_of(source) == far), factor * values, values)


def levels(key, dims, cuts, smallest, top_value):
    def one(position, shards_of):
        heights = jax.random.uniform(jax.random.fold_in(jax.random.fold_in(key, 6), position), (shards_of,), jnp.float32, smallest / len(cuts), top_value / len(cuts))
        return jnp.repeat(jnp.exp(heights), dims[position] // shards_of).reshape((-1,) + (1,) * (len(dims) - position - 1))

    factor_of = one(*cuts[0])
    for cut in cuts[1:]:
        factor_of = factor_of * one(*cut)
    return factor_of


def bell_draw(rng, dims, width, bound, split=(), kind=jnp.bfloat16):
    array = jax.random.normal(rng, dims, jnp.float32) * width
    if len(split) > 0:
        array = levels(rng, dims, split, -0.22, 0.18) * array
    return jnp.clip(array, min=-bound, max=bound).astype(kind)


def noise_with(key, extent, scale, reach, pieces, heavy, kind=jnp.bfloat16):
    entries = scale * jax.random.normal(key, extent, jnp.float32)
    if pieces:
        entries = entries * levels(key, extent, pieces, -0.22, 0.18)
    return jnp.clip(with_spikes(entries, jax.random.fold_in(key, 3), *heavy), -reach, reach).astype(kind)


def setup_inputs(seed: int = 0) -> dict:
    arg_keys = jax.random.split(jax.random.key(seed), 21)
    return {
        "tokens": bell_draw(arg_keys[0], (TOKENS, D), 1.0, 6.0, ((0, 32),)),
        "segment_ids": draw_segment_ids(jax.random.fold_in(arg_keys[20], 71), 0),
        "random_blocks": draw_random_blocks(jax.random.fold_in(arg_keys[20], 71), 0),
        "clip_limit": jax.random.randint(arg_keys[3], (1,), 6, 13).astype(jnp.int32),
        "query_weight": draw_query_weight(jax.random.fold_in(arg_keys[20], 71), 0),
        "query_bias": bell_draw(arg_keys[5], (D,), 0.2, 1.0, ((0, 32),)),
        "key_weight": bell_draw(arg_keys[6], (D, D), D ** -0.5, 0.21875, ((0, 32),)),
        "value_weight": bell_draw(arg_keys[7], (D, D), D ** -0.5, 0.21875, ((0, 32),)),
        "value_bias": bell_draw(arg_keys[8], (D,), 0.2, 1.0, ((0, 32),)),
        "output_weight": bell_draw(arg_keys[9], (D, D), (D // 32) ** -0.5, 1.25, ((0, 32),)),
        "output_bias": bell_draw(arg_keys[10], (D,), 0.2, 1.0, ((0, 32),)),
        "attn_gain": jnp.clip(1.0 + 0.1 * jax.random.normal(arg_keys[11], (D,), jnp.float32), 0.5, 1.5).astype(jnp.bfloat16),
        "attn_shift": bell_draw(arg_keys[12], (D,), 0.2, 1.0, ((0, 32),)),
        "inner_weight": bell_draw(arg_keys[13], (D, FF), D ** -0.5, 0.21875, ((0, 32),)),
        "inner_bias": bell_draw(arg_keys[14], (FF,), 0.2, 1.0, ((0, 32),)),
        "outer_weight": bell_draw(arg_keys[15], (FF, D), (FF // 2) ** -0.5, 0.15625, ((0, 32),)),
        "outer_bias": bell_draw(arg_keys[16], (D,), 0.2, 1.0, ((0, 32),)),
        "final_gain": jnp.clip(1.0 + 0.1 * jax.random.normal(arg_keys[17], (D,), jnp.float32), 0.5, 1.5).astype(jnp.bfloat16),
        "final_shift": bell_draw(arg_keys[18], (D,), 0.2, 1.0, ((0, 32),)),
        "out_cotangent": noise_with(arg_keys[19], (TOKENS, D), 1.0, 6.0, ((0, 32),), (0, 1, 32, 2.75)),
    }


@jax.custom_vjp
def low(v):
    return lax.optimization_barrier(v.astype(jnp.bfloat16)).astype(jnp.float32)

@jax.custom_vjp
def low_back(v):
    return v

def low_keep(v):
    return (low(v), None)

def low_pass(kept, grad):
    return (grad,)

def back_keep(v):
    return (v, None)

def back_low(kept, grad):
    return (low(grad),)
low.defvjp(low_keep, low_pass)
low_back.defvjp(back_keep, back_low)

def matmul(left_side, right_side):
    return jnp.dot(left_side, right_side, precision=lax.Precision.HIGHEST, preferred_element_type=jnp.float32)

def normalize(summed_rows, gain_vec, shift_vec):
    row_mean = lax.optimization_barrier(jnp.mean(summed_rows, axis=-1, keepdims=True))
    centered = summed_rows - row_mean
    row_var = lax.optimization_barrier(jnp.mean(centered * centered, axis=-1, keepdims=True))
    return centered * lax.rsqrt(row_var + 1e-12) * gain_vec + shift_vec

def block_pattern(random_blocks):
    block_total = SEQ // BLOCK
    blocks = jnp.arange(block_total, dtype=jnp.int32)
    picked = jnp.any(random_blocks[:, :, :, None] == blocks[None, None, None, :], axis=2)
    empty_row = jnp.zeros((H, 1, block_total), dtype=bool)
    picked = jnp.concatenate([empty_row, picked, empty_row], axis=1)
    row_block = blocks[:, None]
    col_block = blocks[None, :]
    fixed_blocks = (jnp.abs(row_block - col_block) <= 1) | (row_block == 0) | (row_block == block_total - 1) | (col_block == 0) | (col_block == block_total - 1)
    pattern = picked | fixed_blocks[None]
    return jnp.repeat(jnp.repeat(pattern, BLOCK, axis=1), BLOCK, axis=2)

def sequence_layer(flat_rows, seg_rows, pattern, params):
    query_full, query_lift, key_full, value_full, value_lift, output_full, output_lift, attn_scale, attn_offset, inner_full, inner_lift, outer_full, outer_lift, final_scale, final_offset = params
    groups = seg_rows.shape[0]
    shape_four = (groups, SEQ, H, HD)
    queries = low(low_back(matmul(flat_rows, query_full) + query_lift))
    key_rows = low(low_back(matmul(flat_rows, key_full)))
    values = low(low_back(matmul(flat_rows, value_full) + value_lift))
    logits = low_back(jnp.einsum('gqhd,gkhd->ghqk', queries.reshape(shape_four), key_rows.reshape(shape_four), precision=lax.Precision.HIGHEST) * (1.0 / math.sqrt(HD)))
    same_doc = (seg_rows[:, :, None] == seg_rows[:, None, :]) & (seg_rows[:, None, :] != 0)
    allowed = pattern[None] & same_doc[:, None]
    masked = jnp.where(allowed, logits, -1e+30)
    row_top = lax.optimization_barrier(jnp.max(masked, axis=-1, keepdims=True))
    row_live = jnp.any(allowed, axis=-1, keepdims=True)
    row_base = jnp.where(row_live, row_top, 0.0)
    weights = jnp.exp(jnp.where(allowed, logits - row_base, -1e+30))
    row_total = lax.optimization_barrier(jnp.sum(weights, axis=-1, keepdims=True)) + jnp.where(row_live, 0.0, 1.0)
    probs_low = low(weights / row_total)
    context = jnp.einsum('ghqk,gkhd->gqhd', probs_low, values.reshape(shape_four), precision=lax.Precision.HIGHEST)
    context = low(low_back(context.reshape(groups * SEQ, D)))
    branch = low_back(matmul(context, output_full) + output_lift)
    first_norm = normalize(flat_rows + branch, attn_scale, attn_offset)
    inner = low_back(matmul(low(first_norm), inner_full) + inner_lift)
    outer = low_back(matmul(low(jax.nn.gelu(inner, approximate=True)), outer_full) + outer_lift)
    result = normalize(first_norm + outer, final_scale, final_offset)
    head_top = lax.optimization_barrier(jnp.max(jnp.where(row_live, row_top, -1e+30)[..., 0], axis=(0, 2)))
    return (result, head_top)

def reference(tokens, segment_ids, random_blocks, clip_limit, query_weight, query_bias, key_weight, value_weight, value_bias, output_weight, output_bias, attn_gain, attn_shift, inner_weight, inner_bias, outer_weight, outer_bias, final_gain, final_shift, out_cotangent):
    params = tuple((item.astype(jnp.float32) for item in (query_weight, query_bias, key_weight, value_weight, value_bias, output_weight, output_bias, attn_gain, attn_shift, inner_weight, inner_bias, outer_weight, outer_bias, final_gain, final_shift)))
    token_values = tokens.astype(jnp.float32)
    pattern = block_pattern(random_blocks)
    seq_count = tokens.shape[0] // SEQ
    group_size = math.gcd(seq_count, max(1, 2048 // SEQ))
    step_count = seq_count // group_size
    grouped_segs = segment_ids.reshape(step_count, group_size, SEQ)
    checked_layer = jax.checkpoint(sequence_layer)

    def forward(flat_rows, layer_params):
        grouped_rows = flat_rows.reshape(step_count, group_size * SEQ, D)

        def one_group(running_top, group_item):
            group_out, group_top = checked_layer(group_item[0], group_item[1], pattern, layer_params)
            return (jnp.maximum(running_top, group_top), group_out)
        start_top = jnp.full((H,), -1e+30, dtype=jnp.float32)
        head_top, group_outs = lax.scan(one_group, start_top, (grouped_rows, grouped_segs))
        return (group_outs.reshape(seq_count * SEQ, D), head_top)
    layer_out, pullback, head_maxima = jax.vjp(forward, token_values, params, has_aux=True)
    token_gradient, grads = pullback(out_cotangent.astype(jnp.float32))
    limit_value = clip_limit[0].astype(jnp.float32)
    factor = jnp.sqrt(jnp.minimum(1.0, limit_value / jnp.maximum(head_maxima, 1.0)))
    columns = jnp.repeat(factor, HD)[None, :]
    clipped_query = (query_weight.astype(jnp.float32) * columns).astype(jnp.bfloat16)
    clipped_key = (key_weight.astype(jnp.float32) * columns).astype(jnp.bfloat16)
    return (layer_out.astype(jnp.bfloat16), token_gradient, grads[0], grads[1], grads[2], grads[3], grads[4], grads[5], grads[6], grads[7], grads[8], grads[9], grads[10], grads[11], grads[12], grads[13], grads[14], clipped_query, clipped_key, head_maxima)
```

```python
from functools import partial
import math

import jax
import jax.numpy as jnp
from jax import lax
from jax.experimental import pallas as pl
from jax.experimental.pallas import tpu as pltpu
from jax.sharding import PartitionSpec as P

HD = 64
BLOCK = 64
SEQ = 512
BF = jnp.bfloat16
F32 = jnp.float32
LOW = -1e30
VMEM_MAX = 67043328


def dot(a, b):
    return jnp.dot(a, b, preferred_element_type=F32)


def dot_nt(a, b):
    return lax.dot_general(a, b, (((1,), (1,)), ((), ())), preferred_element_type=F32)


def dot_tn(a, b):
    return lax.dot_general(a, b, (((0,), (0,)), ((), ())), preferred_element_type=F32)


def attn_fwd_body(rb, x, segr, segc, wq, wk, wv, wo, qb, vb, ob,
                  q_o, k_o, v_o, p_o, c_o, z_o, hm_o, bias, s_s):
    g = pl.program_id(0)
    seqs = segr.shape[0]
    pairs = wq.shape[1] // 128

    @pl.when(g == 0)
    def _():
        for s in range(seqs):
            kseg = segr[s:s + 1, :]
            for c in range(SEQ // BLOCK):
                qseg = segc[s * SEQ + c * BLOCK:s * SEQ + (c + 1) * BLOCK, :]
                bias[s, c * BLOCK:(c + 1) * BLOCK, :] = jnp.where((qseg == kseg) & (kseg != 0), 0.0, LOW)
        hm_o[...] = jnp.full(hm_o.shape, LOW, F32)
        z_o[...] = x[...].astype(F32) + ob[...].astype(F32)

    xv = x[...]
    q_o[...] = (dot(xv, wq[...]) + qb[...].astype(F32)).astype(BF)
    k_o[...] = dot(xv, wk[...]).astype(BF)
    v_o[...] = (dot(xv, wv[...]) + vb[...].astype(F32)).astype(BF)

    lane_block = lax.broadcasted_iota(jnp.int32, (1, SEQ), 1) // BLOCK
    first_half = lax.broadcasted_iota(jnp.int32, (1, 128), 1) < HD
    last = SEQ // BLOCK - 2

    def one_pair(it, _):
        s = it // pairs
        pair = it % pairs
        rows = pl.ds(pl.multiple_of(s * SEQ, SEQ), SEQ)
        lanes = pl.ds(pl.multiple_of(pair * 128, 128), 128)
        qp = q_o[rows, lanes]
        kp = k_o[rows, lanes]
        vp = v_o[rows, lanes]
        outs = []
        for j in range(2):
            head = g * (2 * pairs) + pair * 2 + j
            mine = first_half if j == 0 else jnp.logical_not(first_half)
            s_s[j] = dot_nt(jnp.where(mine, qp * 0.125, 0).astype(BF), kp)
            at = head * (6 * 3)
            miss1 = 18 - (rb[at] + rb[at + 1] + rb[at + 2])
            miss6 = 10 - (rb[at + 15] + rb[at + 16] + rb[at + 17])
            skip1 = jnp.where(lane_block == miss1, LOW, 0.0)
            skip6 = jnp.where(lane_block == miss6, LOW, 0.0)
            tops = None
            for c in range(SEQ // BLOCK):
                cr = slice(c * BLOCK, (c + 1) * BLOCK)
                sv = s_s[j, cr, :] + bias[s, cr, :]
                if c == 1:
                    sv = sv + skip1
                if c == last:
                    sv = sv + skip6
                top = jnp.max(sv, axis=1, keepdims=True)
                live = top > -1e29
                e = jnp.exp(sv - jnp.where(live, top, 0.0))
                total = jnp.sum(e, axis=1, keepdims=True) + jnp.where(live, 0.0, 1.0)
                p_o[s * (2 * pairs) + pair * 2 + j, cr, :] = (e * (1.0 / total)).astype(BF)
                tops = top if tops is None else jnp.maximum(tops, top)
            hm = jnp.max(tops, axis=0, keepdims=True)
            hm_o[pl.ds(head, 1), :] = jnp.maximum(hm_o[pl.ds(head, 1), :], hm)
            outs.append(dot(p_o[s * (2 * pairs) + pair * 2 + j], vp))
        c_o[rows, lanes] = jnp.where(first_half, outs[0], outs[1]).astype(BF)
        return 0

    lax.fori_loop(0, seqs * pairs, one_pair, 0)
    z_o[...] += dot(c_o[...], wo[...])


def attn_fwd(rb, x, segr, segc, wq, wk, wv, wo, qb, vb, ob):
    rows, d = x.shape
    seqs = rows // SEQ
    gw = 256
    groups = d // gw
    maps = seqs * (gw // HD)
    full = lambda shape: pl.BlockSpec(shape, lambda g, *_: (0,) * len(shape))
    col = pl.BlockSpec((d, gw), lambda g, *_: (0, g))
    vec = pl.BlockSpec((1, gw), lambda g, *_: (0, g))
    act = pl.BlockSpec((rows, gw), lambda g, *_: (0, g))
    return pl.pallas_call(
        attn_fwd_body,
        grid_spec=pltpu.PrefetchScalarGridSpec(
            num_scalar_prefetch=1, grid=(groups,),
            in_specs=[full((rows, d)), full((seqs, SEQ)), full((rows, 1)), col, col, col,
                      pl.BlockSpec((gw, d), lambda g, *_: (g, 0)), vec, vec, full((1, d))],
            out_specs=[act, act, act, pl.BlockSpec((maps, SEQ, SEQ), lambda g, *_: (g, 0, 0)), act,
                       full((rows, d)), full((16, 128))],
            scratch_shapes=[pltpu.VMEM((seqs, SEQ, SEQ), F32), pltpu.VMEM((2, SEQ, SEQ), F32)]),
        out_shape=[jax.ShapeDtypeStruct((rows, d), BF)] * 3
        + [jax.ShapeDtypeStruct((groups * maps, SEQ, SEQ), BF), jax.ShapeDtypeStruct((rows, d), BF),
           jax.ShapeDtypeStruct((rows, d), F32), jax.ShapeDtypeStruct((16, 128), F32)],
        compiler_params=pltpu.CompilerParams(vmem_limit_bytes=VMEM_MAX),
        name="attn_fwd",
    )(rb, x, segr, segc, wq, wk, wv, wo, qb, vb, ob)


def unit_rows(z):
    mean = jnp.mean(z, axis=-1, keepdims=True)
    c = z - mean
    inv = lax.rsqrt(jnp.mean(c * c, axis=-1, keepdims=True) + 1e-12)
    return c * inv, inv


def norm_back(up, unit, inv, gain):
    e = up * gain
    spread = jnp.mean(e, axis=-1, keepdims=True)
    along = jnp.mean(e * unit, axis=-1, keepdims=True)
    return inv * (e - spread - unit * along)


def col_sum(v):
    return jnp.sum(v, axis=0, keepdims=True)


def ffn_body(z, cot, wi, wo, bi, bo, ag, ash, fg, fs,
             out, dsum, db, dwi, dwo, dbi, small, fl, act, gp, acc, do):
    rows, d = z.shape
    ff = wi.shape[1]
    rt, ct, et = 512, 512, 128
    k0, k1 = math.sqrt(2.0 / math.pi), 0.044715
    agv, ashv = ag[...].astype(F32), ash[...].astype(F32)
    fgv, fsv, bov = fg[...].astype(F32), fs[...].astype(F32), bo[...].astype(F32)

    def prep(i, _):
        r = pl.ds(pl.multiple_of(i * et, et), et)
        unit, _inv = unit_rows(z[r, :])
        first = unit * agv + ashv
        fl[r, :] = first.astype(BF)
        acc[r, :] = first + bov
        return 0

    lax.fori_loop(0, rows // et, prep, 0)

    def up(i, _):
        r = pl.ds(pl.multiple_of((i % (rows // rt)) * rt, rt), rt)
        c = pl.ds(pl.multiple_of((i // (rows // rt)) * ct, ct), ct)
        u = dot(fl[r, :], wi[:, c]) + bi[:, c].astype(F32)
        u2 = u * u
        t = jnp.tanh(u * (k0 + (k0 * k1) * u2))
        h = 0.5 + 0.5 * t
        a = (u * h).astype(BF)
        act[r, c] = a
        gp[r, c] = (h + (0.5 * u) * (1.0 - t * t) * (k0 + (3.0 * k0 * k1) * u2)).astype(gp.dtype)
        acc[r, :] += dot(a, wo[c, :])
        return 0

    lax.fori_loop(0, (ff // ct) * (rows // rt), up, 0)

    small[...] = jnp.zeros(small.shape, F32)

    def mid(i, _):
        r = pl.ds(pl.multiple_of(i * et, et), et)
        unit, inv = unit_rows(acc[r, :])
        out[r, :] = (unit * fgv + fsv).astype(BF)
        upv = cot[r, :].astype(F32)
        small[0:1, :] += col_sum(upv * unit)
        small[1:2, :] += col_sum(upv)
        ds = norm_back(upv, unit, inv, fgv)
        dsl = ds.astype(BF)
        do[r, :] = dsl
        acc[r, :] = ds
        small[2:3, :] += col_sum(dsl.astype(F32))
        return 0

    lax.fori_loop(0, rows // et, mid, 0)

    def down(j, _):
        c = pl.ds(pl.multiple_of(j * ct, ct), ct)
        dwo[c, :] = dot_tn(act[:, c], do[...]).astype(dwo.dtype)
        sums = None
        for i in range(rows // rt):
            r = slice(i * rt, (i + 1) * rt)
            di = dot_nt(do[r, :], wo[c, :]) * gp[r, c].astype(F32)
            dil = di.astype(BF)
            act[r, c] = dil
            s = col_sum(dil.astype(F32))
            sums = s if sums is None else sums + s
            acc[r, :] += dot_nt(dil, wi[:, c])
        dbi[:, c] = sums
        dwi[:, c] = dot_tn(fl[...], act[:, c]).astype(dwi.dtype)
        return 0

    lax.fori_loop(0, ff // ct, down, 0)

    def tail(i, _):
        r = pl.ds(pl.multiple_of(i * et, et), et)
        unit, inv = unit_rows(z[r, :])
        df = acc[r, :]
        small[3:4, :] += col_sum(df * unit)
        small[4:5, :] += col_sum(df)
        ds = norm_back(df, unit, inv, agv)
        dsum[r, :] = ds
        dsl = ds.astype(BF)
        db[r, :] = dsl
        small[5:6, :] += col_sum(dsl.astype(F32))
        return 0

    lax.fori_loop(0, rows // et, tail, 0)


def ffn(z, cot, wi, wo, bi, bo, ag, ash, fg, fs, gdt):
    rows, d = z.shape
    ff = wi.shape[1]
    sd = jax.ShapeDtypeStruct
    vm = pl.BlockSpec(memory_space=pltpu.VMEM)
    return pl.pallas_call(
        ffn_body,
        in_specs=[vm] * 10,
        out_specs=[vm] * 7,
        out_shape=[sd((rows, d), BF), sd((rows, d), F32), sd((rows, d), BF), sd((d, ff), gdt), sd((ff, d), gdt),
                   sd((1, ff), F32), sd((8, d), F32)],
        scratch_shapes=[pltpu.VMEM((rows, d), BF), pltpu.VMEM((rows, ff), BF), pltpu.VMEM((rows, ff), BF),
                        pltpu.VMEM((rows, d), F32), pltpu.VMEM((rows, d), BF)],
        compiler_params=pltpu.CompilerParams(vmem_limit_bytes=VMEM_MAX),
        name="ffn",
    )(z, cot, wi, wo, bi, bo, ag, ash, fg, fs)


def attn_bwd_body(x, db, wq, wk, wv, wo, q, k, v, p, ctx, dsum,
                  dwq, dwk, dwv, dwo, dqb, dvb, dx, dc, dq, dk, dv, dp_s, ds_s):
    g = pl.program_id(0)
    seqs = x.shape[0] // SEQ
    pairs = wq.shape[1] // 128

    @pl.when(g == 0)
    def _():
        dx[...] = dsum[...]

    dbv = db[...]
    dc[...] = dot_nt(dbv, wo[...]).astype(BF)
    dwo[...] = dot_tn(ctx[...], dbv).astype(dwo.dtype)
    first_half = lax.broadcasted_iota(jnp.int32, (1, 128), 1) < HD

    def one_pair(it, _):
        s = it // pairs
        pair = it % pairs
        rows = pl.ds(pl.multiple_of(s * SEQ, SEQ), SEQ)
        lanes = pl.ds(pl.multiple_of(pair * 128, 128), 128)
        qp, kp, vp, dcp = q[rows, lanes], k[rows, lanes], v[rows, lanes], dc[rows, lanes]
        dqs, dks, dvs = [], [], []
        for j in range(2):
            mine = first_half if j == 0 else jnp.logical_not(first_half)
            m = s * (2 * pairs) + pair * 2 + j
            dp_s[j] = dot_nt(jnp.where(mine, dcp, 0).astype(BF), vp)
            for c in range(SEQ // BLOCK):
                cr = slice(c * BLOCK, (c + 1) * BLOCK)
                pv = p[m, cr, :].astype(F32)
                sl = dp_s[j, cr, :]
                mean = jnp.sum(pv * sl, axis=1, keepdims=True)
                ds_s[j, cr, :] = (pv * (sl - mean)).astype(BF)
            dqs.append(dot(ds_s[j], kp))
            dks.append(dot_tn(ds_s[j], qp))
            dvs.append(dot_tn(p[m], dcp))
        dq[rows, lanes] = (jnp.where(first_half, dqs[0], dqs[1]) * 0.125).astype(BF)
        dk[rows, lanes] = (jnp.where(first_half, dks[0], dks[1]) * 0.125).astype(BF)
        dv[rows, lanes] = jnp.where(first_half, dvs[0], dvs[1]).astype(BF)
        return 0

    lax.fori_loop(0, seqs * pairs, one_pair, 0)
    dqb[...] = col_sum(dq[...].astype(F32))
    dvb[...] = col_sum(dv[...].astype(F32))
    xv = x[...]
    dwq[...] = dot_tn(xv, dq[...]).astype(dwq.dtype)
    dwk[...] = dot_tn(xv, dk[...]).astype(dwk.dtype)
    dwv[...] = dot_tn(xv, dv[...]).astype(dwv.dtype)
    dx[...] += dot_nt(dq[...], wq[...]) + dot_nt(dk[...], wk[...]) + dot_nt(dv[...], wv[...])


def attn_bwd(x, db, wq, wk, wv, wo, q, k, v, p, ctx, dsum, gdt):
    rows, d = x.shape
    seqs = rows // SEQ
    gw = 256
    groups = d // gw
    maps = seqs * (gw // HD)
    full = lambda shape: pl.BlockSpec(shape, lambda g: (0,) * len(shape), pipeline_mode=pl.Buffered(1))
    col = pl.BlockSpec((d, gw), lambda g: (0, g))
    row = pl.BlockSpec((gw, d), lambda g: (g, 0))
    vec = pl.BlockSpec((1, gw), lambda g: (0, g))
    act = pl.BlockSpec((rows, gw), lambda g: (0, g))
    sd = jax.ShapeDtypeStruct
    return pl.pallas_call(
        attn_bwd_body,
        grid=(groups,),
        in_specs=[full((rows, d)), full((rows, d)), col, col, col, row, act, act, act,
                  pl.BlockSpec((maps, SEQ, SEQ), lambda g: (g, 0, 0)), act, full((rows, d))],
        out_specs=[col, col, col, row, vec, vec, pl.BlockSpec((rows, d), lambda g: (0, 0))],
        out_shape=[sd((d, d), gdt)] * 4 + [sd((1, d), F32)] * 2 + [sd((rows, d), F32)],
        scratch_shapes=[pltpu.VMEM((rows, gw), BF)] * 4
        + [pltpu.VMEM((2, SEQ, SEQ), F32), pltpu.VMEM((2, SEQ, SEQ), BF)],
        compiler_params=pltpu.CompilerParams(vmem_limit_bytes=VMEM_MAX),
        name="attn_bwd",
    )(x, db, wq, wk, wv, wo, q, k, v, p, ctx, dsum)


def per_device(tokens, segment_ids, random_blocks, clip_limit, query_weight, query_bias, key_weight, value_weight,
               value_bias, output_weight, output_bias, attn_gain, attn_shift, inner_weight, inner_bias,
               outer_weight, outer_bias, final_gain, final_shift, out_cotangent):
    heads = random_blocks.shape[0]
    rows, d = tokens.shape
    gather = lambda a: lax.all_gather(a, "dp", axis=0, tiled=True)
    wq, wk, wv, wo = map(gather, (query_weight, key_weight, value_weight, output_weight))
    wi, wu = gather(inner_weight), gather(outer_weight)
    names = (query_bias, value_bias, output_bias, attn_gain, attn_shift, outer_bias, final_gain, final_shift)
    part = query_bias.shape[0]
    vecs = gather(jnp.concatenate(names + (inner_bias,))[None])
    n = vecs.shape[0]
    qb, vb, ob, ag, ash, bo, fg, fs = (vecs[:, i * part:(i + 1) * part].reshape(1, n * part) for i in range(8))
    bi = vecs[:, 8 * part:].reshape(1, -1)
    q, k, v, p, ctx, z, hm = attn_fwd(
        random_blocks.reshape(-1), tokens, segment_ids.reshape(-1, SEQ), segment_ids.reshape(-1, 1),
        wq, wk, wv, wo, qb, vb, ob)
    out, dsum, db, dwi, dwu, dbi, small = ffn(z, out_cotangent, wi, wu, bi, bo, ag, ash, fg, fs, F32)
    dwq, dwk, dwv, dwo, dqb, dvb, dx = attn_bwd(tokens, db, wq, wk, wv, wo, q, k, v, p, ctx, dsum, F32)
    scatter = lambda a: lax.psum_scatter(a, "dp", scatter_dimension=0, tiled=True)
    dwu, dwi, dwo, dwq, dwk, dwv = (scatter(a) for a in (dwu, dwi, dwo, dwq, dwk, dwv))
    vec = lambda a: a.reshape(n, -1)
    smalls = jnp.concatenate([vec(dqb), vec(dvb), vec(small[5]), vec(small[3]), vec(small[4]), vec(small[2]),
                              vec(small[0]), vec(small[1]), vec(dbi)], axis=1)
    smalls = scatter(smalls)[0]
    dqb, dvb, dob, dag, dash, dbo, dfg, dfs = (smalls[i * part:(i + 1) * part] for i in range(8))
    dbi = smalls[8 * part:]
    head_maxima = lax.pmax(hm[:heads, 0], "dp")
    limit = clip_limit[0].astype(F32)
    factor = jnp.sqrt(jnp.minimum(1.0, limit / jnp.maximum(head_maxima, 1.0)))
    columns = jnp.repeat(factor, HD)[None, :]
    cq = (query_weight.astype(F32) * columns).astype(BF)
    ck = (key_weight.astype(F32) * columns).astype(BF)
    return (out, dx, dwq, dqb, dwk, dwv, dvb, dwo, dob, dag, dash, dwi, dbi, dwu, dbo, dfg, dfs, cq, ck, head_maxima)


def solution(mesh):
    mat, vec, rep = P("dp", None), P("dp"), P()
    in_specs = (mat, vec, rep, rep, mat, vec, mat, mat, vec, mat, vec, vec, vec, mat, vec, mat, vec, vec, vec, mat)
    out_specs = (mat, mat, mat, vec, mat, mat, vec, mat, vec, vec, vec, mat, vec, mat, vec, vec, vec, mat, mat, rep)
    return jax.shard_map(per_device, mesh=mesh, in_specs=in_specs, out_specs=out_specs, check_vma=False)
```

```python
from functools import partial
import math

import jax
import jax.numpy as jnp
from jax import lax
from jax.experimental import pallas as pl
from jax.experimental.pallas import tpu as pltpu
from jax.sharding import PartitionSpec as P

HD = 64
BLOCK = 64
SEQ = 512
BF = jnp.bfloat16
F32 = jnp.float32
LOW = -1e30
VMEM_MAX = 67043328


def dot(a, b):
    return jnp.dot(a, b, preferred_element_type=F32)


def dot_nt(a, b):
    return lax.dot_general(a, b, (((1,), (1,)), ((), ())), preferred_element_type=F32)


def dot_tn(a, b):
    return lax.dot_general(a, b, (((0,), (0,)), ((), ())), preferred_element_type=F32)


def attn_fwd_body(rb, x, segr, segc, wq, wk, wv, wo, qb, vb, ob,
                  q_o, k_o, v_o, p_o, c_o, z_o, hm_o, bias, s_s):
    g = pl.program_id(0)
    seqs = segr.shape[0]
    pairs = wq.shape[1] // 128

    @pl.when(g == 0)
    def _():
        for s in range(seqs):
            kseg = segr[s:s + 1, :]
            for c in range(SEQ // BLOCK):
                qseg = segc[s * SEQ + c * BLOCK:s * SEQ + (c + 1) * BLOCK, :]
                bias[s, c * BLOCK:(c + 1) * BLOCK, :] = jnp.where((qseg == kseg) & (kseg != 0), 0.0, LOW)
        hm_o[...] = jnp.full(hm_o.shape, LOW, F32)
        z_o[...] = x[...].astype(F32) + ob[...].astype(F32)

    xv = x[...]
    q_o[...] = (dot(xv, wq[...]) + qb[...].astype(F32)).astype(BF)
    k_o[...] = dot(xv, wk[...]).astype(BF)
    v_o[...] = (dot(xv, wv[...]) + vb[...].astype(F32)).astype(BF)

    lane_block = lax.broadcasted_iota(jnp.int32, (1, SEQ), 1) // BLOCK
    first_half = lax.broadcasted_iota(jnp.int32, (1, 128), 1) < HD
    last = SEQ // BLOCK - 2

    def one_pair(it, _):
        s = it // pairs
        pair = it % pairs
        rows = pl.ds(pl.multiple_of(s * SEQ, SEQ), SEQ)
        lanes = pl.ds(pl.multiple_of(pair * 128, 128), 128)
        qp = q_o[rows, lanes]
        kp = k_o[rows, lanes]
        vp = v_o[rows, lanes]
        outs = []
        for j in range(2):
            head = g * (2 * pairs) + pair * 2 + j
            mine = first_half if j == 0 else jnp.logical_not(first_half)
            s_s[j] = dot_nt(jnp.where(mine, qp * 0.125, 0).astype(BF), kp)
            at = head * (6 * 3)
            miss1 = 18 - (rb[at] + rb[at + 1] + rb[at + 2])
            miss6 = 10 - (rb[at + 15] + rb[at + 16] + rb[at + 17])
            skip1 = jnp.where(lane_block == miss1, LOW, 0.0)
            skip6 = jnp.where(lane_block == miss6, LOW, 0.0)
            tops = None
            for c in range(SEQ // BLOCK):
                cr = slice(c * BLOCK, (c + 1) * BLOCK)
                sv = s_s[j, cr, :] + bias[s, cr, :]
                if c == 1:
                    sv = sv + skip1
                if c == last:
                    sv = sv + skip6
                top = jnp.max(sv, axis=1, keepdims=True)
                live = top > -1e29
                e = jnp.exp(sv - jnp.where(live, top, 0.0))
                total = jnp.sum(e, axis=1, keepdims=True) + jnp.where(live, 0.0, 1.0)
                p_o[s * (2 * pairs) + pair * 2 + j, cr, :] = (e * (1.0 / total)).astype(BF)
                tops = top if tops is None else jnp.maximum(tops, top)
            hm = jnp.max(tops, axis=0, keepdims=True)
            hm_o[pl.ds(head, 1), :] = jnp.maximum(hm_o[pl.ds(head, 1), :], hm)
            outs.append(dot(p_o[s * (2 * pairs) + pair * 2 + j], vp))
        c_o[rows, lanes] = jnp.where(first_half, outs[0], outs[1]).astype(BF)
        return 0

    lax.fori_loop(0, seqs * pairs, one_pair, 0)
    z_o[...] += dot(c_o[...], wo[...])


def attn_fwd(rb, x, segr, segc, wall, qb, vb, ob):
    rows, d = x.shape
    seqs = rows // SEQ
    gw = 256
    groups = d // gw
    maps = seqs * (gw // HD)
    full = lambda shape: pl.BlockSpec(shape, lambda g, *_: (0,) * len(shape))
    col = lambda i: pl.BlockSpec((None, d, gw), lambda g, *_: (i, 0, g))
    vec = pl.BlockSpec((1, gw), lambda g, *_: (0, g))
    act = pl.BlockSpec((rows, gw), lambda g, *_: (0, g))
    return pl.pallas_call(
        attn_fwd_body,
        grid_spec=pltpu.PrefetchScalarGridSpec(
            num_scalar_prefetch=1, grid=(groups,),
            in_specs=[full((rows, d)), full((seqs, SEQ)), full((rows, 1)), col(0), col(1), col(2),
                      pl.BlockSpec((None, gw, d), lambda g, *_: (3, g, 0)), vec, vec, full((1, d))],
            out_specs=[act, act, act, pl.BlockSpec((maps, SEQ, SEQ), lambda g, *_: (g, 0, 0)), act,
                       full((rows, d)), full((16, 128))],
            scratch_shapes=[pltpu.VMEM((seqs, SEQ, SEQ), F32), pltpu.VMEM((2, SEQ, SEQ), F32)]),
        out_shape=[jax.ShapeDtypeStruct((rows, d), BF)] * 3
        + [jax.ShapeDtypeStruct((groups * maps, SEQ, SEQ), BF), jax.ShapeDtypeStruct((rows, d), BF),
           jax.ShapeDtypeStruct((rows, d), F32), jax.ShapeDtypeStruct((16, 128), F32)],
        compiler_params=pltpu.CompilerParams(vmem_limit_bytes=VMEM_MAX),
        name="attn_fwd",
    )(rb, x, segr, segc, wall, wall, wall, wall, qb, vb, ob)


def unit_rows(z):
    mean = jnp.mean(z, axis=-1, keepdims=True)
    c = z - mean
    inv = lax.rsqrt(jnp.mean(c * c, axis=-1, keepdims=True) + 1e-12)
    return c * inv, inv


def norm_back(up, unit, inv, gain):
    e = up * gain
    spread = jnp.mean(e, axis=-1, keepdims=True)
    along = jnp.mean(e * unit, axis=-1, keepdims=True)
    return inv * (e - spread - unit * along)


def col_sum(v):
    return jnp.sum(v, axis=0, keepdims=True)


def ffn_body(z, cot, wi, wo, bi, bo, ag, ash, fg, fs,
             out, dsum, db, dwi, dwo, dbi, small, fl, act, gp, acc, do):
    rows, d = z.shape
    ff = wi.shape[1]
    rt, ct, et = 512, 512, 128
    k0, k1 = math.sqrt(2.0 / math.pi), 0.044715
    agv, ashv = ag[...].astype(F32), ash[...].astype(F32)
    fgv, fsv, bov = fg[...].astype(F32), fs[...].astype(F32), bo[...].astype(F32)

    def prep(i, _):
        r = pl.ds(pl.multiple_of(i * et, et), et)
        unit, _inv = unit_rows(z[r, :])
        first = unit * agv + ashv
        fl[r, :] = first.astype(BF)
        acc[r, :] = first + bov
        return 0

    lax.fori_loop(0, rows // et, prep, 0)

    def up(i, _):
        r = pl.ds(pl.multiple_of((i % (rows // rt)) * rt, rt), rt)
        c = pl.ds(pl.multiple_of((i // (rows // rt)) * ct, ct), ct)
        u = dot(fl[r, :], wi[:, c]) + bi[:, c].astype(F32)
        u2 = u * u
        t = jnp.tanh(u * (k0 + (k0 * k1) * u2))
        h = 0.5 + 0.5 * t
        a = (u * h).astype(BF)
        act[r, c] = a
        gp[r, c] = (h + (0.5 * u) * (1.0 - t * t) * (k0 + (3.0 * k0 * k1) * u2)).astype(gp.dtype)
        acc[r, :] += dot(a, wo[c, :])
        return 0

    lax.fori_loop(0, (ff // ct) * (rows // rt), up, 0)

    small[...] = jnp.zeros(small.shape, F32)

    def mid(i, _):
        r = pl.ds(pl.multiple_of(i * et, et), et)
        unit, inv = unit_rows(acc[r, :])
        out[r, :] = (unit * fgv + fsv).astype(BF)
        upv = cot[r, :].astype(F32)
        small[0:1, :] += col_sum(upv * unit)
        small[1:2, :] += col_sum(upv)
        ds = norm_back(upv, unit, inv, fgv)
        dsl = ds.astype(BF)
        do[r, :] = dsl
        acc[r, :] = ds
        small[2:3, :] += col_sum(dsl.astype(F32))
        return 0

    lax.fori_loop(0, rows // et, mid, 0)

    def down(j, _):
        c = pl.ds(pl.multiple_of(j * ct, ct), ct)
        dwo[c, :] = dot_tn(act[:, c], do[...]).astype(dwo.dtype)
        sums = None
        for i in range(rows // rt):
            r = slice(i * rt, (i + 1) * rt)
            di = dot_nt(do[r, :], wo[c, :]) * gp[r, c].astype(F32)
            dil = di.astype(BF)
            act[r, c] = dil
            s = col_sum(dil.astype(F32))
            sums = s if sums is None else sums + s
            acc[r, :] += dot_nt(dil, wi[:, c])
        dbi[:, c] = sums
        dwi[:, c] = dot_tn(fl[...], act[:, c]).astype(dwi.dtype)
        return 0

    lax.fori_loop(0, ff // ct, down, 0)

    def tail(i, _):
        r = pl.ds(pl.multiple_of(i * et, et), et)
        unit, inv = unit_rows(z[r, :])
        df = acc[r, :]
        small[3:4, :] += col_sum(df * unit)
        small[4:5, :] += col_sum(df)
        ds = norm_back(df, unit, inv, agv)
        dsum[r, :] = ds
        dsl = ds.astype(BF)
        db[r, :] = dsl
        small[5:6, :] += col_sum(dsl.astype(F32))
        return 0

    lax.fori_loop(0, rows // et, tail, 0)


def ffn(z, cot, wi, wo, bi, bo, ag, ash, fg, fs, gdt):
    rows, d = z.shape
    ff = wi.shape[1]
    sd = jax.ShapeDtypeStruct
    vm = pl.BlockSpec(memory_space=pltpu.VMEM)
    return pl.pallas_call(
        ffn_body,
        in_specs=[vm] * 10,
        out_specs=[vm] * 7,
        out_shape=[sd((rows, d), BF), sd((rows, d), F32), sd((rows, d), BF), sd((d, ff), gdt), sd((ff, d), gdt),
                   sd((1, ff), F32), sd((8, d), F32)],
        scratch_shapes=[pltpu.VMEM((rows, d), BF), pltpu.VMEM((rows, ff), BF), pltpu.VMEM((rows, ff), BF),
                        pltpu.VMEM((rows, d), F32), pltpu.VMEM((rows, d), BF)],
        compiler_params=pltpu.CompilerParams(vmem_limit_bytes=VMEM_MAX),
        name="ffn",
    )(z, cot, wi, wo, bi, bo, ag, ash, fg, fs)


def attn_bwd_body(x, db, wq, wk, wv, wo, q, k, v, p, ctx, dsum,
                  dw, dqb, dvb, dx, dc, dq, dk, dv, dp_s, ds_s):
    g = pl.program_id(0)
    seqs = x.shape[0] // SEQ
    pairs = wq.shape[1] // 128

    @pl.when(g == 0)
    def _():
        dx[...] = dsum[...]

    dbv = db[...]
    dc[...] = dot_nt(dbv, wo[...]).astype(BF)
    part = pl.ds(pl.multiple_of(g * 256, 256), 256)
    dw[3, part, :] = dot_tn(ctx[...], dbv).astype(dw.dtype)
    first_half = lax.broadcasted_iota(jnp.int32, (1, 128), 1) < HD

    def one_pair(it, _):
        s = it // pairs
        pair = it % pairs
        rows = pl.ds(pl.multiple_of(s * SEQ, SEQ), SEQ)
        lanes = pl.ds(pl.multiple_of(pair * 128, 128), 128)
        qp, kp, vp, dcp = q[rows, lanes], k[rows, lanes], v[rows, lanes], dc[rows, lanes]
        dqs, dks, dvs = [], [], []
        for j in range(2):
            mine = first_half if j == 0 else jnp.logical_not(first_half)
            m = s * (2 * pairs) + pair * 2 + j
            dp_s[j] = dot_nt(jnp.where(mine, dcp, 0).astype(BF), vp)
            for c in range(SEQ // BLOCK):
                cr = slice(c * BLOCK, (c + 1) * BLOCK)
                pv = p[m, cr, :].astype(F32)
                sl = dp_s[j, cr, :]
                mean = jnp.sum(pv * sl, axis=1, keepdims=True)
                ds_s[j, cr, :] = (pv * (sl - mean)).astype(BF)
            dqs.append(dot(ds_s[j], kp))
            dks.append(dot_tn(ds_s[j], qp))
            dvs.append(dot_tn(p[m], dcp))
        dq[rows, lanes] = (jnp.where(first_half, dqs[0], dqs[1]) * 0.125).astype(BF)
        dk[rows, lanes] = (jnp.where(first_half, dks[0], dks[1]) * 0.125).astype(BF)
        dv[rows, lanes] = jnp.where(first_half, dvs[0], dvs[1]).astype(BF)
        return 0

    lax.fori_loop(0, seqs * pairs, one_pair, 0)
    dqb[...] = col_sum(dq[...].astype(F32))
    dvb[...] = col_sum(dv[...].astype(F32))
    xv = x[...]
    dw[0, :, part] = dot_tn(xv, dq[...]).astype(dw.dtype)
    dw[1, :, part] = dot_tn(xv, dk[...]).astype(dw.dtype)
    dw[2, :, part] = dot_tn(xv, dv[...]).astype(dw.dtype)
    dx[...] += dot_nt(dq[...], wq[...]) + dot_nt(dk[...], wk[...]) + dot_nt(dv[...], wv[...])


def attn_bwd(x, db, wall, q, k, v, p, ctx, dsum, gdt):
    rows, d = x.shape
    seqs = rows // SEQ
    gw = 256
    groups = d // gw
    maps = seqs * (gw // HD)
    full = lambda shape: pl.BlockSpec(shape, lambda g: (0,) * len(shape), pipeline_mode=pl.Buffered(1))
    col = lambda i: pl.BlockSpec((None, d, gw), lambda g: (i, 0, g))
    row = pl.BlockSpec((None, gw, d), lambda g: (3, g, 0))
    vec = pl.BlockSpec((1, gw), lambda g: (0, g))
    act = pl.BlockSpec((rows, gw), lambda g: (0, g))
    sd = jax.ShapeDtypeStruct
    return pl.pallas_call(
        attn_bwd_body,
        grid=(groups,),
        in_specs=[full((rows, d)), full((rows, d)), col(0), col(1), col(2), row, act, act, act,
                  pl.BlockSpec((maps, SEQ, SEQ), lambda g: (g, 0, 0)), act, full((rows, d))],
        out_specs=[full((4, d, d)), vec, vec, pl.BlockSpec((rows, d), lambda g: (0, 0))],
        out_shape=[sd((4, d, d), gdt)] + [sd((1, d), F32)] * 2 + [sd((rows, d), F32)],
        scratch_shapes=[pltpu.VMEM((rows, gw), BF)] * 4
        + [pltpu.VMEM((2, SEQ, SEQ), F32), pltpu.VMEM((2, SEQ, SEQ), BF)],
        compiler_params=pltpu.CompilerParams(vmem_limit_bytes=VMEM_MAX),
        name="attn_bwd",
    )(x, db, wall, wall, wall, wall, q, k, v, p, ctx, dsum)
MESH_ID = pl.DeviceIdType.MESH


def place():
    me = lax.axis_index("dp")
    c, x, y, z = me % 2, (me // 2) % 2, (me // 4) % 2, me // 8
    fc, fx, fy = 1 - 2 * c, 2 * (1 - 2 * x), 4 * (1 - 2 * y)
    d1 = fx * (1 - c) + fy * c
    d2 = fy * (1 - c) + fx * c
    zs = (0, 8 * (1 - 2 * (z % 2)), 16 * (1 - 2 * (z // 2)), 8 * (3 - 2 * z))
    return me, fc, d1, d2, zs


def meet(me, fc, d1, d2, zs):
    barrier = pltpu.get_barrier_semaphore()
    for off in (fc, d1, d2) + zs[1:]:
        pl.semaphore_signal(barrier, inc=1, device_id=(me + off,), device_id_type=MESH_ID)
    pl.semaphore_wait(barrier, 6)


def unit_of(ref, lead, unit):
    return ref.at[:, unit] if lead else ref.at[unit]


class Gather:
    def __init__(self, where, own, out, send, recv):
        self.where, self.own, self.out, self.send, self.recv = where, own, out, send, recv
        self.lead = len(out.shape) == 4

    def copy(self, slot, unit, dest, own=False):
        return pltpu.make_async_remote_copy(
            src_ref=self.own if own else unit_of(self.out, self.lead, unit), dst_ref=unit_of(self.out, self.lead, unit),
            send_sem=self.send.at[slot], recv_sem=self.recv.at[slot], device_id=(dest,), device_id_type=MESH_ID)

    def begin(self):
        me, fc, d1, d2, zs = self.where
        for k in (1, 2, 3):
            self.copy(k, me, me + zs[k], True).start()
        self.copy(4, me, me + d1, True).start()
        self.copy(8, me, me + d2, True).start()
        self.copy(16, me, me + fc, True).start()

    def landed(self, slot):
        me, fc, d1, d2, zs = self.where
        k = slot % 4
        group = slot // 4
        off = (0, d1, d2, d1 + d2, fc, fc + d2, fc + d1, fc + d1 + d2)[group]
        unit = me + zs[k] + off
        self.copy(slot, unit, me).wait_recv()
        return unit

    def step(self, slot):
        me, fc, d1, d2, zs = self.where
        k, group = slot % 4, slot // 4
        unit = self.landed(slot)
        if group == 0:
            self.copy(4 + k, unit, me + d1).start()
            self.copy(8 + k, unit, me + d2).start()
        if group == 1:
            self.copy(12 + k, unit, me + d2).start()
        if group < 4:
            self.copy(16 + slot, unit, me + fc).start()

    ORDER = (1, 4, 2, 5, 8, 3, 6, 9, 7, 12, 10, 13, 11, 14, 15)

    def finish(self):
        me = self.where[0]
        for slot in range(16, 32):
            self.landed(slot)
        for slot in range(1, 32):
            self.copy(slot, me, me, slot in (1, 2, 3, 4, 8, 16)).wait_send()


def gather_body(*refs):
    n = (len(refs) - 3) // 2
    own, out = refs[:n], refs[n:2 * n]
    send, recv, local = refs[2 * n:]
    where = place()
    me = where[0]
    mine = [pltpu.make_async_copy(own[a], unit_of(out[a], len(out[a].shape) == 4, me), local.at[a]) for a in range(n)]
    for m in mine:
        m.start()
    meet(*where)
    flows = [Gather(where, own[a], out[a], send.at[a], recv.at[a]) for a in range(n)]
    for f in flows:
        f.begin()
    for slot in Gather.ORDER:
        for f in flows:
            f.step(slot)
    for f in flows:
        f.finish()
    for m in mine:
        m.wait()


def gather_all(parts, n, cid):
    na = len(parts)
    return pl.pallas_call(
        gather_body,
        in_specs=[pl.BlockSpec(memory_space=pltpu.VMEM)] * na,
        out_specs=[pl.BlockSpec(memory_space=pl.ANY)] * na,
        out_shape=[jax.ShapeDtypeStruct(p.shape[:-2] + (n,) + p.shape[-2:], p.dtype) for p in parts],
        scratch_shapes=[pltpu.SemaphoreType.DMA((na, 32)), pltpu.SemaphoreType.DMA((na, 32)),
                        pltpu.SemaphoreType.DMA((na,))],
        compiler_params=pltpu.CompilerParams(collective_id=cid, has_side_effects=True, vmem_limit_bytes=16 << 20),
        name="gather_all",
    )(*parts)


class Scatter:
    def __init__(self, where, grad, own, rp, r1, r2, rz, sems, lsem):
        self.where, self.grad, self.own = where, grad, own
        self.rp, self.r1, self.r2, self.rz, self.sems, self.lsem = rp, r1, r2, rz, sems, lsem

    def remote(self, src, dst, slot, off):
        return pltpu.make_async_remote_copy(
            src_ref=src, dst_ref=dst, send_sem=self.sems.at[0, slot], recv_sem=self.sems.at[1, slot],
            device_id=(self.where[0] + off,), device_id_type=MESH_ID)

    def begin(self):
        me, fc, d1, d2, zs = self.where
        lead = len(self.grad.shape) == 4
        for a in (1, 0):
            for b in (1, 0):
                for k in range(4):
                    self.remote(unit_of(self.grad, lead, me + fc + a * d2 + b * d1 + zs[k]), self.rp.at[a, b, k],
                                a, fc).start()
            for b in (1, 0):
                for k in range(4):
                    pltpu.make_async_copy(unit_of(self.grad, lead, me + a * d1 + b * d2 + zs[k]),
                                          self.own.at[a, b, k], self.lsem.at[a]).start()

    def pair(self, a):
        me, fc, d1, d2, zs = self.where
        self.remote(self.own.at[a], self.rp.at[a], a, fc).wait_recv()
        pltpu.make_async_copy(self.own.at[a], self.rp.at[a], self.lsem.at[a]).wait()
        for b in (1, 0):
            self.own[a, b] = (self.own[a, b].astype(F32) + self.rp[a, b].astype(F32)).astype(BF)
            if a == 1:
                self.remote(self.own.at[1, b], self.r1.at[b], 2 + b, d1).start()

    def first(self, b):
        me, fc, d1, d2, zs = self.where
        self.remote(self.own.at[1, b], self.r1.at[b], 2 + b, d1).wait_recv()
        self.own[0, b] = (self.own[0, b].astype(F32) + self.r1[b].astype(F32)).astype(BF)
        if b == 1:
            self.remote(self.own.at[0, 1], self.r2, 4, d2).start()

    def second(self):
        me, fc, d1, d2, zs = self.where
        self.remote(self.own.at[0, 1], self.r2, 4, d2).wait_recv()
        for k in (1, 2, 3):
            self.own[0, 0, k] = (self.own[0, 0, k].astype(F32) + self.r2[k].astype(F32)).astype(BF)
            self.remote(self.own.at[0, 0, k], self.rz.at[k - 1], 4 + k, zs[k]).start()

    def last(self):
        me, fc, d1, d2, zs = self.where
        total = self.own[0, 0, 0].astype(F32) + self.r2[0].astype(F32)
        for k in (1, 2, 3):
            self.remote(self.own.at[0, 0, k], self.rz.at[k - 1], 4 + k, zs[k]).wait_recv()
            total = total + self.rz[k - 1].astype(F32)
        return total

    def drain(self):
        me, fc, d1, d2, zs = self.where
        for a in (1, 0):
            self.remote(self.own.at[a], self.rp.at[a], a, fc).wait_send()
        for b in (1, 0):
            self.remote(self.own.at[1, b], self.r1.at[b], 2 + b, d1).wait_send()
        self.remote(self.own.at[0, 1], self.r2, 4, d2).wait_send()
        for k in (1, 2, 3):
            self.remote(self.own.at[0, 0, k], self.rz.at[k - 1], 4 + k, zs[k]).wait_send()


class Vectors:
    def __init__(self, where, held, got, sems):
        self.where, self.held, self.got, self.sems = where, held, got, sems

    def remote(self, src, slot, off):
        return pltpu.make_async_remote_copy(
            src_ref=self.held.at[src], dst_ref=self.got.at[slot], send_sem=self.sems.at[0, slot],
            recv_sem=self.sems.at[1, slot], device_id=(self.where[0] + off,), device_id_type=MESH_ID)

    def merge(self, a, b):
        row = lax.broadcasted_iota(jnp.int32, a.shape, 0)
        return jnp.where(row == 12, jnp.maximum(a, b), a + b)

    def step(self, i):
        me, fc, d1, d2, zs = self.where
        offs = (fc, d1, d2)
        if i > 0:
            self.remote(i - 1, i - 1, offs[i - 1]).wait_recv()
            self.held[i] = self.merge(self.held[i - 1], self.got[i - 1])
        if i < 3:
            self.remote(i, i, offs[i]).start()
        else:
            for k in (1, 2, 3):
                self.remote(3, 2 + k, zs[k]).start()

    def last(self):
        me, fc, d1, d2, zs = self.where
        total = self.held[3]
        for k in (1, 2, 3):
            self.remote(3, 2 + k, zs[k]).wait_recv()
            total = self.merge(total, self.got[2 + k])
        for i, off in enumerate((fc, d1, d2)):
            self.remote(i, i, off).wait_send()
        for k in (1, 2, 3):
            self.remote(3, 2 + k, zs[k]).wait_send()
        return total


def scatter_body(na, *refs):
    grads, vec = refs[:na], refs[na]
    outs, vout = refs[na + 1:2 * na + 1], refs[2 * na + 1]
    rest = refs[2 * na + 2:]
    bufs, (held, got, sems, lsems, vsems) = rest[:5 * na], rest[5 * na:]
    where = place()
    flows = [Scatter(where, grads[a], *bufs[5 * a:5 * a + 5], sems.at[a], lsems.at[a]) for a in range(na)]
    small = Vectors(where, held, got, vsems)
    held[0] = vec[...]
    meet(*where)
    small.step(0)
    for f in flows:
        f.begin()
    small.step(1)
    for f in flows:
        f.pair(1)
    small.step(2)
    for f in flows:
        f.pair(0)
    small.step(3)
    for f in flows:
        f.first(1)
    for i, f in enumerate(flows):
        f.first(0)
        if i > 0:
            flows[i - 1].second()
    flows[-1].second()
    vout[...] = small.last()
    for f, o in zip(flows, outs):
        o[...] = f.last()
    for f in flows:
        f.drain()


def scatter_all(grads, vec, cid):
    na = len(grads)
    shapes = [g.shape[:-3] + g.shape[-2:] for g in grads]
    bufs = []
    for s in shapes:
        bufs += [pltpu.VMEM((2, 2, 4) + s, BF)] * 2 + [pltpu.VMEM((2, 4) + s, BF), pltpu.VMEM((4,) + s, BF),
                                                         pltpu.VMEM((3,) + s, BF)]
    vm = pl.BlockSpec(memory_space=pltpu.VMEM)
    return pl.pallas_call(
        partial(scatter_body, na),
        in_specs=[pl.BlockSpec(memory_space=pl.ANY)] * na + [vm],
        out_specs=[vm] * (na + 1),
        out_shape=[jax.ShapeDtypeStruct(s, F32) for s in shapes] + [jax.ShapeDtypeStruct(vec.shape, F32)],
        scratch_shapes=bufs + [pltpu.VMEM((4,) + vec.shape, F32), pltpu.VMEM((6,) + vec.shape, F32),
                               pltpu.SemaphoreType.DMA((na, 2, 8)), pltpu.SemaphoreType.DMA((na, 2)),
                               pltpu.SemaphoreType.DMA((2, 6))],
        compiler_params=pltpu.CompilerParams(collective_id=cid, has_side_effects=True, vmem_limit_bytes=VMEM_MAX),
        name="scatter_all",
    )(*grads, vec)


def vectors_part(me, n, vecs, inner_bias):
    part = vecs[0].shape[0]
    d = part * n
    rows = jnp.tile(jnp.stack(vecs), (1, n))
    rows = jnp.where(lax.broadcasted_iota(jnp.int32, rows.shape, 1) // part == me, rows, 0)
    flat = jnp.tile(inner_bias, n)
    flat = jnp.where(lax.broadcasted_iota(jnp.int32, flat.shape, 0) // inner_bias.shape[0] == me, flat, 0)
    flat = flat.reshape(-1, d)
    rest = jnp.zeros((16 - rows.shape[0] - flat.shape[0], d), BF)
    return jnp.concatenate([rows, flat, rest], axis=0)


def per_device(n, tokens, segment_ids, random_blocks, clip_limit, query_weight, query_bias, key_weight, value_weight,
               value_bias, output_weight, output_bias, attn_gain, attn_shift, inner_weight, inner_bias,
               outer_weight, outer_bias, final_gain, final_shift, out_cotangent):
    heads = random_blocks.shape[0]
    rows, d = tokens.shape
    ff = inner_weight.shape[1]
    near = n == 32 and query_weight.shape[0] % 8 == 0
    me = lax.axis_index("dp")
    stack = jnp.stack([query_weight, key_weight, value_weight, output_weight])
    names = (query_bias, value_bias, output_bias, attn_gain, attn_shift, outer_bias, final_gain, final_shift)
    part = query_bias.shape[0]
    vec_part = vectors_part(me, n, names, inner_bias)
    if near:
        wall, vecs, wi, wu = gather_all((stack, vec_part, inner_weight, outer_weight), n, 0)
        wall, wi, wu = wall.reshape(4, d, d), wi.reshape(d, ff), wu.reshape(ff, d)
        vecs = jnp.sum(vecs.astype(F32), axis=0)
    else:
        wall = lax.all_gather(stack, "dp", axis=1, tiled=True)
        wi, wu = (lax.all_gather(a, "dp", axis=0, tiled=True) for a in (inner_weight, outer_weight))
        vecs = lax.psum(vec_part.astype(F32), "dp")
    qb, vb, ob, ag, ash, bo, fg, fs = (vecs[i:i + 1] for i in range(8))
    bi = vecs[8:8 + ff // d].reshape(1, ff)
    gdt = BF if near else F32
    q, k, v, p, ctx, z, hm = attn_fwd(
        random_blocks.reshape(-1), tokens, segment_ids.reshape(-1, SEQ), segment_ids.reshape(-1, 1), wall, qb, vb, ob)
    out, dsum, db, dwi, dwu, dbi, small = ffn(z, out_cotangent, wi, wu, bi, bo, ag, ash, fg, fs, gdt)
    dwall, dqb, dvb, dx = attn_bwd(tokens, db, wall, q, k, v, p, ctx, dsum, gdt)
    hm_row = jnp.pad(hm[:heads, 0], (0, d - heads))[None]
    mine = jnp.concatenate([dqb, dvb, small[5:6], small[3:4], small[4:5], small[2:3], small[0:2],
                            dbi.reshape(-1, d), hm_row, jnp.zeros((16 - 9 - ff // d, d), F32)], axis=0)
    if near:
        dwu, dwi, dwall, total = scatter_all(
            (dwu.reshape(n, -1, d), dwi.reshape(n, -1, ff), dwall.reshape(4, n, -1, d)), mine, 1)
    else:
        scatter = lambda a, at: lax.psum_scatter(a, "dp", scatter_dimension=at, tiled=True)
        dwu, dwi, dwall = scatter(dwu, 0), scatter(dwi, 0), scatter(dwall, 1)
        total = jnp.where(lax.broadcasted_iota(jnp.int32, mine.shape, 0) == 12, lax.pmax(mine, "dp"),
                          lax.psum(mine, "dp"))
    vec8 = lax.dynamic_slice(total, (0, me * part), (8, part))
    dqb, dvb, dob, dag, dash, dbo, dfg, dfs = (vec8[i] for i in range(8))
    wide = inner_bias.shape[0]
    dbi = lax.dynamic_slice(total[8:8 + ff // d].reshape(-1), (me * wide,), (wide,))
    head_maxima = total[12, :heads]
    limit = clip_limit[0].astype(F32)
    factor = jnp.sqrt(jnp.minimum(1.0, limit / jnp.maximum(head_maxima, 1.0)))
    columns = jnp.repeat(factor, HD)[None, :]
    cq = (query_weight.astype(F32) * columns).astype(BF)
    ck = (key_weight.astype(F32) * columns).astype(BF)
    return (out, dx, dwall[0], dqb, dwall[1], dwall[2], dvb, dwall[3], dob, dag, dash, dwi, dbi, dwu, dbo, dfg, dfs,
            cq, ck, head_maxima)


def solution(mesh):
    mat, vec, rep = P("dp", None), P("dp"), P()
    in_specs = (mat, vec, rep, rep, mat, vec, mat, mat, vec, mat, vec, vec, vec, mat, vec, mat, vec, vec, vec, mat)
    out_specs = (mat, mat, mat, vec, mat, mat, vec, mat, vec, vec, vec, mat, vec, mat, vec, vec, vec, mat, mat, rep)
    return jax.shard_map(partial(per_device, mesh.shape["dp"]), mesh=mesh, in_specs=in_specs, out_specs=out_specs,
                         check_vma=False)
```

```python
from functools import partial
import math

import jax
import jax.numpy as jnp
from jax import lax
from jax.experimental import pallas as pl
from jax.experimental.pallas import tpu as pltpu
from jax.sharding import PartitionSpec as P

HD = 64
BLOCK = 64
SEQ = 512
GW = 256
BF = jnp.bfloat16
F32 = jnp.float32
LOW = -1e30
VMEM_MAX = 67043328
MESH_ID = pl.DeviceIdType.MESH
QB, VB, OB, AG, ASH, BO, FG, FS, BI, TOP = 0, 1, 2, 3, 4, 5, 6, 7, 8, 12


def dot(a, b):
    return jnp.dot(a, b, preferred_element_type=F32)


def dot_nt(a, b):
    return lax.dot_general(a, b, (((1,), (1,)), ((), ())), preferred_element_type=F32)


def dot_tn(a, b):
    return lax.dot_general(a, b, (((0,), (0,)), ((), ())), preferred_element_type=F32)


def col_sum(v):
    return jnp.sum(v, axis=0, keepdims=True)


def first_half():
    return lax.broadcasted_iota(jnp.int32, (1, 128), 1) < HD


def same_document(segr, segc, bias):
    for s in range(segr.shape[0]):
        kseg = segr[s:s + 1, :]
        for c in range(SEQ // BLOCK):
            qseg = segc[s * SEQ + c * BLOCK:s * SEQ + (c + 1) * BLOCK, :]
            bias[s, c * BLOCK:(c + 1) * BLOCK, :] = jnp.where((qseg == kseg) & (kseg != 0), 0.0, LOW)


def pair_forward(g, it, rb, q, k, v, p, ctx, hm, bias, s_s):
    pairs = GW // 128
    s, pair = it // pairs, it % pairs
    rows = pl.ds(pl.multiple_of(s * SEQ, SEQ), SEQ)
    lanes = pl.ds(pl.multiple_of(pair * 128, 128), 128)
    lane_block = lax.broadcasted_iota(jnp.int32, (1, SEQ), 1) // BLOCK
    half = first_half()
    last = SEQ // BLOCK - 2
    qp, kp, vp = q[rows, lanes], k[rows, lanes], v[rows, lanes]
    outs = []
    for j in range(2):
        head = g * (2 * pairs) + pair * 2 + j
        m = s * (2 * pairs) + pair * 2 + j
        mine = half if j == 0 else jnp.logical_not(half)
        s_s[j] = dot_nt(jnp.where(mine, qp * 0.125, 0).astype(BF), kp)
        at = head * (6 * 3)
        miss1 = 18 - (rb[at] + rb[at + 1] + rb[at + 2])
        miss6 = 10 - (rb[at + 15] + rb[at + 16] + rb[at + 17])
        skip1 = jnp.where(lane_block == miss1, LOW, 0.0)
        skip6 = jnp.where(lane_block == miss6, LOW, 0.0)
        tops = None
        for c in range(SEQ // BLOCK):
            cr = slice(c * BLOCK, (c + 1) * BLOCK)
            sv = s_s[j, cr, :] + bias[s, cr, :]
            if c == 1:
                sv = sv + skip1
            if c == last:
                sv = sv + skip6
            top = jnp.max(sv, axis=1, keepdims=True)
            live = top > -1e29
            e = jnp.exp(sv - jnp.where(live, top, 0.0))
            total = jnp.sum(e, axis=1, keepdims=True) + jnp.where(live, 0.0, 1.0)
            p[m, cr, :] = (e * (1.0 / total)).astype(BF)
            tops = top if tops is None else jnp.maximum(tops, top)
        top = jnp.max(tops, axis=0, keepdims=True)
        hm[pl.ds(head, 1), :] = jnp.maximum(hm[pl.ds(head, 1), :], top)
        outs.append(dot(p[m], vp))
    ctx[rows, lanes] = jnp.where(half, outs[0], outs[1]).astype(BF)


def pair_backward(it, q, k, v, p, dc, dq, dk, dv, dp_s, ds_s):
    pairs = GW // 128
    s, pair = it // pairs, it % pairs
    rows = pl.ds(pl.multiple_of(s * SEQ, SEQ), SEQ)
    lanes = pl.ds(pl.multiple_of(pair * 128, 128), 128)
    half = first_half()
    qp, kp, vp, dcp = q[rows, lanes], k[rows, lanes], v[rows, lanes], dc[rows, lanes]
    dqs, dks, dvs = [], [], []
    for j in range(2):
        mine = half if j == 0 else jnp.logical_not(half)
        m = s * (2 * pairs) + pair * 2 + j
        dp_s[j] = dot_nt(jnp.where(mine, dcp, 0).astype(BF), vp)
        for c in range(SEQ // BLOCK):
            cr = slice(c * BLOCK, (c + 1) * BLOCK)
            pv = p[m, cr, :].astype(F32)
            sl = dp_s[j, cr, :]
            mean = jnp.sum(pv * sl, axis=1, keepdims=True)
            ds_s[j, cr, :] = (pv * (sl - mean)).astype(BF)
        dqs.append(dot(ds_s[j], kp))
        dks.append(dot_tn(ds_s[j], qp))
        dvs.append(dot_tn(p[m], dcp))
    dq[rows, lanes] = (jnp.where(half, dqs[0], dqs[1]) * 0.125).astype(BF)
    dk[rows, lanes] = (jnp.where(half, dks[0], dks[1]) * 0.125).astype(BF)
    dv[rows, lanes] = jnp.where(half, dvs[0], dvs[1]).astype(BF)


def unit_rows(z):
    mean = jnp.mean(z, axis=-1, keepdims=True)
    c = z - mean
    inv = lax.rsqrt(jnp.mean(c * c, axis=-1, keepdims=True) + 1e-12)
    return c * inv, inv


def norm_back(up, unit, inv, gain):
    e = up * gain
    spread = jnp.mean(e, axis=-1, keepdims=True)
    along = jnp.mean(e * unit, axis=-1, keepdims=True)
    return inv * (e - spread - unit * along)


def ffn_body(z, cot, wi, wo, vecs, out, dsum, db, dwi, dwo, small, fl, act, gp, acc, do):
    rows, d = z.shape
    ff = wi.shape[1]
    rt, et = 512, 128
    k0, k1 = math.sqrt(2.0 / math.pi), 0.044715
    row = lambda i: vecs[i:i + 1, :]
    small[...] = jnp.zeros(small.shape, F32)

    def prep(i, _):
        r = pl.ds(pl.multiple_of(i * et, et), et)
        unit, _inv = unit_rows(z[r, :])
        first = unit * row(AG) + row(ASH)
        fl[r, :] = first.astype(BF)
        acc[r, :] = first + row(BO)
        return 0

    lax.fori_loop(0, rows // et, prep, 0)

    def up(i, _):
        j = i // (rows // rt)
        r = pl.ds(pl.multiple_of((i % (rows // rt)) * rt, rt), rt)
        c = pl.ds(pl.multiple_of(j * d, d), d)
        u = dot(fl[r, :], wi[:, c]) + vecs[pl.ds(BI + j, 1), :]
        u2 = u * u
        t = jnp.tanh(u * (k0 + (k0 * k1) * u2))
        h = 0.5 + 0.5 * t
        a = (u * h).astype(BF)
        act[r, c] = a
        gp[r, c] = (h + (0.5 * u) * (1.0 - t * t) * (k0 + (3.0 * k0 * k1) * u2)).astype(gp.dtype)
        acc[r, :] += dot(a, wo[c, :])
        return 0

    lax.fori_loop(0, (ff // d) * (rows // rt), up, 0)

    def mid(i, _):
        r = pl.ds(pl.multiple_of(i * et, et), et)
        unit, inv = unit_rows(acc[r, :])
        out[r, :] = (unit * row(FG) + row(FS)).astype(BF)
        upv = cot[r, :].astype(F32)
        small[FG:FG + 1, :] += col_sum(upv * unit)
        small[FS:FS + 1, :] += col_sum(upv)
        ds = norm_back(upv, unit, inv, row(FG))
        dsl = ds.astype(BF)
        do[r, :] = dsl
        acc[r, :] = ds
        small[BO:BO + 1, :] += col_sum(dsl.astype(F32))
        return 0

    lax.fori_loop(0, rows // et, mid, 0)

    def down(j, _):
        c = pl.ds(pl.multiple_of(j * d, d), d)
        dwo[c, :] = dot_tn(act[:, c], do[...]).astype(dwo.dtype)
        sums = None
        for i in range(rows // rt):
            r = slice(i * rt, (i + 1) * rt)
            di = dot_nt(do[r, :], wo[c, :]) * gp[r, c].astype(F32)
            dil = di.astype(BF)
            act[r, c] = dil
            s = col_sum(dil.astype(F32))
            sums = s if sums is None else sums + s
            acc[r, :] += dot_nt(dil, wi[:, c])
        small[pl.ds(BI + j, 1), :] = sums
        dwi[:, c] = dot_tn(fl[...], act[:, c]).astype(dwi.dtype)
        return 0

    lax.fori_loop(0, ff // d, down, 0)

    def tail(i, _):
        r = pl.ds(pl.multiple_of(i * et, et), et)
        unit, inv = unit_rows(z[r, :])
        df = acc[r, :]
        small[AG:AG + 1, :] += col_sum(df * unit)
        small[ASH:ASH + 1, :] += col_sum(df)
        ds = norm_back(df, unit, inv, row(AG))
        dsum[r, :] = ds
        dsl = ds.astype(BF)
        db[r, :] = dsl
        small[OB:OB + 1, :] += col_sum(dsl.astype(F32))
        return 0

    lax.fori_loop(0, rows // et, tail, 0)


def ffn(z, cot, wi, wo, vecs, gdt):
    rows, d = z.shape
    ff = wi.shape[1]
    sd = jax.ShapeDtypeStruct
    vm = pl.BlockSpec(memory_space=pltpu.VMEM)
    return pl.pallas_call(
        ffn_body,
        in_specs=[vm] * 5,
        out_specs=[vm] * 6,
        out_shape=[sd((rows, d), BF), sd((rows, d), F32), sd((rows, d), BF), sd((d, ff), gdt), sd((ff, d), gdt),
                   sd((16, d), F32)],
        scratch_shapes=[pltpu.VMEM((rows, d), BF), pltpu.VMEM((rows, ff), BF), pltpu.VMEM((rows, ff), BF),
                        pltpu.VMEM((rows, d), F32), pltpu.VMEM((rows, d), BF)],
        compiler_params=pltpu.CompilerParams(vmem_limit_bytes=VMEM_MAX),
        name="ffn",
    )(z, cot, wi, wo, vecs)


def place():
    me = lax.axis_index("dp")
    c, x, y, z = me % 2, (me // 2) % 2, (me // 4) % 2, me // 8
    fc, fx, fy = 1 - 2 * c, 2 * (1 - 2 * x), 4 * (1 - 2 * y)
    d1 = fx * (1 - c) + fy * c
    d2 = fy * (1 - c) + fx * c
    zs = (0, 8 * (1 - 2 * (z % 2)), 16 * (1 - 2 * (z // 2)), 8 * (3 - 2 * z))
    return me, fc, d1, d2, zs


def meet(me, fc, d1, d2, zs):
    barrier = pltpu.get_barrier_semaphore()
    for off in (fc, d1, d2) + zs[1:]:
        pl.semaphore_signal(barrier, inc=1, device_id=(me + off,), device_id_type=MESH_ID)
    pl.semaphore_wait(barrier, 6)


def unit_of(ref, unit):
    return ref.at[:, unit] if len(ref.shape) == 4 else ref.at[unit]


class Gather:
    ORDER = (1, 4, 2, 5, 8, 3, 6, 9, 7, 12, 10, 13, 11, 14, 15)

    def __init__(self, where, own, out, send, recv):
        self.where, self.own, self.out, self.send, self.recv = where, own, out, send, recv

    def copy(self, slot, unit, dest, own=False):
        return pltpu.make_async_remote_copy(
            src_ref=self.own if own else unit_of(self.out, unit), dst_ref=unit_of(self.out, unit),
            send_sem=self.send.at[slot], recv_sem=self.recv.at[slot], device_id=(dest,), device_id_type=MESH_ID)

    def begin_z(self):
        me, fc, d1, d2, zs = self.where
        for k in (1, 2, 3):
            self.copy(k, me, me + zs[k], True).start()

    def begin_xy(self):
        me, fc, d1, d2, zs = self.where
        self.copy(4, me, me + d1, True).start()
        self.copy(8, me, me + d2, True).start()
        self.copy(16, me, me + fc, True).start()

    def landed(self, slot):
        me, fc, d1, d2, zs = self.where
        unit = me + zs[slot % 4] + (0, d1, d2, d1 + d2, fc, fc + d2, fc + d1, fc + d1 + d2)[slot // 4]
        self.copy(slot, unit, me).wait_recv()
        return unit

    def step(self, slot):
        me, fc, d1, d2, zs = self.where
        k, group = slot % 4, slot // 4
        unit = self.landed(slot)
        if group == 0:
            self.copy(4 + k, unit, me + d1).start()
            self.copy(8 + k, unit, me + d2).start()
        if group == 1:
            self.copy(12 + k, unit, me + d2).start()
        self.copy(16 + slot, unit, me + fc).start()

    def finish(self):
        for slot in range(16, 32):
            self.landed(slot)

    def drain(self):
        me = self.where[0]
        for slot in range(1, 32):
            self.copy(slot, me, me, slot in (1, 2, 3, 4, 8, 16)).wait_send()


LATE = ((1, 0), (4, 1), (2, 2), (5, 3), (8, 4), (3, 5), (6, 6), (9, 7), (7, 8), (12, 9), (10, 10), (13, 11))


def front_body(rb, x, segr, segc, stack, vpart, wis, wus,
               wall_o, wi_o, wu_o, vec_o, q_o, k_o, v_o, p_o, c_o, z_o, hm_o,
               wall, vg, bias, s_s, q_s, k_s, v_s, p_s, c_s, send, recv, local, outs):
    where = place()
    me = where[0]
    rows, d = x.shape
    groups = d // GW
    steps = (rows // SEQ) * (GW // 128)
    owns, targets = (stack, vpart, wis, wus), (wall, vg, wi_o, wu_o)
    mine = [pltpu.make_async_copy(o, unit_of(t, me), local.at[i]) for i, (o, t) in enumerate(zip(owns, targets))]
    for m in mine:
        m.start()
    meet(*where)
    flows = [Gather(where, o, t, send.at[i], recv.at[i]) for i, (o, t) in enumerate(zip(owns, targets))]
    early, late = flows[:2], flows[2:]
    for f in early:
        f.begin_z()
    for f in early:
        f.begin_xy()
    same_document(segr, segc, bias)
    for slot in Gather.ORDER:
        for f in early:
            f.step(slot)
        if slot == 3:
            for f in late:
                f.begin_z()
    for f in late:
        f.begin_xy()
    for f in early:
        f.finish()
    mine[0].wait()
    mine[1].wait()
    keep = pltpu.make_async_copy(wall, wall_o, outs.at[5])
    keep.start()
    vec = jnp.sum(vg[...].astype(F32), axis=0)
    vec_o[...] = vec
    hm_o[...] = jnp.full(hm_o.shape, LOW, F32)
    z_o[...] = x[...].astype(F32) + vec_o[OB:OB + 1, :]

    def put(g, i):
        src = (q_s, k_s, v_s, c_s)[i].at[g] if i < 4 else p_s.at[g]
        return pltpu.make_async_copy(src, (q_o, k_o, v_o, c_o, p_o)[i].at[g], outs.at[i])

    def group(g, _):
        cols = pl.ds(pl.multiple_of(g * GW, GW), GW)
        weight = lambda i: wall[i, :, :, cols].reshape(d, GW)
        xv = x[...]
        q_s[g] = (dot(xv, weight(0)) + vec_o[QB:QB + 1, cols]).astype(BF)
        k_s[g] = dot(xv, weight(1)).astype(BF)
        v_s[g] = (dot(xv, weight(2)) + vec_o[VB:VB + 1, cols]).astype(BF)

        def one_pair(it, _):
            pair_forward(g, it, rb, q_s.at[g], k_s.at[g], v_s.at[g], p_s.at[g], c_s.at[g], hm_o, bias, s_s)
            for slot, when in LATE:
                @pl.when(g * steps + it == when)
                def _():
                    for f in late:
                        f.step(slot)
            return 0

        lax.fori_loop(0, steps, one_pair, 0)
        for i in range(5):
            put(g, i).start()
        return 0

    lax.fori_loop(0, groups, group, 0)
    wo = wall[3].reshape(d, d)
    for g in range(groups):
        z_o[...] += dot(c_s[g], wo[g * GW:(g + 1) * GW, :])
    done = [slot for slot, _ in LATE]
    for slot in Gather.ORDER:
        if slot not in done:
            for f in late:
                f.step(slot)
    for f in late:
        f.finish()
    mine[2].wait()
    mine[3].wait()
    for f in flows:
        f.drain()
    keep.wait()
    for g in range(groups):
        for i in range(5):
            put(g, i).wait()


def front(rb, x, segr, segc, stack, vpart, wis, wus, n):
    rows, d = x.shape
    groups = d // GW
    maps = (rows // SEQ) * (GW // HD)
    sd = jax.ShapeDtypeStruct
    vm, hbm = pl.BlockSpec(memory_space=pltpu.VMEM), pl.BlockSpec(memory_space=pl.ANY)
    whole = lambda a: a.shape[:-2] + (n,) + a.shape[-2:]
    act = (groups, rows, GW)
    return pl.pallas_call(
        front_body,
        in_specs=[pl.BlockSpec(memory_space=pltpu.SMEM)] + [vm] * 7,
        out_specs=[hbm] * 3 + [vm] + [hbm] * 5 + [vm] * 2,
        out_shape=[sd(whole(stack), BF), sd(whole(wis), BF), sd(whole(wus), BF), sd((16, d), F32),
                   sd(act, BF), sd(act, BF), sd(act, BF), sd((groups, maps, SEQ, SEQ), BF), sd(act, BF),
                   sd((rows, d), F32), sd((16, 128), F32)],
        scratch_shapes=[pltpu.VMEM(whole(stack), BF), pltpu.VMEM(whole(vpart), BF),
                        pltpu.VMEM((rows // SEQ, SEQ, SEQ), F32), pltpu.VMEM((2, SEQ, SEQ), F32),
                        pltpu.VMEM(act, BF), pltpu.VMEM(act, BF), pltpu.VMEM(act, BF),
                        pltpu.VMEM((groups, maps, SEQ, SEQ), BF), pltpu.VMEM(act, BF),
                        pltpu.SemaphoreType.DMA((4, 32)), pltpu.SemaphoreType.DMA((4, 32)),
                        pltpu.SemaphoreType.DMA((4,)), pltpu.SemaphoreType.DMA((6,))],
        compiler_params=pltpu.CompilerParams(collective_id=0, has_side_effects=True, vmem_limit_bytes=VMEM_MAX),
        name="front",
    )(rb, x, segr, segc, stack, vpart, wis, wus)


class Scatter:
    def __init__(self, where, grad, own, rp, r1, r2, rz, sems, lsem):
        self.where, self.grad, self.own = where, grad, own
        self.rp, self.r1, self.r2, self.rz, self.sems, self.lsem = rp, r1, r2, rz, sems, lsem

    def remote(self, src, dst, slot, off):
        return pltpu.make_async_remote_copy(
            src_ref=src, dst_ref=dst, send_sem=self.sems.at[0, slot], recv_sem=self.sems.at[1, slot],
            device_id=(self.where[0] + off,), device_id_type=MESH_ID)

    def begin(self):
        me, fc, d1, d2, zs = self.where
        for a in (1, 0):
            for b in (1, 0):
                for k in range(4):
                    self.remote(unit_of(self.grad, me + fc + a * d2 + b * d1 + zs[k]), self.rp.at[a, b, k], a, fc).start()
            if self.own is not None:
                for b in (1, 0):
                    for k in range(4):
                        pltpu.make_async_copy(unit_of(self.grad, me + a * d1 + b * d2 + zs[k]), self.own.at[a, b, k],
                                              self.lsem.at[a]).start()

    def pair(self, a):
        me, fc, d1, d2, zs = self.where
        self.remote(self.rp.at[a], self.rp.at[a], a, fc).wait_recv()
        if self.own is not None:
            pltpu.make_async_copy(self.own.at[a], self.own.at[a], self.lsem.at[a]).wait()
        for b in (1, 0):
            for k in range(4):
                held = self.own[a, b, k] if self.own is not None else (
                    unit_of(self.grad, me + a * d1 + b * d2 + zs[k])[...])
                self.rp[a, b, k] = (held.astype(F32) + self.rp[a, b, k].astype(F32)).astype(BF)
            if a == 1:
                self.remote(self.rp.at[1, b], self.r1.at[b], 2 + b, d1).start()

    def first(self, b):
        me, fc, d1, d2, zs = self.where
        self.remote(self.rp.at[1, b], self.r1.at[b], 2 + b, d1).wait_recv()
        self.rp[0, b] = (self.rp[0, b].astype(F32) + self.r1[b].astype(F32)).astype(BF)
        if b == 1:
            self.remote(self.rp.at[0, 1], self.r2, 4, d2).start()

    def second(self):
        me, fc, d1, d2, zs = self.where
        self.remote(self.rp.at[0, 1], self.r2, 4, d2).wait_recv()
        for k in (1, 2, 3):
            self.rp[0, 0, k] = (self.rp[0, 0, k].astype(F32) + self.r2[k].astype(F32)).astype(BF)
            self.remote(self.rp.at[0, 0, k], self.rz.at[k - 1], 4 + k, zs[k]).start()

    def last(self):
        me, fc, d1, d2, zs = self.where
        total = self.rp[0, 0, 0].astype(F32) + self.r2[0].astype(F32)
        for k in (1, 2, 3):
            self.remote(self.rp.at[0, 0, k], self.rz.at[k - 1], 4 + k, zs[k]).wait_recv()
            total = total + self.rz[k - 1].astype(F32)
        return total

    def drain(self):
        me, fc, d1, d2, zs = self.where
        for a in (1, 0):
            self.remote(self.rp.at[a], self.rp.at[a], a, fc).wait_send()
        for b in (1, 0):
            self.remote(self.rp.at[1, b], self.r1.at[b], 2 + b, d1).wait_send()
        self.remote(self.rp.at[0, 1], self.r2, 4, d2).wait_send()
        for k in (1, 2, 3):
            self.remote(self.rp.at[0, 0, k], self.rz.at[k - 1], 4 + k, zs[k]).wait_send()


def scatter_buffers(shape, own):
    bufs = [pltpu.VMEM((2, 2, 4) + shape, BF)] if own else []
    return bufs + [pltpu.VMEM((2, 2, 4) + shape, BF), pltpu.VMEM((2, 4) + shape, BF), pltpu.VMEM((4,) + shape, BF),
                   pltpu.VMEM((3,) + shape, BF)]


class Vectors:
    def __init__(self, where, held, got, sems):
        self.where, self.held, self.got, self.sems = where, held, got, sems

    def remote(self, src, slot, off):
        return pltpu.make_async_remote_copy(
            src_ref=self.held.at[src], dst_ref=self.got.at[slot], send_sem=self.sems.at[0, slot],
            recv_sem=self.sems.at[1, slot], device_id=(self.where[0] + off,), device_id_type=MESH_ID)

    def merge(self, a, b):
        row = lax.broadcasted_iota(jnp.int32, a.shape, 0)
        return jnp.where(row == TOP, jnp.maximum(a, b), a + b)

    def step(self, i):
        me, fc, d1, d2, zs = self.where
        offs = (fc, d1, d2)
        if i > 0:
            self.remote(i - 1, i - 1, offs[i - 1]).wait_recv()
            self.held[i] = self.merge(self.held[i - 1], self.got[i - 1])
        if i < 3:
            self.remote(i, i, offs[i]).start()
        else:
            for k in (1, 2, 3):
                self.remote(3, 2 + k, zs[k]).start()

    def last(self):
        me, fc, d1, d2, zs = self.where
        total = self.held[3]
        for k in (1, 2, 3):
            self.remote(3, 2 + k, zs[k]).wait_recv()
            total = self.merge(total, self.got[2 + k])
        for i, off in enumerate((fc, d1, d2)):
            self.remote(i, i, off).wait_send()
        for k in (1, 2, 3):
            self.remote(3, 2 + k, zs[k]).wait_send()
        return total


def back_body(x_h, db_h, dsum_h, wall_h, q_h, k_h, v_h, c_h, p_h, small, hm, gu, gi,
              dx, o_q, o_k, o_v, o_o, o_i, o_u, vout, *rest):
    (x, db, wall, q, k, v, c, p, dc, dq, dk, dv, dp_s, ds_s, go, gg, held, got, sems, lsems, vsems, isem) = rest[:22]
    bufs = rest[22:]
    where = place()
    rows, d = x.shape
    groups = d // GW
    n = go.shape[0]
    steps = (rows // SEQ) * (GW // 128)
    small_flow = Vectors(where, held, got, vsems)
    up_flow = Scatter(where, gu, *bufs[0:5], sems.at[0], lsems.at[0])
    in_flow = Scatter(where, gi, *bufs[5:10], sems.at[1], lsems.at[1])
    out_flow = Scatter(where, go, None, *bufs[10:14], sems.at[2], None)
    group_flow = [Scatter(where, gg.at[g], None, *bufs[14 + 4 * g:18 + 4 * g], sems.at[3 + g], None)
                  for g in range(groups)]

    def fetch(i):
        pairs = ((db_h, db), (wall_h.at[3], wall.at[3]), (c_h, c), (dsum_h, dx), (x_h, x),
                 (wall_h.at[pl.ds(0, 3)], wall.at[pl.ds(0, 3)]))
        return pltpu.make_async_copy(*pairs[i], isem.at[i])

    def fetch_group(g, i):
        src = (v_h, q_h, k_h, p_h)[i].at[g]
        dst = ((v, q, k)[i].at[g] if i < 3 else p.at[lax.rem(g, 2)])
        return pltpu.make_async_copy(src, dst, isem.at[6 + 4 * lax.rem(g, 2) + i])

    for i in range(3):
        fetch(i).start()
    for i in range(4):
        fetch_group(0, i).start()
    for i in range(3, 6):
        fetch(i).start()
    meet(*where)
    up_flow.begin()
    in_flow.begin()
    for i in range(3):
        fetch(i).wait()

    dbv = db[...]
    go[...] = jnp.concatenate([dot_tn(c[g], dbv) for g in range(groups)], axis=0).astype(BF).reshape(go.shape)
    out_flow.begin()

    events = {
        0: [(up_flow.pair, 1)], 1: [(in_flow.pair, 1)], 2: [(up_flow.pair, 0)], 3: [(in_flow.pair, 0)],
        4: [(out_flow.pair, 1)], 5: [(up_flow.first, 1), (out_flow.pair, 0)], 6: [(in_flow.first, 1)],
        7: [(up_flow.first, 0)], 8: [(in_flow.first, 0), (group_flow[0].pair, 1)],
        9: [(out_flow.first, 1), (up_flow.second,)], 10: [(out_flow.first, 0), (group_flow[0].pair, 0)],
        11: [(in_flow.second,)],
    }

    def group(g, _):
        cols = pl.ds(pl.multiple_of(g * GW, GW), GW)
        weight = lambda i: wall[i, :, cols]
        for i in range(4):
            fetch_group(g, i).wait()

        @pl.when(g + 1 < groups)
        def _():
            for i in range(4):
                fetch_group(g + 1, i).start()

        dc[...] = dot_nt(db[...], wall[3, cols, :]).astype(BF)

        def one_pair(it, _):
            pair_backward(it, q.at[g], k.at[g], v.at[g], p.at[lax.rem(g, 2)], dc, dq, dk, dv, dp_s, ds_s)
            for when, todo in events.items():
                @pl.when(g * steps + it == when)
                def _():
                    for fn, *a in todo:
                        fn(*a)
            return 0

        lax.fori_loop(0, steps, one_pair, 0)
        held[0, QB:QB + 1, cols] = col_sum(dq[...].astype(F32))
        held[0, VB:VB + 1, cols] = col_sum(dv[...].astype(F32))

        @pl.when(g == 0)
        def _():
            for i in range(3, 6):
                fetch(i).wait()

        xv = x[...]
        for i, part in enumerate((dq, dk, dv)):
            gg[g, i] = dot_tn(xv, part[...]).astype(BF).reshape(n, d // n, GW)
        for i in range(groups):
            @pl.when(g == i)
            def _():
                group_flow[i].begin()
        dx[...] += dot_nt(dq[...], weight(0)) + dot_nt(dk[...], weight(1)) + dot_nt(dv[...], weight(2))
        return 0

    held[0] = small[...]
    lax.fori_loop(0, groups, group, 0)
    diag = lax.broadcasted_iota(jnp.int32, hm.shape, 0) == lax.broadcasted_iota(jnp.int32, hm.shape, 1)
    held[0, TOP:TOP + 1, 0:128] = jnp.sum(jnp.where(diag, hm[...], 0.0), axis=0, keepdims=True)
    small_flow.step(0)
    g1, g2 = group_flow[1:]
    g1.pair(1)
    g2.pair(1)
    small_flow.step(1)
    out_flow.second()
    group_flow[0].first(1)
    g1.pair(0)
    g2.pair(0)
    small_flow.step(2)
    g1.first(1)
    g2.first(1)
    small_flow.step(3)
    group_flow[0].first(0)
    g1.first(0)
    g2.first(0)
    for f in group_flow:
        f.second()
    o_u[...] = up_flow.last()
    o_i[...] = in_flow.last()
    o_o[...] = out_flow.last()
    for g, f in enumerate(group_flow):
        t = f.last()
        for i, o in enumerate((o_q, o_k, o_v)):
            o[:, g * GW:(g + 1) * GW] = t[i]
    vout[...] = small_flow.last()
    for f in [up_flow, in_flow, out_flow] + group_flow:
        f.drain()


def back(x, db, dsum, wall, q, k, v, c, p, small, hm, gu, gi):
    rows, d = x.shape
    groups, n = d // GW, gu.shape[0]
    maps = (rows // SEQ) * (GW // HD)
    r, ru, ff = d // n, gu.shape[1], gi.shape[2]
    sd = jax.ShapeDtypeStruct
    vm, hbm = pl.BlockSpec(memory_space=pltpu.VMEM), pl.BlockSpec(memory_space=pl.ANY)
    act = pltpu.VMEM((groups, rows, GW), BF)
    one = pltpu.VMEM((rows, GW), BF)
    bufs = scatter_buffers((ru, d), True) + scatter_buffers((r, ff), True) + scatter_buffers((r, d), False)
    for _ in range(groups):
        bufs += scatter_buffers((3, r, GW), False)
    return pl.pallas_call(
        back_body,
        in_specs=[hbm] * 9 + [vm] * 2 + [hbm] * 2,
        out_specs=[vm] * 8,
        out_shape=[sd((rows, d), F32)] + [sd((r, d), F32)] * 4 + [sd((r, ff), F32), sd((ru, d), F32), sd((16, d), F32)],
        scratch_shapes=[pltpu.VMEM((rows, d), BF), pltpu.VMEM((rows, d), BF), pltpu.VMEM((4, d, d), BF),
                        act, act, act, act, pltpu.VMEM((2, maps, SEQ, SEQ), BF), one, one, one, one,
                        pltpu.VMEM((2, SEQ, SEQ), F32), pltpu.VMEM((2, SEQ, SEQ), BF),
                        pltpu.VMEM((n, r, d), BF), pltpu.VMEM((groups, 3, n, r, GW), BF),
                        pltpu.VMEM((4, 16, d), F32), pltpu.VMEM((6, 16, d), F32),
                        pltpu.SemaphoreType.DMA((3 + groups, 2, 8)), pltpu.SemaphoreType.DMA((2, 2)),
                        pltpu.SemaphoreType.DMA((2, 6)), pltpu.SemaphoreType.DMA((14,))] + bufs,
        compiler_params=pltpu.CompilerParams(collective_id=1, has_side_effects=True, vmem_limit_bytes=VMEM_MAX),
        name="back",
    )(x, db, dsum, wall, q, k, v, c, p, small, hm, gu, gi)


def attn_fwd_body(rb, x, segr, segc, wq, wk, wv, wo, vecs, q, k, v, p, c, z, hm, bias, s_s):
    g = pl.program_id(0)

    @pl.when(g == 0)
    def _():
        same_document(segr, segc, bias)
        hm[...] = jnp.full(hm.shape, LOW, F32)
        z[...] = x[...].astype(F32) + vecs[OB:OB + 1, :]

    cols = pl.ds(pl.multiple_of(g * GW, GW), GW)
    xv = x[...]
    q[...] = (dot(xv, wq[...]) + vecs[QB:QB + 1, cols]).astype(BF)
    k[...] = dot(xv, wk[...]).astype(BF)
    v[...] = (dot(xv, wv[...]) + vecs[VB:VB + 1, cols]).astype(BF)

    def one_pair(it, _):
        pair_forward(g, it, rb, q, k, v, p, c, hm, bias, s_s)
        return 0

    lax.fori_loop(0, x.shape[0] // SEQ * (GW // 128), one_pair, 0)
    z[...] += dot(c[...], wo[...])


def attn_fwd(rb, x, segr, segc, wall, vecs):
    rows, d = x.shape
    groups, seqs = d // GW, rows // SEQ
    maps = seqs * (GW // HD)
    full = lambda shape: pl.BlockSpec(shape, lambda g, *_: (0,) * len(shape))
    col = lambda i: pl.BlockSpec((None, d, GW), lambda g, *_: (i, 0, g))
    act = pl.BlockSpec((None, rows, GW), lambda g, *_: (g, 0, 0))
    sd = jax.ShapeDtypeStruct
    return pl.pallas_call(
        attn_fwd_body,
        grid_spec=pltpu.PrefetchScalarGridSpec(
            num_scalar_prefetch=1, grid=(groups,),
            in_specs=[full((rows, d)), full((seqs, SEQ)), full((rows, 1)), col(0), col(1), col(2),
                      pl.BlockSpec((None, GW, d), lambda g, *_: (3, g, 0)), full((16, d))],
            out_specs=[act, act, act, pl.BlockSpec((None, maps, SEQ, SEQ), lambda g, *_: (g, 0, 0, 0)), act,
                       full((rows, d)), full((16, 128))],
            scratch_shapes=[pltpu.VMEM((seqs, SEQ, SEQ), F32), pltpu.VMEM((2, SEQ, SEQ), F32)]),
        out_shape=[sd((groups, rows, GW), BF)] * 3
        + [sd((groups, maps, SEQ, SEQ), BF), sd((groups, rows, GW), BF), sd((rows, d), F32), sd((16, 128), F32)],
        compiler_params=pltpu.CompilerParams(vmem_limit_bytes=VMEM_MAX),
        name="attn_fwd",
    )(rb, x, segr, segc, wall, wall, wall, wall, vecs)


def attn_bwd_body(x, db, wq, wk, wv, wo, q, k, v, p, c, dsum, dw, dqb, dvb, dx, dc, dq, dk, dv, dp_s, ds_s):
    g = pl.program_id(0)

    @pl.when(g == 0)
    def _():
        dx[...] = dsum[...]

    dbv = db[...]
    cols = pl.ds(pl.multiple_of(g * GW, GW), GW)
    dc[...] = dot_nt(dbv, wo[...]).astype(BF)
    dw[3, cols, :] = dot_tn(c[...], dbv).astype(dw.dtype)

    def one_pair(it, _):
        pair_backward(it, q, k, v, p, dc, dq, dk, dv, dp_s, ds_s)
        return 0

    lax.fori_loop(0, x.shape[0] // SEQ * (GW // 128), one_pair, 0)
    dqb[...] = col_sum(dq[...].astype(F32))
    dvb[...] = col_sum(dv[...].astype(F32))
    xv = x[...]
    for i, part in enumerate((dq, dk, dv)):
        dw[i, :, cols] = dot_tn(xv, part[...]).astype(dw.dtype)
    dx[...] += dot_nt(dq[...], wq[...]) + dot_nt(dk[...], wk[...]) + dot_nt(dv[...], wv[...])


def attn_bwd(x, db, wall, q, k, v, p, c, dsum, gdt):
    rows, d = x.shape
    groups = d // GW
    maps = (rows // SEQ) * (GW // HD)
    full = lambda shape: pl.BlockSpec(shape, lambda g: (0,) * len(shape), pipeline_mode=pl.Buffered(1))
    col = lambda i: pl.BlockSpec((None, d, GW), lambda g: (i, 0, g))
    vec = pl.BlockSpec((1, GW), lambda g: (0, g))
    act = pl.BlockSpec((None, rows, GW), lambda g: (g, 0, 0))
    sd = jax.ShapeDtypeStruct
    return pl.pallas_call(
        attn_bwd_body,
        grid=(groups,),
        in_specs=[full((rows, d)), full((rows, d)), col(0), col(1), col(2),
                  pl.BlockSpec((None, GW, d), lambda g: (3, g, 0)), act, act, act,
                  pl.BlockSpec((None, maps, SEQ, SEQ), lambda g: (g, 0, 0, 0)), act, full((rows, d))],
        out_specs=[full((4, d, d)), vec, vec, full((rows, d))],
        out_shape=[sd((4, d, d), gdt)] + [sd((1, d), F32)] * 2 + [sd((rows, d), F32)],
        scratch_shapes=[pltpu.VMEM((rows, GW), BF)] * 4
        + [pltpu.VMEM((2, SEQ, SEQ), F32), pltpu.VMEM((2, SEQ, SEQ), BF)],
        compiler_params=pltpu.CompilerParams(vmem_limit_bytes=VMEM_MAX),
        name="attn_bwd",
    )(x, db, wall, wall, wall, wall, q, k, v, p, c, dsum)


def far_layer(n, rb, tokens, segr, segc, cot, stack, vec_part, inner_weight, outer_weight):
    d, ff = tokens.shape[1], inner_weight.shape[1]
    wall = lax.all_gather(stack, "dp", axis=1, tiled=True)
    wi, wu = (lax.all_gather(a, "dp", axis=0, tiled=True) for a in (inner_weight, outer_weight))
    vecs = lax.psum(vec_part.astype(F32), "dp")
    q, k, v, p, c, z, hm = attn_fwd(rb, tokens, segr, segc, wall, vecs)
    out, dsum, db, dwi, dwu, small = ffn(z, cot, wi, wu, vecs, F32)
    dwall, dqb, dvb, dx = attn_bwd(tokens, db, wall, q, k, v, p, c, dsum, F32)
    mine = small.at[QB:QB + 1].set(dqb).at[VB:VB + 1].set(dvb).at[TOP, :hm.shape[0]].set(hm[:, 0])
    scatter = lambda a, at: lax.psum_scatter(a, "dp", scatter_dimension=at, tiled=True)
    dwu, dwi, dwall = scatter(dwu, 0), scatter(dwi, 0), scatter(dwall, 1)
    row = lax.broadcasted_iota(jnp.int32, mine.shape, 0)
    total = jnp.where(row == TOP, lax.pmax(mine, "dp"), lax.psum(mine, "dp"))
    return out, dx, dwall[0], dwall[1], dwall[2], dwall[3], dwi, dwu, total


def near_layer(n, rb, tokens, segr, segc, cot, stack, vec_part, inner_weight, outer_weight):
    d, ff = tokens.shape[1], inner_weight.shape[1]
    wall, wi, wu, vecs, q, k, v, p, c, z, hm = front(rb, tokens, segr, segc, stack, vec_part, inner_weight,
                                                     outer_weight, n)
    out, dsum, db, dwi, dwu, small = ffn(z, cot, wi.reshape(d, ff), wu.reshape(ff, d), vecs, BF)
    dx, dwq, dwk, dwv, dwo, dwi, dwu, total = back(
        tokens, db, dsum, wall.reshape(4, d, d), q, k, v, c, p, small, hm, dwu.reshape(n, -1, d), dwi.reshape(n, -1, ff))
    return out, dx, dwq, dwk, dwv, dwo, dwi, dwu, total


def vectors_part(me, n, vecs, inner_bias):
    part = vecs[0].shape[0]
    d = part * n
    rows = jnp.tile(jnp.stack(vecs), (1, n))
    rows = jnp.where(lax.broadcasted_iota(jnp.int32, rows.shape, 1) // part == me, rows, 0)
    flat = jnp.tile(inner_bias, n)
    flat = jnp.where(lax.broadcasted_iota(jnp.int32, flat.shape, 0) // inner_bias.shape[0] == me, flat, 0)
    flat = flat.reshape(-1, d)
    rest = jnp.zeros((16 - rows.shape[0] - flat.shape[0], d), BF)
    return jnp.concatenate([rows, flat, rest], axis=0)


def per_device(n, tokens, segment_ids, random_blocks, clip_limit, query_weight, query_bias, key_weight, value_weight,
               value_bias, output_weight, output_bias, attn_gain, attn_shift, inner_weight, inner_bias,
               outer_weight, outer_bias, final_gain, final_shift, out_cotangent):
    heads = random_blocks.shape[0]
    d, ff = tokens.shape[1], inner_weight.shape[1]
    me = lax.axis_index("dp")
    stack = jnp.stack([query_weight, key_weight, value_weight, output_weight])
    names = (query_bias, value_bias, output_bias, attn_gain, attn_shift, outer_bias, final_gain, final_shift)
    part, wide = query_bias.shape[0], inner_bias.shape[0]
    layer = near_layer if n == 32 and query_weight.shape[0] % 8 == 0 else far_layer
    out, dx, dwq, dwk, dwv, dwo, dwi, dwu, total = layer(
        n, random_blocks.reshape(-1), tokens, segment_ids.reshape(-1, SEQ), segment_ids.reshape(-1, 1), out_cotangent,
        stack, vectors_part(me, n, names, inner_bias), inner_weight, outer_weight)
    vec8 = lax.dynamic_slice(total, (0, me * part), (8, part))
    dqb, dvb, dob, dag, dash, dbo, dfg, dfs = (vec8[i] for i in range(8))
    dbi = lax.dynamic_slice(total[BI:BI + ff // d].reshape(-1), (me * wide,), (wide,))
    head_maxima = total[TOP, :heads]
    limit = clip_limit[0].astype(F32)
    factor = jnp.sqrt(jnp.minimum(1.0, limit / jnp.maximum(head_maxima, 1.0)))
    columns = jnp.repeat(factor, HD)[None, :]
    cq = (query_weight.astype(F32) * columns).astype(BF)
    ck = (key_weight.astype(F32) * columns).astype(BF)
    return (out, dx, dwq, dqb, dwk, dwv, dvb, dwo, dob, dag, dash, dwi, dbi, dwu, dbo, dfg, dfs, cq, ck, head_maxima)


def solution(mesh):
    mat, vec, rep = P("dp", None), P("dp"), P()
    in_specs = (mat, vec, rep, rep, mat, vec, mat, mat, vec, mat, vec, vec, vec, mat, vec, mat, vec, vec, vec, mat)
    out_specs = (mat, mat, mat, vec, mat, mat, vec, mat, vec, vec, vec, mat, vec, mat, vec, vec, vec, mat, mat, rep)
    return jax.shard_map(partial(per_device, mesh.shape["dp"]), mesh=mesh, in_specs=in_specs, out_specs=out_specs,
                         check_vma=False)
```

```python
from functools import partial
import math

import jax
import jax.numpy as jnp
from jax import lax
from jax.experimental import pallas as pl
from jax.experimental.pallas import tpu as pltpu
from jax.sharding import PartitionSpec as P

HD = 64
BLOCK = 64
SEQ = 512
GW = 256
BF = jnp.bfloat16
F32 = jnp.float32
LOW = -1e30
VMEM_MAX = 67043328
MESH_ID = pl.DeviceIdType.MESH
QB, VB, OB, AG, ASH, BO, FG, FS, BI, TOP = 0, 1, 2, 3, 4, 5, 6, 7, 8, 12


def dot(a, b):
    return jnp.dot(a, b, preferred_element_type=F32)


def dot_nt(a, b):
    return lax.dot_general(a, b, (((1,), (1,)), ((), ())), preferred_element_type=F32)


def dot_tn(a, b):
    return lax.dot_general(a, b, (((0,), (0,)), ((), ())), preferred_element_type=F32)


def col_sum(v):
    return jnp.sum(v, axis=0, keepdims=True)


def first_half():
    return lax.broadcasted_iota(jnp.int32, (1, 128), 1) < HD


def same_document(segr, segc, bias):
    for s in range(segr.shape[0]):
        kseg = segr[s:s + 1, :]
        for c in range(SEQ // BLOCK):
            qseg = segc[s * SEQ + c * BLOCK:s * SEQ + (c + 1) * BLOCK, :]
            bias[s, c * BLOCK:(c + 1) * BLOCK, :] = jnp.where((qseg == kseg) & (kseg != 0), 0.0, LOW)


def pair_forward(g, it, rb, q, k, v, p, ctx, hm, bias, s_s):
    pairs = GW // 128
    s, pair = it // pairs, it % pairs
    rows = pl.ds(pl.multiple_of(s * SEQ, SEQ), SEQ)
    lanes = pl.ds(pl.multiple_of(pair * 128, 128), 128)
    lane_block = lax.broadcasted_iota(jnp.int32, (1, SEQ), 1) // BLOCK
    half = first_half()
    last = SEQ // BLOCK - 2
    qp, kp, vp = q[rows, lanes], k[rows, lanes], v[rows, lanes]
    outs = []
    for j in range(2):
        head = g * (2 * pairs) + pair * 2 + j
        keys = pl.ds(pl.multiple_of((pair * 2 + j) * SEQ, SEQ), SEQ)
        mine = half if j == 0 else jnp.logical_not(half)
        s_s[j] = dot_nt(jnp.where(mine, qp * 0.125, 0).astype(BF), kp)
        at = head * (6 * 3)
        miss1 = 18 - (rb[at] + rb[at + 1] + rb[at + 2])
        miss6 = 10 - (rb[at + 15] + rb[at + 16] + rb[at + 17])
        skip1 = jnp.where(lane_block == miss1, LOW, 0.0)
        skip6 = jnp.where(lane_block == miss6, LOW, 0.0)
        tops = None
        for c in range(SEQ // BLOCK):
            cr = slice(c * BLOCK, (c + 1) * BLOCK)
            sv = s_s[j, cr, :] + bias[s, cr, :]
            if c == 1:
                sv = sv + skip1
            if c == last:
                sv = sv + skip6
            top = jnp.max(sv, axis=1, keepdims=True)
            live = top > -1e29
            e = jnp.exp(sv - jnp.where(live, top, 0.0))
            total = jnp.sum(e, axis=1, keepdims=True) + jnp.where(live, 0.0, 1.0)
            p[pl.ds(pl.multiple_of(s * SEQ + c * BLOCK, BLOCK), BLOCK), keys] = (e * (1.0 / total)).astype(BF)
            tops = top if tops is None else jnp.maximum(tops, top)
        top = jnp.max(tops, axis=0, keepdims=True)
        hm[pl.ds(head, 1), :] = jnp.maximum(hm[pl.ds(head, 1), :], top)
        outs.append(dot(p[rows, keys], vp))
    ctx[rows, lanes] = jnp.where(half, outs[0], outs[1]).astype(BF)


def pair_backward(it, q, k, v, p, dc, dq, dk, dv, dp_s, ds_s):
    pairs = GW // 128
    s, pair = it // pairs, it % pairs
    rows = pl.ds(pl.multiple_of(s * SEQ, SEQ), SEQ)
    lanes = pl.ds(pl.multiple_of(pair * 128, 128), 128)
    half = first_half()
    qp, kp, vp, dcp = q[rows, lanes], k[rows, lanes], v[rows, lanes], dc[rows, lanes]
    dqs, dks, dvs = [], [], []
    for j in range(2):
        mine = half if j == 0 else jnp.logical_not(half)
        keys = pl.ds(pl.multiple_of((pair * 2 + j) * SEQ, SEQ), SEQ)
        dp_s[j][...] = dot_nt(jnp.where(mine, dcp, 0).astype(BF), vp)
        for c in range(SEQ // BLOCK):
            cr = slice(c * BLOCK, (c + 1) * BLOCK)
            pv = p[pl.ds(pl.multiple_of(s * SEQ + c * BLOCK, BLOCK), BLOCK), keys].astype(F32)
            sl = dp_s[j][cr, :]
            mean = jnp.sum(pv * sl, axis=1, keepdims=True)
            ds_s[j][cr, :] = (pv * (sl - mean)).astype(BF)
        dqs.append(dot(ds_s[j][...], kp))
        dks.append(dot_tn(ds_s[j][...], qp))
        dvs.append(dot_tn(p[rows, keys], dcp))
    dq[rows, lanes] = (jnp.where(half, dqs[0], dqs[1]) * 0.125).astype(BF)
    dk[rows, lanes] = (jnp.where(half, dks[0], dks[1]) * 0.125).astype(BF)
    dv[rows, lanes] = jnp.where(half, dvs[0], dvs[1]).astype(BF)


def unit_rows(z):
    mean = jnp.mean(z, axis=-1, keepdims=True)
    c = z - mean
    inv = lax.rsqrt(jnp.mean(c * c, axis=-1, keepdims=True) + 1e-12)
    return c * inv, inv


def norm_back(up, unit, inv, gain):
    e = up * gain
    spread = jnp.mean(e, axis=-1, keepdims=True)
    along = jnp.mean(e * unit, axis=-1, keepdims=True)
    return inv * (e - spread - unit * along)


def ffn_body(z, cot, wi, wo, vecs, out, dsum, db, dwi, dwo, small, fl, act, gp, acc, do):
    rows, d = z.shape
    ff = wi.shape[1]
    rt, et = 512, 128
    k0, k1 = math.sqrt(2.0 / math.pi), 0.044715
    row = lambda i: vecs[i:i + 1, :]
    small[...] = jnp.zeros(small.shape, F32)

    def prep(i, _):
        r = pl.ds(pl.multiple_of(i * et, et), et)
        unit, _inv = unit_rows(z[r, :])
        first = unit * row(AG) + row(ASH)
        fl[r, :] = first.astype(BF)
        acc[r, :] = first + row(BO)
        return 0

    lax.fori_loop(0, rows // et, prep, 0)

    def up(i, _):
        j = i // (rows // rt)
        r = pl.ds(pl.multiple_of((i % (rows // rt)) * rt, rt), rt)
        c = pl.ds(pl.multiple_of(j * d, d), d)
        u = dot(fl[r, :], wi[:, c]) + vecs[pl.ds(BI + j, 1), :]
        u2 = u * u
        t = jnp.tanh(u * (k0 + (k0 * k1) * u2))
        h = 0.5 + 0.5 * t
        a = (u * h).astype(BF)
        act[r, c] = a
        gp[r, c] = (h + (0.5 * u) * (1.0 - t * t) * (k0 + (3.0 * k0 * k1) * u2)).astype(gp.dtype)
        acc[r, :] += dot(a, wo[c, :])
        return 0

    lax.fori_loop(0, (ff // d) * (rows // rt), up, 0)

    def mid(i, _):
        r = pl.ds(pl.multiple_of(i * et, et), et)
        unit, inv = unit_rows(acc[r, :])
        out[r, :] = (unit * row(FG) + row(FS)).astype(BF)
        upv = cot[r, :].astype(F32)
        small[FG:FG + 1, :] += col_sum(upv * unit)
        small[FS:FS + 1, :] += col_sum(upv)
        ds = norm_back(upv, unit, inv, row(FG))
        dsl = ds.astype(BF)
        do[r, :] = dsl
        acc[r, :] = ds
        small[BO:BO + 1, :] += col_sum(dsl.astype(F32))
        return 0

    lax.fori_loop(0, rows // et, mid, 0)

    def down(j, _):
        c = pl.ds(pl.multiple_of(j * d, d), d)
        dwo[c, :] = dot_tn(act[:, c], do[...]).astype(dwo.dtype)
        sums = None
        for i in range(rows // rt):
            r = slice(i * rt, (i + 1) * rt)
            di = dot_nt(do[r, :], wo[c, :]) * gp[r, c].astype(F32)
            dil = di.astype(BF)
            act[r, c] = dil
            s = col_sum(dil.astype(F32))
            sums = s if sums is None else sums + s
            acc[r, :] += dot_nt(dil, wi[:, c])
        small[pl.ds(BI + j, 1), :] = sums
        dwi[:, c] = dot_tn(fl[...], act[:, c]).astype(dwi.dtype)
        return 0

    lax.fori_loop(0, ff // d, down, 0)

    def tail(i, _):
        r = pl.ds(pl.multiple_of(i * et, et), et)
        unit, inv = unit_rows(z[r, :])
        df = acc[r, :]
        small[AG:AG + 1, :] += col_sum(df * unit)
        small[ASH:ASH + 1, :] += col_sum(df)
        ds = norm_back(df, unit, inv, row(AG))
        dsum[r, :] = ds
        dsl = ds.astype(BF)
        db[r, :] = dsl
        small[OB:OB + 1, :] += col_sum(dsl.astype(F32))
        return 0

    lax.fori_loop(0, rows // et, tail, 0)


def ffn(z, cot, wi, wo, vecs, gdt):
    rows, d = z.shape
    ff = wi.shape[1]
    sd = jax.ShapeDtypeStruct
    vm = pl.BlockSpec(memory_space=pltpu.VMEM)
    return pl.pallas_call(
        ffn_body,
        in_specs=[vm] * 5,
        out_specs=[vm] * 6,
        out_shape=[sd((rows, d), BF), sd((rows, d), F32), sd((rows, d), BF), sd((d, ff), gdt), sd((ff, d), gdt),
                   sd((16, d), F32)],
        scratch_shapes=[pltpu.VMEM((rows, d), BF), pltpu.VMEM((rows, ff), BF), pltpu.VMEM((rows, ff), BF),
                        pltpu.VMEM((rows, d), F32), pltpu.VMEM((rows, d), BF)],
        compiler_params=pltpu.CompilerParams(vmem_limit_bytes=VMEM_MAX),
        name="ffn",
    )(z, cot, wi, wo, vecs)


def place():
    me = lax.axis_index("dp")
    c, x, y, z = me % 2, (me // 2) % 2, (me // 4) % 2, me // 8
    fc, fx, fy = 1 - 2 * c, 2 * (1 - 2 * x), 4 * (1 - 2 * y)
    d1 = fx * (1 - c) + fy * c
    d2 = fy * (1 - c) + fx * c
    zs = (0, 8 * (1 - 2 * (z % 2)), 16 * (1 - 2 * (z // 2)), 8 * (3 - 2 * z))
    return me, fc, d1, d2, zs


def greet(me, fc, d1, d2, zs):
    for off in (fc, d1, d2) + zs[1:]:
        pl.semaphore_signal(pltpu.get_barrier_semaphore(), inc=1, device_id=(me + off,), device_id_type=MESH_ID)


def meet():
    pl.semaphore_wait(pltpu.get_barrier_semaphore(), 6)


def unit_of(ref, unit):
    return ref.at[:, unit] if len(ref.shape) == 4 else ref.at[unit]


class Gather:
    ORDER = (1, 4, 2, 5, 8, 3, 6, 9, 7, 12, 10, 13, 11, 14, 15)

    def __init__(self, where, own, out, send, recv):
        self.where, self.own, self.out, self.send, self.recv = where, own, out, send, recv

    def copy(self, slot, unit, dest, own=False):
        return pltpu.make_async_remote_copy(
            src_ref=self.own if own else unit_of(self.out, unit), dst_ref=unit_of(self.out, unit),
            send_sem=self.send.at[slot], recv_sem=self.recv.at[slot], device_id=(dest,), device_id_type=MESH_ID)

    def begin_z(self):
        me, fc, d1, d2, zs = self.where
        for k in (1, 2, 3):
            self.copy(k, me, me + zs[k], True).start()

    def begin_xy(self):
        me, fc, d1, d2, zs = self.where
        self.copy(4, me, me + d1, True).start()
        self.copy(8, me, me + d2, True).start()
        self.copy(16, me, me + fc, True).start()

    def landed(self, slot):
        me, fc, d1, d2, zs = self.where
        unit = me + zs[slot % 4] + (0, d1, d2, d1 + d2, fc, fc + d2, fc + d1, fc + d1 + d2)[slot // 4]
        self.copy(slot, unit, me).wait_recv()
        return unit

    def step(self, slot):
        me, fc, d1, d2, zs = self.where
        k, group = slot % 4, slot // 4
        unit = self.landed(slot)
        if group == 0:
            self.copy(4 + k, unit, me + d1).start()
            self.copy(8 + k, unit, me + d2).start()
        if group == 1:
            self.copy(12 + k, unit, me + d2).start()
        self.copy(16 + slot, unit, me + fc).start()

    def finish(self):
        for slot in range(16, 32):
            self.landed(slot)

    def drain(self):
        me = self.where[0]
        for slot in range(1, 32):
            self.copy(slot, me, me, slot in (1, 2, 3, 4, 8, 16)).wait_send()


LATE = ((1, 0), (4, 1), (2, 2), (5, 3), (8, 4), (3, 5), (6, 6), (9, 7), (7, 8), (12, 9), (10, 10), (13, 11))


def front_body(rb, x, segr, segc, stack, vpart, wis, wus,
               wall_o, wi_o, wu_o, vec_o, q_o, k_o, v_o, p_o, c_o, z_o, hm_o,
               wall, vg, bias, s_s, q_s, k_s, v_s, p_s, c_s, send, recv, local, outs):
    where = place()
    me = where[0]
    rows, d = x.shape
    groups = d // GW
    steps = (rows // SEQ) * (GW // 128)
    owns, targets = (stack, vpart, wis, wus), (wall, vg, wi_o, wu_o)
    mine = [pltpu.make_async_copy(o, unit_of(t, me), local.at[i]) for i, (o, t) in enumerate(zip(owns, targets))]
    for m in mine:
        m.start()
    greet(*where)
    meet()
    flows = [Gather(where, o, t, send.at[i], recv.at[i]) for i, (o, t) in enumerate(zip(owns, targets))]
    early, late = flows[:2], flows[2:]
    for f in early:
        f.begin_z()
    for f in early:
        f.begin_xy()
    same_document(segr, segc, bias)
    for slot in Gather.ORDER:
        for f in early:
            f.step(slot)
        if slot == 3:
            for f in late:
                f.begin_z()
    for f in late:
        f.begin_xy()
    for f in early:
        f.finish()
    mine[0].wait()
    mine[1].wait()
    keep = pltpu.make_async_copy(wall, wall_o, outs.at[5])
    keep.start()
    vec = jnp.sum(vg[...].astype(F32), axis=0)
    vec_o[...] = vec
    hm_o[...] = jnp.full(hm_o.shape, LOW, F32)
    z_o[...] = x[...].astype(F32) + vec_o[OB:OB + 1, :]

    def put(g, i):
        src = (q_s, k_s, v_s, c_s)[i].at[g] if i < 4 else p_s.at[g]
        return pltpu.make_async_copy(src, (q_o, k_o, v_o, c_o, p_o)[i].at[g], outs.at[i])

    def group(g, _):
        cols = pl.ds(pl.multiple_of(g * GW, GW), GW)
        weight = lambda i: wall[i, :, :, cols].reshape(d, GW)
        xv = x[...]
        q_s[g] = (dot(xv, weight(0)) + vec_o[QB:QB + 1, cols]).astype(BF)
        k_s[g] = dot(xv, weight(1)).astype(BF)
        v_s[g] = (dot(xv, weight(2)) + vec_o[VB:VB + 1, cols]).astype(BF)

        def one_pair(it, _):
            pair_forward(g, it, rb, q_s.at[g], k_s.at[g], v_s.at[g], p_s.at[g], c_s.at[g], hm_o, bias, s_s)
            for slot, when in LATE:
                @pl.when(g * steps + it == when)
                def _():
                    for f in late:
                        f.step(slot)
            return 0

        lax.fori_loop(0, steps, one_pair, 0)
        for i in range(5):
            put(g, i).start()
        return 0

    lax.fori_loop(0, groups, group, 0)
    wo = wall[3].reshape(d, d)
    for g in range(groups):
        z_o[...] += dot(c_s[g], wo[g * GW:(g + 1) * GW, :])
    done = [slot for slot, _ in LATE]
    for slot in Gather.ORDER:
        if slot not in done:
            for f in late:
                f.step(slot)
    for f in late:
        f.finish()
    mine[2].wait()
    mine[3].wait()
    for f in flows:
        f.drain()
    keep.wait()
    for g in range(groups):
        for i in range(5):
            put(g, i).wait()


def front(rb, x, segr, segc, stack, vpart, wis, wus, n):
    rows, d = x.shape
    groups = d // GW
    maps = (groups, rows, GW // HD * SEQ)
    sd = jax.ShapeDtypeStruct
    vm, hbm = pl.BlockSpec(memory_space=pltpu.VMEM), pl.BlockSpec(memory_space=pl.ANY)
    whole = lambda a: a.shape[:-2] + (n,) + a.shape[-2:]
    act = (groups, rows, GW)
    return pl.pallas_call(
        front_body,
        in_specs=[pl.BlockSpec(memory_space=pltpu.SMEM)] + [vm] * 7,
        out_specs=[hbm] * 3 + [vm] + [hbm] * 5 + [vm] * 2,
        out_shape=[sd(whole(stack), BF), sd(whole(wis), BF), sd(whole(wus), BF), sd((16, d), F32),
                   sd(act, BF), sd(act, BF), sd(act, BF), sd(maps, BF), sd(act, BF),
                   sd((rows, d), F32), sd((16, 128), F32)],
        scratch_shapes=[pltpu.VMEM(whole(stack), BF), pltpu.VMEM(whole(vpart), BF),
                        pltpu.VMEM((rows // SEQ, SEQ, SEQ), F32), pltpu.VMEM((2, SEQ, SEQ), F32),
                        pltpu.VMEM(act, BF), pltpu.VMEM(act, BF), pltpu.VMEM(act, BF),
                        pltpu.VMEM(maps, BF), pltpu.VMEM(act, BF),
                        pltpu.SemaphoreType.DMA((4, 32)), pltpu.SemaphoreType.DMA((4, 32)),
                        pltpu.SemaphoreType.DMA((4,)), pltpu.SemaphoreType.DMA((6,))],
        compiler_params=pltpu.CompilerParams(collective_id=0, has_side_effects=True, vmem_limit_bytes=VMEM_MAX),
        name="front",
    )(rb, x, segr, segc, stack, vpart, wis, wus)


class Scatter:
    def __init__(self, where, grad, rp, r1, r2, rz, sems):
        self.where, self.grad, self.rp, self.r1, self.r2, self.rz, self.sems = where, grad, rp, r1, r2, rz, sems

    def remote(self, src, dst, slot, off):
        return pltpu.make_async_remote_copy(
            src_ref=src, dst_ref=dst, send_sem=self.sems.at[0, slot], recv_sem=self.sems.at[1, slot],
            device_id=(self.where[0] + off,), device_id_type=MESH_ID)

    def begin(self):
        me, fc, d1, d2, zs = self.where
        for a in (1, 0):
            for b in (1, 0):
                for k in range(4):
                    self.remote(unit_of(self.grad, me + fc + a * d2 + b * d1 + zs[k]), self.rp.at[a, b, k], a, fc).start()

    def pair(self, a):
        me, fc, d1, d2, zs = self.where
        self.remote(self.rp.at[a], self.rp.at[a], a, fc).wait_recv()
        for b in (1, 0):
            for k in range(4):
                held = unit_of(self.grad, me + a * d1 + b * d2 + zs[k])[...]
                self.rp[a, b, k] = (held.astype(F32) + self.rp[a, b, k].astype(F32)).astype(BF)
            if a == 1:
                self.remote(self.rp.at[1, b], self.r1.at[b], 2 + b, d1).start()

    def first(self, b):
        me, fc, d1, d2, zs = self.where
        self.remote(self.rp.at[1, b], self.r1.at[b], 2 + b, d1).wait_recv()
        self.rp[0, b] = (self.rp[0, b].astype(F32) + self.r1[b].astype(F32)).astype(BF)
        if b == 1:
            self.remote(self.rp.at[0, 1], self.r2, 4, d2).start()

    def second(self):
        me, fc, d1, d2, zs = self.where
        self.remote(self.rp.at[0, 1], self.r2, 4, d2).wait_recv()
        for k in (1, 2, 3):
            self.rp[0, 0, k] = (self.rp[0, 0, k].astype(F32) + self.r2[k].astype(F32)).astype(BF)
            self.remote(self.rp.at[0, 0, k], self.rz.at[k - 1], 4 + k, zs[k]).start()

    def near(self):
        return self.rp[0, 0, 0].astype(F32) + self.r2[0].astype(F32)

    def far(self, k):
        self.remote(self.rp.at[0, 0, k], self.rz.at[k - 1], 4 + k, self.where[4][k]).wait_recv()
        return self.rz[k - 1].astype(F32)

    def last(self):
        return self.near() + self.far(1) + self.far(2) + self.far(3)

    def core_sent(self):
        for a in (1, 0):
            self.remote(self.rp.at[a], self.rp.at[a], a, self.where[1]).wait_send()

    def drain(self):
        me, fc, d1, d2, zs = self.where
        for b in (1, 0):
            self.remote(self.rp.at[1, b], self.r1.at[b], 2 + b, d1).wait_send()
        self.remote(self.rp.at[0, 1], self.r2, 4, d2).wait_send()
        for k in (1, 2, 3):
            self.remote(self.rp.at[0, 0, k], self.rz.at[k - 1], 4 + k, zs[k]).wait_send()


class Plane(Scatter):
    def __init__(self, k, *rest):
        Scatter.__init__(self, *rest)
        self.k = k

    def begin(self):
        me, fc, d1, d2, zs = self.where
        for a in (1, 0):
            for b in (1, 0):
                self.remote(self.grad.at[lax.rem(me, 8) + fc + a * d2 + b * d1], self.rp.at[a, b], a, fc).start()

    def pair(self, a):
        me, fc, d1, d2, zs = self.where
        self.remote(self.rp.at[a], self.rp.at[a], a, fc).wait_recv()
        for b in (1, 0):
            held = self.grad[lax.rem(me, 8) + a * d1 + b * d2]
            self.rp[a, b] = (held.astype(F32) + self.rp[a, b].astype(F32)).astype(BF)
            if a == 1:
                self.remote(self.rp.at[1, b], self.r1.at[b], 2 + b, d1).start()

    def along(self):
        return self.remote(self.rp.at[0, 0], self.rz.at[self.k - 1], 4 + self.k, self.where[4][self.k])

    def second(self):
        self.remote(self.rp.at[0, 1], self.r2, 4, self.where[3]).wait_recv()
        if self.k:
            self.rp[0, 0] = (self.rp[0, 0].astype(F32) + self.r2[...].astype(F32)).astype(BF)
            self.along().start()

    def near(self):
        return self.rp[0, 0].astype(F32) + self.r2[...].astype(F32)

    def far(self):
        self.along().wait_recv()
        return self.rz[self.k - 1].astype(F32)

    def drain(self):
        me, fc, d1, d2, zs = self.where
        for b in (1, 0):
            self.remote(self.rp.at[1, b], self.r1.at[b], 2 + b, d1).wait_send()
        self.remote(self.rp.at[0, 1], self.r2, 4, d2).wait_send()
        if self.k:
            self.along().wait_send()


def scatter_buffers(lead, shape):
    return [pltpu.VMEM(lead + (2, 2, 4) + shape, BF), pltpu.VMEM(lead + (2, 4) + shape, BF),
            pltpu.VMEM(lead + (4,) + shape, BF), pltpu.VMEM(lead + (3,) + shape, BF)]


class Vectors:
    def __init__(self, where, held, got, sems):
        self.where, self.held, self.got, self.sems = where, held, got, sems

    def remote(self, src, slot, off):
        return pltpu.make_async_remote_copy(
            src_ref=self.held.at[src], dst_ref=self.got.at[slot], send_sem=self.sems.at[0, slot],
            recv_sem=self.sems.at[1, slot], device_id=(self.where[0] + off,), device_id_type=MESH_ID)

    def merge(self, a, b):
        row = lax.broadcasted_iota(jnp.int32, a.shape, 0)
        return jnp.where(row == TOP, jnp.maximum(a, b), a + b)

    def step(self, i):
        me, fc, d1, d2, zs = self.where
        offs = (fc, d1, d2)
        if i > 0:
            self.remote(i - 1, i - 1, offs[i - 1]).wait_recv()
            self.held[i] = self.merge(self.held[i - 1], self.got[i - 1])
        if i < 3:
            self.remote(i, i, offs[i]).start()
        else:
            for k in (1, 2, 3):
                self.remote(3, 2 + k, zs[k]).start()

    def last(self):
        me, fc, d1, d2, zs = self.where
        total = self.held[3]
        for k in (1, 2, 3):
            self.remote(3, 2 + k, zs[k]).wait_recv()
            total = self.merge(total, self.got[2 + k])
        for i, off in enumerate((fc, d1, d2)):
            self.remote(i, i, off).wait_send()
        for k in (1, 2, 3):
            self.remote(3, 2 + k, zs[k]).wait_send()
        return total


def rear_body(z_h, cot_h, wi_h, wu_h, x_h, wall_h, q_h, k_h, v_h, c_h, p_h, vecs, hm,
              out_h, dx, o_q, o_k, o_v, o_o, o_i, o_u, vout,
              wi, wu, ag, z, fl, do, db, gu, gi, gg, held, got, usems, nsems, sems, vsems, isem, osem, *bufs):
    where = place()
    zi = where[0] // 8
    rows, d = z.shape
    ff = wi.shape[1]
    groups, n = gg.shape[0], gi.shape[1]
    rt, et = 512, 128
    k0, k1 = math.sqrt(2.0 / math.pi), 0.044715
    act, gp, small = ag.at[0], ag.at[1], held.at[0]
    row = lambda i: vecs[i:i + 1, :]
    part = lambda j: pl.ds(pl.multiple_of(j * d, d), d)
    beside = lambda k: (zi % 2 + k % 2 - 2 * (zi % 2) * (k % 2)) + 2 * (zi // 2 + k // 2 - 2 * (zi // 2) * (k // 2))

    def up_flow(it):
        k = (it + 1) % 4 if isinstance(it, int) else None
        return Plane(k, where, gu.at[lax.rem(it, 2)], bufs[0].at[it], bufs[1].at[it], bufs[2].at[it], bufs[3], usems.at[it])

    def in_flow(it):
        return Scatter(where, gi.at[lax.rem(it, 2)], *(b.at[it] for b in bufs[4:8]), nsems.at[it])

    small_flow = Vectors(where, held, got, vsems)
    out_flow = Scatter(where, gi.at[0], *bufs[8:12], sems.at[0])
    group_flow = [Scatter(where, gg.at[g], *bufs[12 + 4 * g:16 + 4 * g], sems.at[1 + g]) for g in range(groups)]

    def get_up(j):
        return pltpu.make_async_copy(wi_h.at[:, part(j)], wi.at[:, part(j)], isem.at[j])

    def get_down(j):
        return pltpu.make_async_copy(wu_h.at[part(j)], wu.at[part(j)], isem.at[4 + j])

    def get_wall(i):
        return pltpu.make_async_copy(wall_h.at[i], wi.at[:, pl.ds(i * d, d)], isem.at[i])

    def get_ctx(g):
        return pltpu.make_async_copy(c_h.at[g], fl.at[:, pl.ds(g * GW, GW)], isem.at[4 + g])

    get_z = pltpu.make_async_copy(z_h, z, isem.at[8])
    get_cot = pltpu.make_async_copy(cot_h, do, isem.at[9])
    get_x = pltpu.make_async_copy(x_h, do, isem.at[9])
    put_out = pltpu.make_async_copy(db, out_h, osem)
    mid_cols = pl.ds(0, GW // HD * SEQ)

    def get_group(g, i):
        cols = pl.ds(pl.multiple_of(g * GW, GW), GW)
        src = (v_h, q_h, k_h, p_h)[i].at[g]
        dst = wu.at[pl.ds((2, 0, 1)[i] * rows, rows), cols] if i < 3 else ag.at[lax.rem(g, 2), :, mid_cols]
        return pltpu.make_async_copy(src, dst, isem.at[10 + 4 * lax.rem(g, 2) + i])

    get_z.start()
    for j in range(ff // d):
        get_up(j).start()
        get_down(j).start()
    get_cot.start()
    greet(*where)
    small[...] = jnp.zeros(small.shape, F32)
    get_z.wait()

    def prep(i, _):
        r = pl.ds(pl.multiple_of(i * et, et), et)
        unit, _inv = unit_rows(z[r, :])
        first = unit * row(AG) + row(ASH)
        fl[r, :] = first.astype(BF)
        dx[r, :] = first + row(BO)
        return 0

    lax.fori_loop(0, rows // et, prep, 0)

    def up(i, _):
        j = i // (rows // rt)
        r = pl.ds(pl.multiple_of((i % (rows // rt)) * rt, rt), rt)
        c = part(j)

        @pl.when(i % (rows // rt) == 0)
        def _():
            get_up(j).wait()
            get_down(j).wait()

        u = dot(fl[r, :], wi[:, c]) + vecs[pl.ds(BI + j, 1), :]
        u2 = u * u
        t = jnp.tanh(u * (k0 + (k0 * k1) * u2))
        h = 0.5 + 0.5 * t
        a = (u * h).astype(BF)
        act[r, c] = a
        gp[r, c] = (h + (0.5 * u) * (1.0 - t * t) * (k0 + (3.0 * k0 * k1) * u2)).astype(BF)
        dx[r, :] += dot(a, wu[c, :])
        return 0

    lax.fori_loop(0, (ff // d) * (rows // rt), up, 0)
    get_cot.wait()

    def mid(i, _):
        r = pl.ds(pl.multiple_of(i * et, et), et)
        unit, inv = unit_rows(dx[r, :])
        db[r, :] = (unit * row(FG) + row(FS)).astype(BF)
        upv = do[r, :].astype(F32)
        small[FG:FG + 1, :] += col_sum(upv * unit)
        small[FS:FS + 1, :] += col_sum(upv)
        ds = norm_back(upv, unit, inv, row(FG))
        dsl = ds.astype(BF)
        do[r, :] = dsl
        dx[r, :] = ds
        small[BO:BO + 1, :] += col_sum(dsl.astype(F32))
        return 0

    lax.fori_loop(0, rows // et, mid, 0)
    put_out.start()
    meet()

    def down(it, _):
        j = beside((it + 1) % 4)
        c = part(j)
        slot = lax.rem(it, 2)

        @pl.when(it >= 2)
        def _():
            up_flow(it - 2).core_sent()

        gu[slot] = dot_tn(act[:, c], do[...]).astype(BF).reshape(gu.shape[1:])
        up_flow(it).begin()
        sums = None
        for i in range(rows // rt):
            r = slice(i * rt, (i + 1) * rt)
            di = dot_nt(do[r, :], wu[c, :]) * gp[r, c].astype(F32)
            dil = di.astype(BF)
            act[r, c] = dil
            s = col_sum(dil.astype(F32))
            sums = s if sums is None else sums + s
            dx[r, :] += dot_nt(dil, wi[:, c])
            if i == 0:
                @pl.when(it >= 1)
                def _():
                    in_flow(it - 1).pair(1)
                    in_flow(it - 1).pair(0)
        small[pl.ds(BI + j, 1), :] = sums
        up_flow(it).pair(1)
        up_flow(it).pair(0)

        @pl.when(it >= 2)
        def _():
            in_flow(it - 2).core_sent()

        gi[slot] = dot_tn(fl[...], act[:, c]).reshape(gi.shape[1:]).astype(BF)
        in_flow(it).begin()

        @pl.when(it >= 2)
        def _():
            for f in (up_flow(it - 2), in_flow(it - 2)):
                f.first(1)
                f.first(0)

        return 0

    lax.fori_loop(0, ff // d, down, 0)
    get_wall(3).start()
    for i in range(4):
        get_group(0, i).start()
    for g in range(groups):
        get_ctx(g).start()
    get_x.start()
    for i in range(3):
        get_wall(i).start()
    put_out.wait()

    def tail(i, _):
        r = pl.ds(pl.multiple_of(i * et, et), et)
        unit, inv = unit_rows(z[r, :])
        df = dx[r, :]
        small[AG:AG + 1, :] += col_sum(df * unit)
        small[ASH:ASH + 1, :] += col_sum(df)
        ds = norm_back(df, unit, inv, row(AG))
        dx[r, :] = ds
        dsl = ds.astype(BF)
        db[r, :] = dsl
        small[OB:OB + 1, :] += col_sum(dsl.astype(F32))
        return 0

    lax.fori_loop(0, rows // et, tail, 0)
    in_flow(3).pair(1)
    in_flow(3).pair(0)
    for g in range(groups):
        get_ctx(g).wait()
    in_flow(2).core_sent()
    gi[0] = dot_tn(fl[...], db[...]).reshape(gi.shape[1:]).astype(BF)
    out_flow.begin()
    get_wall(3).wait()

    steps = (rows // SEQ) * (GW // 128)
    edge = GW // HD * SEQ
    dc, dq, dk, dv = (act.at[:, pl.ds(edge + i * GW, GW)] for i in range(4))
    dp_s = [z.at[pl.ds(j * SEQ, SEQ), pl.ds(0, SEQ)] for j in range(2)]
    ds_s = [gp.at[pl.ds(j * SEQ, SEQ), pl.ds(edge, SEQ)] for j in range(2)]
    both = lambda f: [(f.first, 1), (f.first, 0)]
    g0, g1, g2 = group_flow
    events = {
        0: [(up_flow(0).second,), (in_flow(0).second,), (out_flow.pair, 1)],
        1: [(out_flow.pair, 0)] + both(up_flow(2)),
        2: both(in_flow(2)) + [(up_flow(1).second,)],
        3: [(in_flow(1).second,)],
        4: both(up_flow(3)),
        5: both(in_flow(3)) + [(g0.pair, 1)],
        6: [(g0.pair, 0), (up_flow(2).second,), (out_flow.first, 1)],
        7: [(out_flow.first, 0), (in_flow(2).second,)],
        8: [(up_flow(3).second,), (in_flow(3).second,), (g0.first, 1)],
        9: [(g0.first, 0), (g1.pair, 1)],
        10: [(g1.pair, 0), (out_flow.second,)],
        11: [(g0.second,), (g1.first, 1)],
    }

    def group(g, _):
        cols = pl.ds(pl.multiple_of(g * GW, GW), GW)
        for i in range(4):
            get_group(g, i).wait()

        @pl.when(g + 1 < groups)
        def _():
            for i in range(4):
                get_group(g + 1, i).start()

        dc[...] = dot_nt(db[...], wi[cols, 3 * d:4 * d]).astype(BF)
        heads = [wu.at[pl.ds(i * rows, rows), cols] for i in range(3)]

        def one_pair(it, _):
            pair_backward(it, *heads, ag.at[lax.rem(g, 2)], dc, dq, dk, dv, dp_s, ds_s)
            for when, todo in events.items():
                @pl.when(g * steps + it == when)
                def _():
                    for fn, *a in todo:
                        fn(*a)
            return 0

        lax.fori_loop(0, steps, one_pair, 0)
        small[QB:QB + 1, cols] = col_sum(dq[...].astype(F32))
        small[VB:VB + 1, cols] = col_sum(dv[...].astype(F32))

        @pl.when(g == 0)
        def _():
            get_x.wait()
            for i in range(3):
                get_wall(i).wait()

        xv = do[...]
        for i, grad in enumerate((dq, dk, dv)):
            gg[g, i] = dot_tn(xv, grad[...]).reshape(n, d // n, GW).astype(BF)
        for i in range(groups):
            @pl.when(g == i)
            def _():
                group_flow[i].begin()
        weight = lambda i: wi[:, pl.ds(pl.multiple_of(i * d + g * GW, GW), GW)]
        dx[...] += dot_nt(dq[...], weight(0)) + dot_nt(dk[...], weight(1)) + dot_nt(dv[...], weight(2))
        return 0

    lax.fori_loop(0, groups, group, 0)
    diag = lax.broadcasted_iota(jnp.int32, hm.shape, 0) == lax.broadcasted_iota(jnp.int32, hm.shape, 1)
    small[TOP:TOP + 1, 0:128] = jnp.sum(jnp.where(diag, hm[...], 0.0), axis=0, keepdims=True)
    small_flow.step(0)
    g2.pair(1)
    g2.pair(0)
    small_flow.step(1)
    g1.first(0)
    g2.first(1)
    small_flow.step(2)
    g1.second()
    g2.first(0)
    small_flow.step(3)
    o_u[...] = up_flow(3).near() + up_flow(0).far() + up_flow(1).far() + up_flow(2).far()
    for it in range(4):
        k = (it + 1) % 4
        total = in_flow(it).near()
        for m in (1, 2, 3):
            total = total + in_flow(((k ^ m) - 1) % 4).far(m)
        o_i[:, part(beside(k))] = total
    o_o[...] = out_flow.last()
    g2.second()
    for g, f in enumerate(group_flow):
        t = f.last()
        for i, o in enumerate((o_q, o_k, o_v)):
            o[:, g * GW:(g + 1) * GW] = t[i]
    vout[...] = small_flow.last()
    up_flow(2).core_sent()
    up_flow(3).core_sent()
    in_flow(3).core_sent()
    for f in [out_flow] + group_flow:
        f.core_sent()
    for f in [up_flow(i) for i in range(4)] + [in_flow(i) for i in range(4)] + [out_flow] + group_flow:
        f.drain()


def rear(n, z, cot, wi, wu, x, wall, q, k, v, c, p, vecs, hm):
    rows, d = x.shape
    ff = wi.shape[1]
    groups = d // GW
    r, ru = d // n, ff // n
    sd = jax.ShapeDtypeStruct
    vm, hbm = pl.BlockSpec(memory_space=pltpu.VMEM), pl.BlockSpec(memory_space=pl.ANY)
    flat = pltpu.VMEM((rows, d), BF)
    bufs = [pltpu.VMEM((4, 2, 2, ru, d), BF), pltpu.VMEM((4, 2, ru, d), BF), pltpu.VMEM((4, ru, d), BF),
            pltpu.VMEM((3, ru, d), BF)]
    bufs += scatter_buffers((4,), (r, d)) + scatter_buffers((), (r, d))
    for _ in range(groups):
        bufs += scatter_buffers((), (3, r, GW))
    return pl.pallas_call(
        rear_body,
        in_specs=[hbm] * 11 + [vm] * 2,
        out_specs=[hbm] + [vm] * 8,
        out_shape=[sd((rows, d), BF), sd((rows, d), F32)] + [sd((r, d), F32)] * 4
        + [sd((r, ff), F32), sd((ru, d), F32), sd((16, d), F32)],
        scratch_shapes=[pltpu.VMEM((d, ff), BF), pltpu.VMEM((ff, d), BF), pltpu.VMEM((2, rows, ff), BF),
                        pltpu.VMEM((rows, d), F32), flat, flat, flat, pltpu.VMEM((2, 8, ru, d), BF),
                        pltpu.VMEM((2, n, r, d), BF), pltpu.VMEM((groups, 3, n, r, GW), BF),
                        pltpu.VMEM((4, 16, d), F32), pltpu.VMEM((6, 16, d), F32),
                        pltpu.SemaphoreType.DMA((4, 2, 8)), pltpu.SemaphoreType.DMA((4, 2, 8)),
                        pltpu.SemaphoreType.DMA((1 + groups, 2, 8)), pltpu.SemaphoreType.DMA((2, 6)),
                        pltpu.SemaphoreType.DMA((18,)), pltpu.SemaphoreType.DMA] + bufs,
        compiler_params=pltpu.CompilerParams(collective_id=1, has_side_effects=True, vmem_limit_bytes=VMEM_MAX),
        name="rear",
    )(z, cot, wi, wu, x, wall, q, k, v, c, p, vecs, hm)


def attn_fwd_body(rb, x, segr, segc, wq, wk, wv, wo, vecs, q, k, v, p, c, z, hm, bias, s_s):
    g = pl.program_id(0)

    @pl.when(g == 0)
    def _():
        same_document(segr, segc, bias)
        hm[...] = jnp.full(hm.shape, LOW, F32)
        z[...] = x[...].astype(F32) + vecs[OB:OB + 1, :]

    cols = pl.ds(pl.multiple_of(g * GW, GW), GW)
    xv = x[...]
    q[...] = (dot(xv, wq[...]) + vecs[QB:QB + 1, cols]).astype(BF)
    k[...] = dot(xv, wk[...]).astype(BF)
    v[...] = (dot(xv, wv[...]) + vecs[VB:VB + 1, cols]).astype(BF)

    def one_pair(it, _):
        pair_forward(g, it, rb, q, k, v, p, c, hm, bias, s_s)
        return 0

    lax.fori_loop(0, x.shape[0] // SEQ * (GW // 128), one_pair, 0)
    z[...] += dot(c[...], wo[...])


def attn_fwd(rb, x, segr, segc, wall, vecs):
    rows, d = x.shape
    groups, seqs = d // GW, rows // SEQ
    keys = GW // HD * SEQ
    full = lambda shape: pl.BlockSpec(shape, lambda g, *_: (0,) * len(shape))
    col = lambda i: pl.BlockSpec((None, d, GW), lambda g, *_: (i, 0, g))
    act = pl.BlockSpec((None, rows, GW), lambda g, *_: (g, 0, 0))
    sd = jax.ShapeDtypeStruct
    return pl.pallas_call(
        attn_fwd_body,
        grid_spec=pltpu.PrefetchScalarGridSpec(
            num_scalar_prefetch=1, grid=(groups,),
            in_specs=[full((rows, d)), full((seqs, SEQ)), full((rows, 1)), col(0), col(1), col(2),
                      pl.BlockSpec((None, GW, d), lambda g, *_: (3, g, 0)), full((16, d))],
            out_specs=[act, act, act, pl.BlockSpec((None, rows, keys), lambda g, *_: (g, 0, 0)), act,
                       full((rows, d)), full((16, 128))],
            scratch_shapes=[pltpu.VMEM((seqs, SEQ, SEQ), F32), pltpu.VMEM((2, SEQ, SEQ), F32)]),
        out_shape=[sd((groups, rows, GW), BF)] * 3
        + [sd((groups, rows, keys), BF), sd((groups, rows, GW), BF), sd((rows, d), F32), sd((16, 128), F32)],
        compiler_params=pltpu.CompilerParams(vmem_limit_bytes=VMEM_MAX),
        name="attn_fwd",
    )(rb, x, segr, segc, wall, wall, wall, wall, vecs)


def attn_bwd_body(x, db, wq, wk, wv, wo, q, k, v, p, c, dsum, dw, dqb, dvb, dx, dc, dq, dk, dv, dp_s, ds_s):
    g = pl.program_id(0)

    @pl.when(g == 0)
    def _():
        dx[...] = dsum[...]

    dbv = db[...]
    cols = pl.ds(pl.multiple_of(g * GW, GW), GW)
    dc[...] = dot_nt(dbv, wo[...]).astype(BF)
    dw[3, cols, :] = dot_tn(c[...], dbv).astype(dw.dtype)

    def one_pair(it, _):
        pair_backward(it, q, k, v, p, dc, dq, dk, dv, [dp_s.at[0], dp_s.at[1]], [ds_s.at[0], ds_s.at[1]])
        return 0

    lax.fori_loop(0, x.shape[0] // SEQ * (GW // 128), one_pair, 0)
    dqb[...] = col_sum(dq[...].astype(F32))
    dvb[...] = col_sum(dv[...].astype(F32))
    xv = x[...]
    for i, part in enumerate((dq, dk, dv)):
        dw[i, :, cols] = dot_tn(xv, part[...]).astype(dw.dtype)
    dx[...] += dot_nt(dq[...], wq[...]) + dot_nt(dk[...], wk[...]) + dot_nt(dv[...], wv[...])


def attn_bwd(x, db, wall, q, k, v, p, c, dsum, gdt):
    rows, d = x.shape
    groups = d // GW
    keys = GW // HD * SEQ
    full = lambda shape: pl.BlockSpec(shape, lambda g: (0,) * len(shape), pipeline_mode=pl.Buffered(1))
    col = lambda i: pl.BlockSpec((None, d, GW), lambda g: (i, 0, g))
    vec = pl.BlockSpec((1, GW), lambda g: (0, g))
    act = pl.BlockSpec((None, rows, GW), lambda g: (g, 0, 0))
    sd = jax.ShapeDtypeStruct
    return pl.pallas_call(
        attn_bwd_body,
        grid=(groups,),
        in_specs=[full((rows, d)), full((rows, d)), col(0), col(1), col(2),
                  pl.BlockSpec((None, GW, d), lambda g: (3, g, 0)), act, act, act,
                  pl.BlockSpec((None, rows, keys), lambda g: (g, 0, 0)), act, full((rows, d))],
        out_specs=[full((4, d, d)), vec, vec, full((rows, d))],
        out_shape=[sd((4, d, d), gdt)] + [sd((1, d), F32)] * 2 + [sd((rows, d), F32)],
        scratch_shapes=[pltpu.VMEM((rows, GW), BF)] * 4
        + [pltpu.VMEM((2, SEQ, SEQ), F32), pltpu.VMEM((2, SEQ, SEQ), BF)],
        compiler_params=pltpu.CompilerParams(vmem_limit_bytes=VMEM_MAX),
        name="attn_bwd",
    )(x, db, wall, wall, wall, wall, q, k, v, p, c, dsum)


def far_layer(n, rb, tokens, segr, segc, cot, stack, vec_part, inner_weight, outer_weight):
    d, ff = tokens.shape[1], inner_weight.shape[1]
    wall = lax.all_gather(stack, "dp", axis=1, tiled=True)
    wi, wu = (lax.all_gather(a, "dp", axis=0, tiled=True) for a in (inner_weight, outer_weight))
    vecs = lax.psum(vec_part.astype(F32), "dp")
    q, k, v, p, c, z, hm = attn_fwd(rb, tokens, segr, segc, wall, vecs)
    out, dsum, db, dwi, dwu, small = ffn(z, cot, wi, wu, vecs, F32)
    dwall, dqb, dvb, dx = attn_bwd(tokens, db, wall, q, k, v, p, c, dsum, F32)
    mine = small.at[QB:QB + 1].set(dqb).at[VB:VB + 1].set(dvb).at[TOP, :hm.shape[0]].set(hm[:, 0])
    scatter = lambda a, at: lax.psum_scatter(a, "dp", scatter_dimension=at, tiled=True)
    dwu, dwi, dwall = scatter(dwu, 0), scatter(dwi, 0), scatter(dwall, 1)
    row = lax.broadcasted_iota(jnp.int32, mine.shape, 0)
    total = jnp.where(row == TOP, lax.pmax(mine, "dp"), lax.psum(mine, "dp"))
    return out, dx, dwall[0], dwall[1], dwall[2], dwall[3], dwi, dwu, total


def near_layer(n, rb, tokens, segr, segc, cot, stack, vec_part, inner_weight, outer_weight):
    d, ff = tokens.shape[1], inner_weight.shape[1]
    wall, wi, wu, vecs, q, k, v, p, c, z, hm = front(rb, tokens, segr, segc, stack, vec_part, inner_weight,
                                                     outer_weight, n)
    out, dx, dwq, dwk, dwv, dwo, dwi, dwu, total = rear(
        n, z, cot, wi.reshape(d, ff), wu.reshape(ff, d), tokens, wall.reshape(4, d, d), q, k, v, c, p, vecs, hm)
    return out, dx, dwq, dwk, dwv, dwo, dwi, dwu, total


def vectors_part(me, n, vecs, inner_bias):
    part = vecs[0].shape[0]
    d = part * n
    rows = jnp.tile(jnp.stack(vecs), (1, n))
    rows = jnp.where(lax.broadcasted_iota(jnp.int32, rows.shape, 1) // part == me, rows, 0)
    flat = jnp.tile(inner_bias, n)
    flat = jnp.where(lax.broadcasted_iota(jnp.int32, flat.shape, 0) // inner_bias.shape[0] == me, flat, 0)
    flat = flat.reshape(-1, d)
    rest = jnp.zeros((16 - rows.shape[0] - flat.shape[0], d), BF)
    return jnp.concatenate([rows, flat, rest], axis=0)


def per_device(n, tokens, segment_ids, random_blocks, clip_limit, query_weight, query_bias, key_weight, value_weight,
               value_bias, output_weight, output_bias, attn_gain, attn_shift, inner_weight, inner_bias,
               outer_weight, outer_bias, final_gain, final_shift, out_cotangent):
    heads = random_blocks.shape[0]
    d, ff = tokens.shape[1], inner_weight.shape[1]
    me = lax.axis_index("dp")
    stack = jnp.stack([query_weight, key_weight, value_weight, output_weight])
    names = (query_bias, value_bias, output_bias, attn_gain, attn_shift, outer_bias, final_gain, final_shift)
    part, wide = query_bias.shape[0], inner_bias.shape[0]
    rows = tokens.shape[0]
    layer = near_layer if n == 32 and (rows, d, ff) == (2 * SEQ, 3 * GW, 6 * SEQ) else far_layer
    out, dx, dwq, dwk, dwv, dwo, dwi, dwu, total = layer(
        n, random_blocks.reshape(-1), tokens, segment_ids.reshape(-1, SEQ), segment_ids.reshape(-1, 1), out_cotangent,
        stack, vectors_part(me, n, names, inner_bias), inner_weight, outer_weight)
    vec8 = lax.dynamic_slice(total, (0, me * part), (8, part))
    dqb, dvb, dob, dag, dash, dbo, dfg, dfs = (vec8[i] for i in range(8))
    dbi = lax.dynamic_slice(total[BI:BI + ff // d].reshape(-1), (me * wide,), (wide,))
    head_maxima = total[TOP, :heads]
    limit = clip_limit[0].astype(F32)
    factor = jnp.sqrt(jnp.minimum(1.0, limit / jnp.maximum(head_maxima, 1.0)))
    columns = jnp.repeat(factor, HD)[None, :]
    cq = (query_weight.astype(F32) * columns).astype(BF)
    ck = (key_weight.astype(F32) * columns).astype(BF)
    return (out, dx, dwq, dqb, dwk, dwv, dvb, dwo, dob, dag, dash, dwi, dbi, dwu, dbo, dfg, dfs, cq, ck, head_maxima)


def solution(mesh):
    mat, vec, rep = P("dp", None), P("dp"), P()
    in_specs = (mat, vec, rep, rep, mat, vec, mat, mat, vec, mat, vec, vec, vec, mat, vec, mat, vec, vec, vec, mat)
    out_specs = (mat, mat, mat, vec, mat, mat, vec, mat, vec, vec, vec, mat, vec, mat, vec, vec, vec, mat, mat, rep)
    return jax.shard_map(partial(per_device, mesh.shape["dp"]), mesh=mesh, in_specs=in_specs, out_specs=out_specs,
                         check_vma=False)
```

```python
from functools import partial
import math

import jax
import jax.numpy as jnp
from jax import lax
from jax.experimental import pallas as pl
from jax.experimental.pallas import tpu as pltpu
from jax.sharding import PartitionSpec as P

HD = 64
BLOCK = 64
SEQ = 512
GW = 256
BF = jnp.bfloat16
F32 = jnp.float32
LOW = -1e30
VMEM_MAX = 67043328
MESH_ID = pl.DeviceIdType.MESH
QB, VB, OB, AG, ASH, BO, FG, FS, BI, TOP = 0, 1, 2, 3, 4, 5, 6, 7, 8, 12


def dot(a, b):
    return jnp.dot(a, b, preferred_element_type=F32)


def dot_nt(a, b):
    return lax.dot_general(a, b, (((1,), (1,)), ((), ())), preferred_element_type=F32)


def dot_tn(a, b):
    return lax.dot_general(a, b, (((0,), (0,)), ((), ())), preferred_element_type=F32)


def col_sum(v):
    return jnp.sum(v, axis=0, keepdims=True)


def first_half():
    return lax.broadcasted_iota(jnp.int32, (1, 128), 1) < HD


def same_document(key_ids, query_ids, bias):
    for s in range(bias.shape[0]):
        kseg = key_ids(s)
        for c in range(SEQ // BLOCK):
            bias[s, c * BLOCK:(c + 1) * BLOCK, :] = jnp.where((query_ids(s, c) == kseg) & (kseg != 0), 0.0, LOW)


def same_document_flat(seg, bias):
    ids = seg[...].astype(F32)
    turned = jnp.transpose(ids)
    per = SEQ // 128
    key_ids = lambda s: jnp.concatenate([ids[s * per + i:s * per + i + 1, :] for i in range(per)], axis=1)

    def query_ids(s, c):
        i, r = s * per + c * BLOCK // 128, c * BLOCK % 128
        return turned[r:r + BLOCK, i:i + 1]

    same_document(key_ids, query_ids, bias)


def whole_vectors(pieces, vec, wide):
    n, d = pieces.shape[0], vec.shape[1]
    lane = lax.broadcasted_iota(jnp.int32, (1, 128), 1)

    def spread(values, width):
        tiles = [0.0] * (d // 128)
        for i, value in enumerate(values):
            t, at = i * width // 128, i * width % 128
            moved = pltpu.roll(value, at, 1) if at else value
            tiles[t] = tiles[t] + (jnp.where(lane >= at, moved, 0.0) if at + width > 128 else moved)
            if at + width > 128:
                tiles[t + 1] = tiles[t + 1] + jnp.where(lane < at, moved, 0.0)
        return jnp.concatenate(tiles, axis=1)

    vec[0:8, :] = spread([pieces[u, 0:8, :] for u in range(n)], d // n)
    per = d // wide
    inner = [spread([pieces[j * per + i, 8:16, :] for i in range(per)], wide) for j in range(n // per)]
    for j, v in enumerate(inner):
        vec[8 + j:9 + j, :] = v[0:1, :]
    vec[8 + len(inner):16, :] = jnp.zeros((8 - len(inner), d), F32)


def pair_forward(g, it, rb, q, k, v, p, ctx, hm, bias, s_s):
    pairs = GW // 128
    s, pair = it // pairs, it % pairs
    rows = pl.ds(pl.multiple_of(s * SEQ, SEQ), SEQ)
    lanes = pl.ds(pl.multiple_of(pair * 128, 128), 128)
    lane_block = lax.broadcasted_iota(jnp.int32, (1, SEQ), 1) // BLOCK
    half = first_half()
    last = SEQ // BLOCK - 2
    qp, kp, vp = q[rows, lanes], k[rows, lanes], v[rows, lanes]
    outs = []
    for j in range(2):
        head = g * (2 * pairs) + pair * 2 + j
        keys = pl.ds(pl.multiple_of((pair * 2 + j) * SEQ, SEQ), SEQ)
        mine = half if j == 0 else jnp.logical_not(half)
        s_s[j] = dot_nt(jnp.where(mine, qp * 0.125, 0).astype(BF), kp)
        miss1, miss6 = 18 - rb(head, 0), 10 - rb(head, 5)
        skip1 = jnp.where(lane_block == miss1, LOW, 0.0)
        skip6 = jnp.where(lane_block == miss6, LOW, 0.0)
        tops = None
        for c in range(SEQ // BLOCK):
            cr = slice(c * BLOCK, (c + 1) * BLOCK)
            sv = s_s[j, cr, :] + bias[s, cr, :]
            if c == 1:
                sv = sv + skip1
            if c == last:
                sv = sv + skip6
            top = jnp.max(sv, axis=1, keepdims=True)
            live = top > -1e29
            e = jnp.exp(sv - jnp.where(live, top, 0.0))
            total = jnp.sum(e, axis=1, keepdims=True) + jnp.where(live, 0.0, 1.0)
            p[pl.ds(pl.multiple_of(s * SEQ + c * BLOCK, BLOCK), BLOCK), keys] = (e * (1.0 / total)).astype(BF)
            tops = top if tops is None else jnp.maximum(tops, top)
        top = jnp.max(tops, axis=0, keepdims=True)
        hm[pl.ds(head, 1), :] = jnp.maximum(hm[pl.ds(head, 1), :], top)
        outs.append(dot(p[rows, keys], vp))
    ctx[rows, lanes] = jnp.where(half, outs[0], outs[1]).astype(BF)


def pair_backward(it, q, k, v, p, dc, dq, dk, dv, dp_s, ds_s):
    pairs = GW // 128
    s, pair = it // pairs, it % pairs
    rows = pl.ds(pl.multiple_of(s * SEQ, SEQ), SEQ)
    lanes = pl.ds(pl.multiple_of(pair * 128, 128), 128)
    half = first_half()
    qp, kp, vp, dcp = q[rows, lanes], k[rows, lanes], v[rows, lanes], dc[rows, lanes]
    dqs, dks, dvs = [], [], []
    for j in range(2):
        mine = half if j == 0 else jnp.logical_not(half)
        keys = pl.ds(pl.multiple_of((pair * 2 + j) * SEQ, SEQ), SEQ)
        dp_s[j][...] = dot_nt(jnp.where(mine, dcp, 0).astype(BF), vp)
        for c in range(SEQ // BLOCK):
            cr = slice(c * BLOCK, (c + 1) * BLOCK)
            pv = p[pl.ds(pl.multiple_of(s * SEQ + c * BLOCK, BLOCK), BLOCK), keys].astype(F32)
            sl = dp_s[j][cr, :]
            mean = jnp.sum(pv * sl, axis=1, keepdims=True)
            ds_s[j][cr, :] = (pv * (sl - mean)).astype(BF)
        dqs.append(dot(ds_s[j][...], kp))
        dks.append(dot_tn(ds_s[j][...], qp))
        dvs.append(dot_tn(p[rows, keys], dcp))
    dq[rows, lanes] = (jnp.where(half, dqs[0], dqs[1]) * 0.125).astype(BF)
    dk[rows, lanes] = (jnp.where(half, dks[0], dks[1]) * 0.125).astype(BF)
    dv[rows, lanes] = jnp.where(half, dvs[0], dvs[1]).astype(BF)


def unit_rows(z):
    mean = jnp.mean(z, axis=-1, keepdims=True)
    c = z - mean
    inv = lax.rsqrt(jnp.mean(c * c, axis=-1, keepdims=True) + 1e-12)
    return c * inv, inv


def norm_back(up, unit, inv, gain):
    e = up * gain
    spread = jnp.mean(e, axis=-1, keepdims=True)
    along = jnp.mean(e * unit, axis=-1, keepdims=True)
    return inv * (e - spread - unit * along)


def ffn_body(z, cot, wi, wo, vecs, out, dsum, db, dwi, dwo, small, fl, act, gp, acc, do):
    rows, d = z.shape
    ff = wi.shape[1]
    rt, et = 512, 128
    k0, k1 = math.sqrt(2.0 / math.pi), 0.044715
    row = lambda i: vecs[i:i + 1, :]
    small[...] = jnp.zeros(small.shape, F32)

    def prep(i, _):
        r = pl.ds(pl.multiple_of(i * et, et), et)
        unit, _inv = unit_rows(z[r, :])
        first = unit * row(AG) + row(ASH)
        fl[r, :] = first.astype(BF)
        acc[r, :] = first + row(BO)
        return 0

    lax.fori_loop(0, rows // et, prep, 0)

    def up(i, _):
        j = i // (rows // rt)
        r = pl.ds(pl.multiple_of((i % (rows // rt)) * rt, rt), rt)
        c = pl.ds(pl.multiple_of(j * d, d), d)
        u = dot(fl[r, :], wi[:, c]) + vecs[pl.ds(BI + j, 1), :]
        u2 = u * u
        t = jnp.tanh(u * (k0 + (k0 * k1) * u2))
        h = 0.5 + 0.5 * t
        a = (u * h).astype(BF)
        act[r, c] = a
        gp[r, c] = (h + (0.5 * u) * (1.0 - t * t) * (k0 + (3.0 * k0 * k1) * u2)).astype(gp.dtype)
        acc[r, :] += dot(a, wo[c, :])
        return 0

    lax.fori_loop(0, (ff // d) * (rows // rt), up, 0)

    def mid(i, _):
        r = pl.ds(pl.multiple_of(i * et, et), et)
        unit, inv = unit_rows(acc[r, :])
        out[r, :] = (unit * row(FG) + row(FS)).astype(BF)
        upv = cot[r, :].astype(F32)
        small[FG:FG + 1, :] += col_sum(upv * unit)
        small[FS:FS + 1, :] += col_sum(upv)
        ds = norm_back(upv, unit, inv, row(FG))
        dsl = ds.astype(BF)
        do[r, :] = dsl
        acc[r, :] = ds
        small[BO:BO + 1, :] += col_sum(dsl.astype(F32))
        return 0

    lax.fori_loop(0, rows // et, mid, 0)

    def down(j, _):
        c = pl.ds(pl.multiple_of(j * d, d), d)
        dwo[c, :] = dot_tn(act[:, c], do[...]).astype(dwo.dtype)
        sums = None
        for i in range(rows // rt):
            r = slice(i * rt, (i + 1) * rt)
            di = dot_nt(do[r, :], wo[c, :]) * gp[r, c].astype(F32)
            dil = di.astype(BF)
            act[r, c] = dil
            s = col_sum(dil.astype(F32))
            sums = s if sums is None else sums + s
            acc[r, :] += dot_nt(dil, wi[:, c])
        small[pl.ds(BI + j, 1), :] = sums
        dwi[:, c] = dot_tn(fl[...], act[:, c]).astype(dwi.dtype)
        return 0

    lax.fori_loop(0, ff // d, down, 0)

    def tail(i, _):
        r = pl.ds(pl.multiple_of(i * et, et), et)
        unit, inv = unit_rows(z[r, :])
        df = acc[r, :]
        small[AG:AG + 1, :] += col_sum(df * unit)
        small[ASH:ASH + 1, :] += col_sum(df)
        ds = norm_back(df, unit, inv, row(AG))
        dsum[r, :] = ds
        dsl = ds.astype(BF)
        db[r, :] = dsl
        small[OB:OB + 1, :] += col_sum(dsl.astype(F32))
        return 0

    lax.fori_loop(0, rows // et, tail, 0)


def ffn(z, cot, wi, wo, vecs, gdt):
    rows, d = z.shape
    ff = wi.shape[1]
    sd = jax.ShapeDtypeStruct
    vm = pl.BlockSpec(memory_space=pltpu.VMEM)
    return pl.pallas_call(
        ffn_body,
        in_specs=[vm] * 5,
        out_specs=[vm] * 6,
        out_shape=[sd((rows, d), BF), sd((rows, d), F32), sd((rows, d), BF), sd((d, ff), gdt), sd((ff, d), gdt),
                   sd((16, d), F32)],
        scratch_shapes=[pltpu.VMEM((rows, d), BF), pltpu.VMEM((rows, ff), BF), pltpu.VMEM((rows, ff), BF),
                        pltpu.VMEM((rows, d), F32), pltpu.VMEM((rows, d), BF)],
        compiler_params=pltpu.CompilerParams(vmem_limit_bytes=VMEM_MAX),
        name="ffn",
    )(z, cot, wi, wo, vecs)


def place():
    me = lax.axis_index("dp")
    c, x, y, z = me % 2, (me // 2) % 2, (me // 4) % 2, me // 8
    fc, fx, fy = 1 - 2 * c, 2 * (1 - 2 * x), 4 * (1 - 2 * y)
    d1 = fx * (1 - c) + fy * c
    d2 = fy * (1 - c) + fx * c
    zs = (0, 8 * (1 - 2 * (z % 2)), 16 * (1 - 2 * (z // 2)), 8 * (3 - 2 * z))
    return me, fc, d1, d2, zs


def greet(me, fc, d1, d2, zs):
    for off in (fc, d1, d2) + zs[1:]:
        pl.semaphore_signal(pltpu.get_barrier_semaphore(), inc=1, device_id=(me + off,), device_id_type=MESH_ID)


def meet():
    pl.semaphore_wait(pltpu.get_barrier_semaphore(), 6)


def unit_of(ref, unit):
    return ref.at[:, unit] if len(ref.shape) == 4 else ref.at[unit]


class Gather:
    ORDER = (1, 4, 2, 5, 8, 3, 6, 9, 7, 12, 10, 13, 11, 14, 15)

    def __init__(self, where, own, out, send, recv):
        self.where, self.own, self.out, self.send, self.recv = where, own, out, send, recv

    def copy(self, slot, unit, dest, own=False):
        return pltpu.make_async_remote_copy(
            src_ref=self.own if own else unit_of(self.out, unit), dst_ref=unit_of(self.out, unit),
            send_sem=self.send.at[slot], recv_sem=self.recv.at[slot], device_id=(dest,), device_id_type=MESH_ID)

    def begin_z(self):
        me, fc, d1, d2, zs = self.where
        for k in (1, 2, 3):
            self.copy(k, me, me + zs[k], True).start()

    def begin_xy(self):
        me, fc, d1, d2, zs = self.where
        self.copy(4, me, me + d1, True).start()
        self.copy(8, me, me + d2, True).start()
        self.copy(16, me, me + fc, True).start()

    def landed(self, slot):
        me, fc, d1, d2, zs = self.where
        unit = me + zs[slot % 4] + (0, d1, d2, d1 + d2, fc, fc + d2, fc + d1, fc + d1 + d2)[slot // 4]
        self.copy(slot, unit, me).wait_recv()
        return unit

    def step(self, slot):
        me, fc, d1, d2, zs = self.where
        k, group = slot % 4, slot // 4
        unit = self.landed(slot)
        if group == 0:
            self.copy(4 + k, unit, me + d1).start()
            self.copy(8 + k, unit, me + d2).start()
        if group == 1:
            self.copy(12 + k, unit, me + d2).start()
        self.copy(16 + slot, unit, me + fc).start()

    def finish(self):
        for slot in range(16, 32):
            self.landed(slot)

    def drain(self):
        me = self.where[0]
        for slot in range(1, 32):
            self.copy(slot, me, me, slot in (1, 2, 3, 4, 8, 16)).wait_send()


LATE = ((1, 0), (4, 1), (2, 2), (5, 3), (8, 4), (3, 5), (6, 6), (9, 7), (7, 8), (12, 9), (10, 10), (13, 11))


def front_body(rb, x, seg, wq, wk, wv, wo, vpart, wis, wus,
               wall_o, wi_o, wu_o, vec_o, q_o, k_o, v_o, p_o, c_o, z_o, hm_o,
               wall, vg, bias, s_s, q_s, k_s, v_s, p_s, c_s, send, recv, local, outs):
    where = place()
    me = where[0]
    rows, d = x.shape
    groups = d // GW
    steps = (rows // SEQ) * (GW // 128)
    owns, targets = (wall.at[:, me], vpart, wis, wus), (wall, vg, wi_o, wu_o)
    mine = [pltpu.make_async_copy(o, unit_of(t, me), local.at[i]) for i, (o, t) in enumerate(zip(owns[1:], targets[1:]))]
    four = [pltpu.make_async_copy(w, wall.at[i, me], local.at[3 + i]) for i, w in enumerate((wq, wk, wv, wo))]
    for m in four + mine:
        m.start()
    greet(*where)
    for m in four:
        m.wait()
    meet()
    flows = [Gather(where, o, t, send.at[i], recv.at[i]) for i, (o, t) in enumerate(zip(owns, targets))]
    early, late = flows[:2], flows[2:]
    for f in early:
        f.begin_z()
    for f in early:
        f.begin_xy()
    same_document_flat(seg, bias)
    for slot in Gather.ORDER:
        for f in early:
            f.step(slot)
        if slot == 3:
            for f in late:
                f.begin_z()
    for f in late:
        f.begin_xy()
    for f in early:
        f.finish()
    mine[0].wait()
    keep = pltpu.make_async_copy(wall, wall_o, outs.at[5])
    keep.start()
    whole_vectors(vg, vec_o, wus.shape[0])
    hm_o[...] = jnp.full(hm_o.shape, LOW, F32)
    z_o[...] = x[...].astype(F32) + vec_o[OB:OB + 1, :]

    def put(g, i):
        src = (q_s, k_s, v_s, c_s)[i].at[g] if i < 4 else p_s.at[g]
        return pltpu.make_async_copy(src, (q_o, k_o, v_o, c_o, p_o)[i].at[g], outs.at[i])

    def group(g, _):
        cols = pl.ds(pl.multiple_of(g * GW, GW), GW)
        weight = lambda i: wall[i, :, :, cols].reshape(d, GW)
        xv = x[...]
        q_s[g] = (dot(xv, weight(0)) + vec_o[QB:QB + 1, cols]).astype(BF)
        k_s[g] = dot(xv, weight(1)).astype(BF)
        v_s[g] = (dot(xv, weight(2)) + vec_o[VB:VB + 1, cols]).astype(BF)

        def one_pair(it, _):
            pair_forward(g, it, lambda h, i: jnp.sum(rb[h].astype(F32)[i:i + 1, :], axis=1, keepdims=True).astype(jnp.int32),
                         q_s.at[g], k_s.at[g], v_s.at[g], p_s.at[g], c_s.at[g], hm_o, bias, s_s)
            for slot, when in LATE:
                @pl.when(g * steps + it == when)
                def _():
                    for f in late:
                        f.step(slot)
            return 0

        lax.fori_loop(0, steps, one_pair, 0)
        for i in range(5):
            put(g, i).start()
        return 0

    lax.fori_loop(0, groups, group, 0)
    wo = wall[3].reshape(d, d)
    for g in range(groups):
        z_o[...] += dot(c_s[g], wo[g * GW:(g + 1) * GW, :])
    done = [slot for slot, _ in LATE]
    for slot in Gather.ORDER:
        if slot not in done:
            for f in late:
                f.step(slot)
    for f in late:
        f.finish()
    mine[1].wait()
    mine[2].wait()
    for f in flows:
        f.drain()
    keep.wait()
    for g in range(groups):
        for i in range(5):
            put(g, i).wait()


def front(rb, x, seg, wq, wk, wv, wo, vpart, wis, wus, n):
    rows, d = x.shape
    groups = d // GW
    maps = (groups, rows, GW // HD * SEQ)
    sd = jax.ShapeDtypeStruct
    vm, hbm = pl.BlockSpec(memory_space=pltpu.VMEM), pl.BlockSpec(memory_space=pl.ANY)
    whole = lambda a: (n,) + a.shape
    four = (4, n) + wq.shape
    act = (groups, rows, GW)
    return pl.pallas_call(
        front_body,
        in_specs=[vm] * 3 + [hbm] * 4 + [vm] * 3,
        out_specs=[hbm] * 3 + [vm] + [hbm] * 5 + [vm] * 2,
        out_shape=[sd(four, BF), sd(whole(wis), BF), sd(whole(wus), BF), sd((16, d), F32),
                   sd(act, BF), sd(act, BF), sd(act, BF), sd(maps, BF), sd(act, BF),
                   sd((rows, d), F32), sd((16, 128), F32)],
        scratch_shapes=[pltpu.VMEM(four, BF), pltpu.VMEM(whole(vpart), F32),
                        pltpu.VMEM((rows // SEQ, SEQ, SEQ), F32), pltpu.VMEM((2, SEQ, SEQ), F32),
                        pltpu.VMEM(act, BF), pltpu.VMEM(act, BF), pltpu.VMEM(act, BF),
                        pltpu.VMEM(maps, BF), pltpu.VMEM(act, BF),
                        pltpu.SemaphoreType.DMA((4, 32)), pltpu.SemaphoreType.DMA((4, 32)),
                        pltpu.SemaphoreType.DMA((7,)), pltpu.SemaphoreType.DMA((6,))],
        compiler_params=pltpu.CompilerParams(collective_id=0, has_side_effects=True, vmem_limit_bytes=VMEM_MAX),
        name="front",
    )(rb, x, seg, wq, wk, wv, wo, vpart, wis, wus)


class Scatter:
    def __init__(self, where, grad, rp, r1, r2, rz, sems):
        self.where, self.grad, self.rp, self.r1, self.r2, self.rz, self.sems = where, grad, rp, r1, r2, rz, sems

    def remote(self, src, dst, slot, off):
        return pltpu.make_async_remote_copy(
            src_ref=src, dst_ref=dst, send_sem=self.sems.at[0, slot], recv_sem=self.sems.at[1, slot],
            device_id=(self.where[0] + off,), device_id_type=MESH_ID)

    def begin(self):
        me, fc, d1, d2, zs = self.where
        for a in (1, 0):
            for b in (1, 0):
                for k in range(4):
                    self.remote(unit_of(self.grad, me + fc + a * d2 + b * d1 + zs[k]), self.rp.at[a, b, k], a, fc).start()

    def pair(self, a):
        me, fc, d1, d2, zs = self.where
        self.remote(self.rp.at[a], self.rp.at[a], a, fc).wait_recv()
        for b in (1, 0):
            for k in range(4):
                held = unit_of(self.grad, me + a * d1 + b * d2 + zs[k])[...]
                self.rp[a, b, k] = (held.astype(F32) + self.rp[a, b, k].astype(F32)).astype(BF)
            if a == 1:
                self.remote(self.rp.at[1, b], self.r1.at[b], 2 + b, d1).start()

    def first(self, b):
        me, fc, d1, d2, zs = self.where
        self.remote(self.rp.at[1, b], self.r1.at[b], 2 + b, d1).wait_recv()
        self.rp[0, b] = (self.rp[0, b].astype(F32) + self.r1[b].astype(F32)).astype(BF)
        if b == 1:
            self.remote(self.rp.at[0, 1], self.r2, 4, d2).start()

    def second(self):
        me, fc, d1, d2, zs = self.where
        self.remote(self.rp.at[0, 1], self.r2, 4, d2).wait_recv()
        for k in (1, 2, 3):
            self.rp[0, 0, k] = (self.rp[0, 0, k].astype(F32) + self.r2[k].astype(F32)).astype(BF)
            self.remote(self.rp.at[0, 0, k], self.rz.at[k - 1], 4 + k, zs[k]).start()

    def near(self):
        return self.rp[0, 0, 0].astype(F32) + self.r2[0].astype(F32)

    def far(self, k):
        self.remote(self.rp.at[0, 0, k], self.rz.at[k - 1], 4 + k, self.where[4][k]).wait_recv()
        return self.rz[k - 1].astype(F32)

    def last(self):
        return self.near() + self.far(1) + self.far(2) + self.far(3)

    def core_sent(self):
        for a in (1, 0):
            self.remote(self.rp.at[a], self.rp.at[a], a, self.where[1]).wait_send()

    def drain(self):
        me, fc, d1, d2, zs = self.where
        for b in (1, 0):
            self.remote(self.rp.at[1, b], self.r1.at[b], 2 + b, d1).wait_send()
        self.remote(self.rp.at[0, 1], self.r2, 4, d2).wait_send()
        for k in (1, 2, 3):
            self.remote(self.rp.at[0, 0, k], self.rz.at[k - 1], 4 + k, zs[k]).wait_send()


class Plane(Scatter):
    def __init__(self, k, *rest):
        Scatter.__init__(self, *rest)
        self.k = k

    def begin(self):
        me, fc, d1, d2, zs = self.where
        for a in (1, 0):
            for b in (1, 0):
                self.remote(self.grad.at[lax.rem(me, 8) + fc + a * d2 + b * d1], self.rp.at[a, b], a, fc).start()

    def pair(self, a):
        me, fc, d1, d2, zs = self.where
        self.remote(self.rp.at[a], self.rp.at[a], a, fc).wait_recv()
        for b in (1, 0):
            held = self.grad[lax.rem(me, 8) + a * d1 + b * d2]
            self.rp[a, b] = (held.astype(F32) + self.rp[a, b].astype(F32)).astype(BF)
            if a == 1:
                self.remote(self.rp.at[1, b], self.r1.at[b], 2 + b, d1).start()

    def along(self):
        return self.remote(self.rp.at[0, 0], self.rz.at[self.k - 1], 4 + self.k, self.where[4][self.k])

    def second(self):
        self.remote(self.rp.at[0, 1], self.r2, 4, self.where[3]).wait_recv()
        if self.k:
            self.rp[0, 0] = (self.rp[0, 0].astype(F32) + self.r2[...].astype(F32)).astype(BF)
            self.along().start()

    def near(self):
        return self.rp[0, 0].astype(F32) + self.r2[...].astype(F32)

    def far(self):
        self.along().wait_recv()
        return self.rz[self.k - 1].astype(F32)

    def drain(self):
        me, fc, d1, d2, zs = self.where
        for b in (1, 0):
            self.remote(self.rp.at[1, b], self.r1.at[b], 2 + b, d1).wait_send()
        self.remote(self.rp.at[0, 1], self.r2, 4, d2).wait_send()
        if self.k:
            self.along().wait_send()


def scatter_buffers(lead, shape):
    return [pltpu.VMEM(lead + (2, 2, 4) + shape, BF), pltpu.VMEM(lead + (2, 4) + shape, BF),
            pltpu.VMEM(lead + (4,) + shape, BF), pltpu.VMEM(lead + (3,) + shape, BF)]


class Vectors:
    def __init__(self, where, held, got, sems):
        self.where, self.held, self.got, self.sems = where, held, got, sems

    def remote(self, src, slot, off):
        return pltpu.make_async_remote_copy(
            src_ref=self.held.at[src], dst_ref=self.got.at[slot], send_sem=self.sems.at[0, slot],
            recv_sem=self.sems.at[1, slot], device_id=(self.where[0] + off,), device_id_type=MESH_ID)

    def merge(self, a, b):
        row = lax.broadcasted_iota(jnp.int32, a.shape, 0)
        return jnp.where(row == TOP, jnp.maximum(a, b), a + b)

    def step(self, i):
        me, fc, d1, d2, zs = self.where
        offs = (fc, d1, d2)
        if i > 0:
            self.remote(i - 1, i - 1, offs[i - 1]).wait_recv()
            self.held[i] = self.merge(self.held[i - 1], self.got[i - 1])
        if i < 3:
            self.remote(i, i, offs[i]).start()
        else:
            for k in (1, 2, 3):
                self.remote(3, 2 + k, zs[k]).start()

    def last(self):
        me, fc, d1, d2, zs = self.where
        total = self.held[3]
        for k in (1, 2, 3):
            self.remote(3, 2 + k, zs[k]).wait_recv()
            total = self.merge(total, self.got[2 + k])
        for i, off in enumerate((fc, d1, d2)):
            self.remote(i, i, off).wait_send()
        for k in (1, 2, 3):
            self.remote(3, 2 + k, zs[k]).wait_send()
        return total


def rear_body(z_h, cot_h, wi_h, wu_h, x_h, wall_h, q_h, k_h, v_h, c_h, p_h, vecs, hm,
              out_h, dx, o_q, o_k, o_v, o_o, o_i, o_u, vout,
              wi, wu, ag, z, fl, do, db, gu, gi, gg, held, got, usems, nsems, sems, vsems, isem, osem, *bufs):
    where = place()
    zi = where[0] // 8
    rows, d = z.shape
    ff = wi.shape[1]
    groups, n = gg.shape[0], gi.shape[1]
    rt, et = 512, 128
    k0, k1 = math.sqrt(2.0 / math.pi), 0.044715
    act, gp, small = ag.at[0], ag.at[1], held.at[0]
    row = lambda i: vecs[i:i + 1, :]
    part = lambda j: pl.ds(pl.multiple_of(j * d, d), d)
    beside = lambda k: (zi % 2 + k % 2 - 2 * (zi % 2) * (k % 2)) + 2 * (zi // 2 + k // 2 - 2 * (zi // 2) * (k // 2))

    def up_flow(it):
        k = (it + 1) % 4 if isinstance(it, int) else None
        return Plane(k, where, gu.at[lax.rem(it, 2)], bufs[0].at[it], bufs[1].at[it], bufs[2].at[it], bufs[3], usems.at[it])

    def in_flow(it):
        return Scatter(where, gi.at[lax.rem(it, 2)], *(b.at[it] for b in bufs[4:8]), nsems.at[it])

    small_flow = Vectors(where, held, got, vsems)
    out_flow = Scatter(where, gi.at[0], *bufs[8:12], sems.at[0])
    group_flow = [Scatter(where, gg.at[g], *bufs[12 + 4 * g:16 + 4 * g], sems.at[1 + g]) for g in range(groups)]

    def get_up(j):
        return pltpu.make_async_copy(wi_h.at[:, part(j)], wi.at[:, part(j)], isem.at[j])

    def get_down(j):
        return pltpu.make_async_copy(wu_h.at[part(j)], wu.at[part(j)], isem.at[4 + j])

    def get_wall(i):
        return pltpu.make_async_copy(wall_h.at[i], wi.at[:, pl.ds(i * d, d)], isem.at[i])

    def get_ctx(g):
        return pltpu.make_async_copy(c_h.at[g], fl.at[:, pl.ds(g * GW, GW)], isem.at[4 + g])

    get_z = pltpu.make_async_copy(z_h, z, isem.at[8])
    get_cot = pltpu.make_async_copy(cot_h, do, isem.at[9])
    get_x = pltpu.make_async_copy(x_h, do, isem.at[9])
    put_out = pltpu.make_async_copy(db, out_h, osem)
    mid_cols = pl.ds(0, GW // HD * SEQ)

    def get_group(g, i):
        cols = pl.ds(pl.multiple_of(g * GW, GW), GW)
        src = (v_h, q_h, k_h, p_h)[i].at[g]
        dst = wu.at[pl.ds((2, 0, 1)[i] * rows, rows), cols] if i < 3 else ag.at[lax.rem(g, 2), :, mid_cols]
        return pltpu.make_async_copy(src, dst, isem.at[10 + 4 * lax.rem(g, 2) + i])

    get_z.start()
    for j in range(ff // d):
        get_up(j).start()
        get_down(j).start()
    get_cot.start()
    greet(*where)
    small[...] = jnp.zeros(small.shape, F32)
    get_z.wait()

    def prep(i, _):
        r = pl.ds(pl.multiple_of(i * et, et), et)
        unit, _inv = unit_rows(z[r, :])
        first = unit * row(AG) + row(ASH)
        fl[r, :] = first.astype(BF)
        dx[r, :] = first + row(BO)
        return 0

    lax.fori_loop(0, rows // et, prep, 0)

    def up(i, _):
        j = i // (rows // rt)
        r = pl.ds(pl.multiple_of((i % (rows // rt)) * rt, rt), rt)
        c = part(j)

        @pl.when(i % (rows // rt) == 0)
        def _():
            get_up(j).wait()
            get_down(j).wait()

        u = dot(fl[r, :], wi[:, c]) + vecs[pl.ds(BI + j, 1), :]
        u2 = u * u
        t = jnp.tanh(u * (k0 + (k0 * k1) * u2))
        h = 0.5 + 0.5 * t
        a = (u * h).astype(BF)
        act[r, c] = a
        gp[r, c] = (h + (0.5 * u) * (1.0 - t * t) * (k0 + (3.0 * k0 * k1) * u2)).astype(BF)
        dx[r, :] += dot(a, wu[c, :])
        return 0

    lax.fori_loop(0, (ff // d) * (rows // rt), up, 0)
    get_cot.wait()

    def mid(i, _):
        r = pl.ds(pl.multiple_of(i * et, et), et)
        unit, inv = unit_rows(dx[r, :])
        db[r, :] = (unit * row(FG) + row(FS)).astype(BF)
        upv = do[r, :].astype(F32)
        small[FG:FG + 1, :] += col_sum(upv * unit)
        small[FS:FS + 1, :] += col_sum(upv)
        ds = norm_back(upv, unit, inv, row(FG))
        dsl = ds.astype(BF)
        do[r, :] = dsl
        dx[r, :] = ds
        small[BO:BO + 1, :] += col_sum(dsl.astype(F32))
        return 0

    lax.fori_loop(0, rows // et, mid, 0)
    put_out.start()
    meet()

    def down(it, _):
        j = beside((it + 1) % 4)
        c = part(j)
        slot = lax.rem(it, 2)

        @pl.when(it >= 2)
        def _():
            up_flow(it - 2).core_sent()

        gu[slot] = dot_tn(act[:, c], do[...]).astype(BF).reshape(gu.shape[1:])
        up_flow(it).begin()
        sums = None
        for i in range(rows // rt):
            r = slice(i * rt, (i + 1) * rt)
            di = dot_nt(do[r, :], wu[c, :]) * gp[r, c].astype(F32)
            dil = di.astype(BF)
            act[r, c] = dil
            s = col_sum(dil.astype(F32))
            sums = s if sums is None else sums + s
            dx[r, :] += dot_nt(dil, wi[:, c])
            if i == 0:
                @pl.when(it >= 1)
                def _():
                    in_flow(it - 1).pair(1)
                    in_flow(it - 1).pair(0)
        small[pl.ds(BI + j, 1), :] = sums
        up_flow(it).pair(1)
        up_flow(it).pair(0)

        @pl.when(it >= 2)
        def _():
            in_flow(it - 2).core_sent()

        gi[slot] = dot_tn(fl[...], act[:, c]).reshape(gi.shape[1:]).astype(BF)
        in_flow(it).begin()

        @pl.when(it >= 2)
        def _():
            for f in (up_flow(it - 2), in_flow(it - 2)):
                f.first(1)
                f.first(0)

        return 0

    lax.fori_loop(0, ff // d, down, 0)
    get_wall(3).start()
    for i in range(4):
        get_group(0, i).start()
    for g in range(groups):
        get_ctx(g).start()
    get_x.start()
    for i in range(3):
        get_wall(i).start()
    put_out.wait()

    def tail(i, _):
        r = pl.ds(pl.multiple_of(i * et, et), et)
        unit, inv = unit_rows(z[r, :])
        df = dx[r, :]
        small[AG:AG + 1, :] += col_sum(df * unit)
        small[ASH:ASH + 1, :] += col_sum(df)
        ds = norm_back(df, unit, inv, row(AG))
        dx[r, :] = ds
        dsl = ds.astype(BF)
        db[r, :] = dsl
        small[OB:OB + 1, :] += col_sum(dsl.astype(F32))
        return 0

    lax.fori_loop(0, rows // et, tail, 0)
    in_flow(3).pair(1)
    in_flow(3).pair(0)
    for g in range(groups):
        get_ctx(g).wait()
    in_flow(2).core_sent()
    gi[0] = dot_tn(fl[...], db[...]).reshape(gi.shape[1:]).astype(BF)
    out_flow.begin()
    get_wall(3).wait()

    steps = (rows // SEQ) * (GW // 128)
    edge = GW // HD * SEQ
    dc, dq, dk, dv = (act.at[:, pl.ds(edge + i * GW, GW)] for i in range(4))
    dp_s = [z.at[pl.ds(j * SEQ, SEQ), pl.ds(0, SEQ)] for j in range(2)]
    ds_s = [gp.at[pl.ds(j * SEQ, SEQ), pl.ds(edge, SEQ)] for j in range(2)]
    both = lambda f: [(f.first, 1), (f.first, 0)]
    g0, g1, g2 = group_flow
    events = {
        0: [(up_flow(0).second,), (in_flow(0).second,), (out_flow.pair, 1)],
        1: [(out_flow.pair, 0)] + both(up_flow(2)),
        2: both(in_flow(2)) + [(up_flow(1).second,)],
        3: [(in_flow(1).second,)],
        4: both(up_flow(3)),
        5: both(in_flow(3)) + [(g0.pair, 1)],
        6: [(g0.pair, 0), (up_flow(2).second,), (out_flow.first, 1)],
        7: [(out_flow.first, 0), (in_flow(2).second,)],
        8: [(up_flow(3).second,), (in_flow(3).second,), (g0.first, 1)],
        9: [(g0.first, 0), (g1.pair, 1)],
        10: [(g1.pair, 0), (out_flow.second,)],
        11: [(g0.second,), (g1.first, 1)],
    }

    def group(g, _):
        cols = pl.ds(pl.multiple_of(g * GW, GW), GW)
        for i in range(4):
            get_group(g, i).wait()

        @pl.when(g + 1 < groups)
        def _():
            for i in range(4):
                get_group(g + 1, i).start()

        dc[...] = dot_nt(db[...], wi[cols, 3 * d:4 * d]).astype(BF)
        heads = [wu.at[pl.ds(i * rows, rows), cols] for i in range(3)]

        def one_pair(it, _):
            pair_backward(it, *heads, ag.at[lax.rem(g, 2)], dc, dq, dk, dv, dp_s, ds_s)
            for when, todo in events.items():
                @pl.when(g * steps + it == when)
                def _():
                    for fn, *a in todo:
                        fn(*a)
            return 0

        lax.fori_loop(0, steps, one_pair, 0)
        small[QB:QB + 1, cols] = col_sum(dq[...].astype(F32))
        small[VB:VB + 1, cols] = col_sum(dv[...].astype(F32))

        @pl.when(g == 0)
        def _():
            get_x.wait()
            for i in range(3):
                get_wall(i).wait()

        xv = do[...]
        for i, grad in enumerate((dq, dk, dv)):
            gg[g, i] = dot_tn(xv, grad[...]).reshape(n, d // n, GW).astype(BF)
        for i in range(groups):
            @pl.when(g == i)
            def _():
                group_flow[i].begin()
        weight = lambda i: wi[:, pl.ds(pl.multiple_of(i * d + g * GW, GW), GW)]
        dx[...] += dot_nt(dq[...], weight(0)) + dot_nt(dk[...], weight(1)) + dot_nt(dv[...], weight(2))
        return 0

    lax.fori_loop(0, groups, group, 0)
    diag = lax.broadcasted_iota(jnp.int32, hm.shape, 0) == lax.broadcasted_iota(jnp.int32, hm.shape, 1)
    small[TOP:TOP + 1, 0:128] = jnp.sum(jnp.where(diag, hm[...], 0.0), axis=0, keepdims=True)
    small_flow.step(0)
    g2.pair(1)
    g2.pair(0)
    small_flow.step(1)
    g1.first(0)
    g2.first(1)
    small_flow.step(2)
    g1.second()
    g2.first(0)
    small_flow.step(3)
    o_u[...] = up_flow(3).near() + up_flow(0).far() + up_flow(1).far() + up_flow(2).far()
    for it in range(4):
        k = (it + 1) % 4
        total = in_flow(it).near()
        for m in (1, 2, 3):
            total = total + in_flow(((k ^ m) - 1) % 4).far(m)
        o_i[:, part(beside(k))] = total
    o_o[...] = out_flow.last()
    g2.second()
    for g, f in enumerate(group_flow):
        t = f.last()
        for i, o in enumerate((o_q, o_k, o_v)):
            o[:, g * GW:(g + 1) * GW] = t[i]
    vout[...] = small_flow.last()
    up_flow(2).core_sent()
    up_flow(3).core_sent()
    in_flow(3).core_sent()
    for f in [out_flow] + group_flow:
        f.core_sent()
    for f in [up_flow(i) for i in range(4)] + [in_flow(i) for i in range(4)] + [out_flow] + group_flow:
        f.drain()


def rear(n, z, cot, wi, wu, x, wall, q, k, v, c, p, vecs, hm):
    rows, d = x.shape
    ff = wi.shape[1]
    groups = d // GW
    r, ru = d // n, ff // n
    sd = jax.ShapeDtypeStruct
    vm, hbm = pl.BlockSpec(memory_space=pltpu.VMEM), pl.BlockSpec(memory_space=pl.ANY)
    flat = pltpu.VMEM((rows, d), BF)
    bufs = [pltpu.VMEM((4, 2, 2, ru, d), BF), pltpu.VMEM((4, 2, ru, d), BF), pltpu.VMEM((4, ru, d), BF),
            pltpu.VMEM((3, ru, d), BF)]
    bufs += scatter_buffers((4,), (r, d)) + scatter_buffers((), (r, d))
    for _ in range(groups):
        bufs += scatter_buffers((), (3, r, GW))
    return pl.pallas_call(
        rear_body,
        in_specs=[hbm] * 11 + [vm] * 2,
        out_specs=[hbm] + [vm] * 8,
        out_shape=[sd((rows, d), BF), sd((rows, d), F32)] + [sd((r, d), F32)] * 4
        + [sd((r, ff), F32), sd((ru, d), F32), sd((16, d), F32)],
        scratch_shapes=[pltpu.VMEM((d, ff), BF), pltpu.VMEM((ff, d), BF), pltpu.VMEM((2, rows, ff), BF),
                        pltpu.VMEM((rows, d), F32), flat, flat, flat, pltpu.VMEM((2, 8, ru, d), BF),
                        pltpu.VMEM((2, n, r, d), BF), pltpu.VMEM((groups, 3, n, r, GW), BF),
                        pltpu.VMEM((4, 16, d), F32), pltpu.VMEM((6, 16, d), F32),
                        pltpu.SemaphoreType.DMA((4, 2, 8)), pltpu.SemaphoreType.DMA((4, 2, 8)),
                        pltpu.SemaphoreType.DMA((1 + groups, 2, 8)), pltpu.SemaphoreType.DMA((2, 6)),
                        pltpu.SemaphoreType.DMA((18,)), pltpu.SemaphoreType.DMA] + bufs,
        compiler_params=pltpu.CompilerParams(collective_id=1, has_side_effects=True, vmem_limit_bytes=VMEM_MAX),
        name="rear",
    )(z, cot, wi, wu, x, wall, q, k, v, c, p, vecs, hm)


def attn_fwd_body(rb, x, segr, segc, wq, wk, wv, wo, vecs, q, k, v, p, c, z, hm, bias, s_s):
    g = pl.program_id(0)

    @pl.when(g == 0)
    def _():
        same_document(lambda s: segr[s:s + 1, :], lambda s, c: segc[s * SEQ + c * BLOCK:s * SEQ + (c + 1) * BLOCK, :], bias)
        hm[...] = jnp.full(hm.shape, LOW, F32)
        z[...] = x[...].astype(F32) + vecs[OB:OB + 1, :]

    cols = pl.ds(pl.multiple_of(g * GW, GW), GW)
    xv = x[...]
    q[...] = (dot(xv, wq[...]) + vecs[QB:QB + 1, cols]).astype(BF)
    k[...] = dot(xv, wk[...]).astype(BF)
    v[...] = (dot(xv, wv[...]) + vecs[VB:VB + 1, cols]).astype(BF)

    def one_pair(it, _):
        pair_forward(g, it, lambda h, i: rb[h * 18 + i * 3] + rb[h * 18 + i * 3 + 1] + rb[h * 18 + i * 3 + 2], q, k, v, p, c, hm, bias, s_s)
        return 0

    lax.fori_loop(0, x.shape[0] // SEQ * (GW // 128), one_pair, 0)
    z[...] += dot(c[...], wo[...])


def attn_fwd(rb, x, segr, segc, wall, vecs):
    rows, d = x.shape
    groups, seqs = d // GW, rows // SEQ
    keys = GW // HD * SEQ
    full = lambda shape: pl.BlockSpec(shape, lambda g, *_: (0,) * len(shape))
    col = lambda i: pl.BlockSpec((None, d, GW), lambda g, *_: (i, 0, g))
    act = pl.BlockSpec((None, rows, GW), lambda g, *_: (g, 0, 0))
    sd = jax.ShapeDtypeStruct
    return pl.pallas_call(
        attn_fwd_body,
        grid_spec=pltpu.PrefetchScalarGridSpec(
            num_scalar_prefetch=1, grid=(groups,),
            in_specs=[full((rows, d)), full((seqs, SEQ)), full((rows, 1)), col(0), col(1), col(2),
                      pl.BlockSpec((None, GW, d), lambda g, *_: (3, g, 0)), full((16, d))],
            out_specs=[act, act, act, pl.BlockSpec((None, rows, keys), lambda g, *_: (g, 0, 0)), act,
                       full((rows, d)), full((16, 128))],
            scratch_shapes=[pltpu.VMEM((seqs, SEQ, SEQ), F32), pltpu.VMEM((2, SEQ, SEQ), F32)]),
        out_shape=[sd((groups, rows, GW), BF)] * 3
        + [sd((groups, rows, keys), BF), sd((groups, rows, GW), BF), sd((rows, d), F32), sd((16, 128), F32)],
        compiler_params=pltpu.CompilerParams(vmem_limit_bytes=VMEM_MAX),
        name="attn_fwd",
    )(rb, x, segr, segc, wall, wall, wall, wall, vecs)


def attn_bwd_body(x, db, wq, wk, wv, wo, q, k, v, p, c, dsum, dw, dqb, dvb, dx, dc, dq, dk, dv, dp_s, ds_s):
    g = pl.program_id(0)

    @pl.when(g == 0)
    def _():
        dx[...] = dsum[...]

    dbv = db[...]
    cols = pl.ds(pl.multiple_of(g * GW, GW), GW)
    dc[...] = dot_nt(dbv, wo[...]).astype(BF)
    dw[3, cols, :] = dot_tn(c[...], dbv).astype(dw.dtype)

    def one_pair(it, _):
        pair_backward(it, q, k, v, p, dc, dq, dk, dv, [dp_s.at[0], dp_s.at[1]], [ds_s.at[0], ds_s.at[1]])
        return 0

    lax.fori_loop(0, x.shape[0] // SEQ * (GW // 128), one_pair, 0)
    dqb[...] = col_sum(dq[...].astype(F32))
    dvb[...] = col_sum(dv[...].astype(F32))
    xv = x[...]
    for i, part in enumerate((dq, dk, dv)):
        dw[i, :, cols] = dot_tn(xv, part[...]).astype(dw.dtype)
    dx[...] += dot_nt(dq[...], wq[...]) + dot_nt(dk[...], wk[...]) + dot_nt(dv[...], wv[...])


def attn_bwd(x, db, wall, q, k, v, p, c, dsum, gdt):
    rows, d = x.shape
    groups = d // GW
    keys = GW // HD * SEQ
    full = lambda shape: pl.BlockSpec(shape, lambda g: (0,) * len(shape), pipeline_mode=pl.Buffered(1))
    col = lambda i: pl.BlockSpec((None, d, GW), lambda g: (i, 0, g))
    vec = pl.BlockSpec((1, GW), lambda g: (0, g))
    act = pl.BlockSpec((None, rows, GW), lambda g: (g, 0, 0))
    sd = jax.ShapeDtypeStruct
    return pl.pallas_call(
        attn_bwd_body,
        grid=(groups,),
        in_specs=[full((rows, d)), full((rows, d)), col(0), col(1), col(2),
                  pl.BlockSpec((None, GW, d), lambda g: (3, g, 0)), act, act, act,
                  pl.BlockSpec((None, rows, keys), lambda g: (g, 0, 0)), act, full((rows, d))],
        out_specs=[full((4, d, d)), vec, vec, full((rows, d))],
        out_shape=[sd((4, d, d), gdt)] + [sd((1, d), F32)] * 2 + [sd((rows, d), F32)],
        scratch_shapes=[pltpu.VMEM((rows, GW), BF)] * 4
        + [pltpu.VMEM((2, SEQ, SEQ), F32), pltpu.VMEM((2, SEQ, SEQ), BF)],
        compiler_params=pltpu.CompilerParams(vmem_limit_bytes=VMEM_MAX),
        name="attn_bwd",
    )(x, db, wall, wall, wall, wall, q, k, v, p, c, dsum)


def far_layer(me, n, random_blocks, tokens, segment_ids, cot, weights, vecs, inner_weight, inner_bias, outer_weight, limit):
    d, ff = tokens.shape[1], inner_weight.shape[1]
    heads, part, wide = random_blocks.shape[0], vecs[0].shape[0], inner_bias.shape[0]
    wall = lax.all_gather(jnp.stack(weights), "dp", axis=1, tiled=True)
    wi, wu = (lax.all_gather(a, "dp", axis=0, tiled=True) for a in (inner_weight, outer_weight))
    vecs = lax.psum(vectors_part(me, n, vecs, inner_bias).astype(F32), "dp")
    q, k, v, p, c, z, hm = attn_fwd(random_blocks.reshape(-1), tokens, segment_ids.reshape(-1, SEQ),
                                    segment_ids.reshape(-1, 1), wall, vecs)
    out, dsum, db, dwi, dwu, small = ffn(z, cot, wi, wu, vecs, F32)
    dwall, dqb, dvb, dx = attn_bwd(tokens, db, wall, q, k, v, p, c, dsum, F32)
    mine = small.at[QB:QB + 1].set(dqb).at[VB:VB + 1].set(dvb).at[TOP, :hm.shape[0]].set(hm[:, 0])
    scatter = lambda a, at: lax.psum_scatter(a, "dp", scatter_dimension=at, tiled=True)
    dwu, dwi, dwall = scatter(dwu, 0), scatter(dwi, 0), scatter(dwall, 1)
    row = lax.broadcasted_iota(jnp.int32, mine.shape, 0)
    total = jnp.where(row == TOP, lax.pmax(mine, "dp"), lax.psum(mine, "dp"))
    vec8 = lax.dynamic_slice(total, (0, me * part), (8, part))
    dbi = lax.dynamic_slice(total[BI:BI + ff // d].reshape(-1), (me * wide,), (wide,))
    head_maxima = total[TOP, :heads]
    factor = jnp.sqrt(jnp.minimum(1.0, limit[0].astype(F32) / jnp.maximum(head_maxima, 1.0)))
    columns = jnp.repeat(factor, HD)[None, :]
    cq, ck = ((w.astype(F32) * columns).astype(BF) for w in weights[:2])
    return out, dx, dwall[0], dwall[1], dwall[2], dwall[3], dwi, dwu, [vec8[i] for i in range(8)], dbi, cq, ck, head_maxima


def near_layer(me, n, random_blocks, tokens, segment_ids, cot, weights, vecs, inner_weight, inner_bias, outer_weight, limit):
    d, ff = tokens.shape[1], inner_weight.shape[1]
    heads, part, wide = random_blocks.shape[0], vecs[0].shape[0], inner_bias.shape[0]
    pieces = jnp.concatenate([jnp.pad(jnp.stack(vecs), ((0, 0), (0, 128 - part))),
                              jnp.pad(inner_bias[None, :], ((0, 7), (0, 128 - wide)))]).astype(F32)
    wall, wi, wu, vec, q, k, v, p, c, z, hm = front(random_blocks, tokens, segment_ids.reshape(-1, 128), *weights, pieces,
                                                    inner_weight, outer_weight, n)
    raw = rear(n, z, cot, wi.reshape(d, ff), wu.reshape(ff, d), tokens, wall.reshape(4, d, d), q, k, v, c, p, vec, hm)
    out, dx, dwq, dwk, dwv, dwo, dwi, dwu, cq, ck, *fins = finish(n, heads, limit, weights[0], weights[1], *raw)
    fins = [a.reshape(-1) for a in fins]
    return out, dx, dwq, dwk, dwv, dwo, dwi, dwu, fins[:8], fins[8], cq, ck, fins[9]


def finish_body(n, heads, limit, wq, wk, total, *refs):
    count = 8
    srcs, dsts, refs = refs[:count], refs[count:2 * count], refs[2 * count:]
    (cq, ck), fins, held, sems = refs[:2], refs[2:12], refs[12:-1], refs[-1]
    jobs = []
    for src, dst, tmp in zip(srcs, dsts, held):
        cut = 4 if src.shape[0] >= 512 else 1
        step = src.shape[0] // cut
        for i in range(cut):
            at = pl.ds(i * step, step)
            slot = len(jobs)
            jobs.append((pltpu.make_async_copy(src.at[at], tmp.at[at], sems.at[0, slot]),
                         pltpu.make_async_copy(tmp.at[at], dst.at[at], sems.at[1, slot])))
    for get, _ in jobs:
        get.start()
    me = lax.axis_index("dp")
    d = total.shape[1]
    part, wide = d // n, held[7].shape[0]
    top = total[TOP:TOP + 1, 0:128]
    head = lax.broadcasted_iota(jnp.int32, (1, d), 1) // HD
    columns = jnp.zeros((1, d), F32)
    for h in range(heads):
        columns = jnp.where(head == h, top[:, h:h + 1], columns)
    factor = jnp.sqrt(jnp.minimum(1.0, limit[0].astype(F32) / jnp.maximum(columns, 1.0)))
    cq[...] = (wq[...].astype(F32) * factor).astype(BF)
    ck[...] = (wk[...].astype(F32) * factor).astype(BF)
    mine = pltpu.roll(total[0:8, :], d - me * part, 1)
    for i in range(8):
        fins[i][...] = mine[i:i + 1, 0:part]
    per = d // wide
    inner = jnp.broadcast_to(total[pl.ds(BI + me // per, 1), :], (8, d))
    fins[8][...] = pltpu.roll(inner, d - (me % per) * wide, 1)[0:1, 0:wide]
    fins[9][...] = top[:, 0:heads]
    for get, put in jobs:
        get.wait()
        put.start()
    for _, put in jobs:
        put.wait()


def finish(n, heads, limit, wq, wk, *raw):
    mats, total = raw[:8], raw[8]
    vm, hbm = pl.BlockSpec(memory_space=pltpu.VMEM), pl.BlockSpec(memory_space=pl.ANY)
    sd = jax.ShapeDtypeStruct
    return pl.pallas_call(
        partial(finish_body, n, heads),
        in_specs=[pl.BlockSpec(memory_space=pltpu.SMEM)] + [vm] * 3 + [hbm] * 8,
        out_specs=[hbm] * 8 + [vm] * 12,
        out_shape=[sd(a.shape, a.dtype) for a in mats] + [sd(wq.shape, BF)] * 2 + [sd((1, mats[2].shape[0]), F32)] * 8
        + [sd((1, mats[7].shape[0]), F32), sd((1, heads), F32)],
        scratch_shapes=[pltpu.VMEM(a.shape, a.dtype) for a in mats] + [pltpu.SemaphoreType.DMA((2, 16))],
        compiler_params=pltpu.CompilerParams(vmem_limit_bytes=VMEM_MAX),
        name="finish",
    )(limit, wq, wk, total, *mats)


def vectors_part(me, n, vecs, inner_bias):
    part = vecs[0].shape[0]
    d = part * n
    rows = jnp.tile(jnp.stack(vecs), (1, n))
    rows = jnp.where(lax.broadcasted_iota(jnp.int32, rows.shape, 1) // part == me, rows, 0)
    flat = jnp.tile(inner_bias, n)
    flat = jnp.where(lax.broadcasted_iota(jnp.int32, flat.shape, 0) // inner_bias.shape[0] == me, flat, 0)
    flat = flat.reshape(-1, d)
    rest = jnp.zeros((16 - rows.shape[0] - flat.shape[0], d), BF)
    return jnp.concatenate([rows, flat, rest], axis=0)


def per_device(n, tokens, segment_ids, random_blocks, clip_limit, query_weight, query_bias, key_weight, value_weight,
               value_bias, output_weight, output_bias, attn_gain, attn_shift, inner_weight, inner_bias,
               outer_weight, outer_bias, final_gain, final_shift, out_cotangent):
    rows, d = tokens.shape
    near = n == 32 and (rows, d, inner_weight.shape[1]) == (2 * SEQ, 3 * GW, 6 * SEQ)
    weights = (query_weight, key_weight, value_weight, output_weight)
    vecs = (query_bias, value_bias, output_bias, attn_gain, attn_shift, outer_bias, final_gain, final_shift)
    out, dx, dwq, dwk, dwv, dwo, dwi, dwu, vec8, dbi, cq, ck, head_maxima = (near_layer if near else far_layer)(
        lax.axis_index("dp"), n, random_blocks, tokens, segment_ids, out_cotangent, weights, vecs, inner_weight, inner_bias,
        outer_weight, clip_limit)
    dqb, dvb, dob, dag, dash, dbo, dfg, dfs = vec8
    return (out, dx, dwq, dqb, dwk, dwv, dvb, dwo, dob, dag, dash, dwi, dbi, dwu, dbo, dfg, dfs, cq, ck, head_maxima)


def solution(mesh):
    mat, vec, rep = P("dp", None), P("dp"), P()
    in_specs = (mat, vec, rep, rep, mat, vec, mat, mat, vec, mat, vec, vec, vec, mat, vec, mat, vec, vec, vec, mat)
    out_specs = (mat, mat, mat, vec, mat, mat, vec, mat, vec, vec, vec, mat, vec, mat, vec, vec, vec, mat, mat, rep)
    return jax.shard_map(partial(per_device, mesh.shape["dp"]), mesh=mesh, in_specs=in_specs, out_specs=out_specs,
                         check_vma=False)
```

```python
from functools import partial
import math

import jax
import jax.numpy as jnp
from jax import lax
from jax.experimental import pallas as pl
from jax.experimental.pallas import tpu as pltpu
from jax.sharding import PartitionSpec as P

HD = 64
BLOCK = 64
SEQ = 512
GW = 256
BF = jnp.bfloat16
F32 = jnp.float32
LOW = -1e30
VMEM_MAX = 67043328
MESH_ID = pl.DeviceIdType.MESH
QB, VB, OB, AG, ASH, BO, FG, FS, BI, TOP = 0, 1, 2, 3, 4, 5, 6, 7, 8, 12


def dot(a, b):
    return jnp.dot(a, b, preferred_element_type=F32)


def dot_nt(a, b):
    return lax.dot_general(a, b, (((1,), (1,)), ((), ())), preferred_element_type=F32)


def dot_tn(a, b):
    return lax.dot_general(a, b, (((0,), (0,)), ((), ())), preferred_element_type=F32)


def col_sum(v):
    return jnp.sum(v, axis=0, keepdims=True)


def first_half():
    return lax.broadcasted_iota(jnp.int32, (1, 128), 1) < HD


def same_document(key_ids, query_ids, bias):
    for s in range(bias.shape[0]):
        kseg = key_ids(s)
        for c in range(SEQ // BLOCK):
            bias[s, c * BLOCK:(c + 1) * BLOCK, :] = jnp.where((query_ids(s, c) == kseg) & (kseg != 0), 0.0, LOW)


def same_document_flat(seg, bias):
    ids = seg[...].astype(F32)
    turned = jnp.transpose(ids)
    per = SEQ // 128
    key_ids = lambda s: jnp.concatenate([ids[s * per + i:s * per + i + 1, :] for i in range(per)], axis=1)

    def query_ids(s, c):
        i, r = s * per + c * BLOCK // 128, c * BLOCK % 128
        return turned[r:r + BLOCK, i:i + 1]

    same_document(key_ids, query_ids, bias)


def whole_vectors(pieces, vec, wide):
    n, d = pieces.shape[0], vec.shape[1]
    lane = lax.broadcasted_iota(jnp.int32, (1, 128), 1)

    def spread(values, width):
        tiles = [0.0] * (d // 128)
        for i, value in enumerate(values):
            t, at = i * width // 128, i * width % 128
            moved = pltpu.roll(value, at, 1) if at else value
            tiles[t] = tiles[t] + (jnp.where(lane >= at, moved, 0.0) if at + width > 128 else moved)
            if at + width > 128:
                tiles[t + 1] = tiles[t + 1] + jnp.where(lane < at, moved, 0.0)
        return jnp.concatenate(tiles, axis=1)

    vec[0:8, :] = spread([pieces[u, 0:8, :] for u in range(n)], d // n)
    per = d // wide
    inner = [spread([pieces[j * per + i, 8:16, :] for i in range(per)], wide) for j in range(n // per)]
    for j, v in enumerate(inner):
        vec[8 + j:9 + j, :] = v[0:1, :]
    vec[8 + len(inner):16, :] = jnp.zeros((8 - len(inner), d), F32)


def pair_forward(g, it, rb, q, k, v, p, ctx, hm, bias, s_s):
    pairs = GW // 128
    s, pair = it // pairs, it % pairs
    rows = pl.ds(pl.multiple_of(s * SEQ, SEQ), SEQ)
    lanes = pl.ds(pl.multiple_of(pair * 128, 128), 128)
    lane_block = lax.broadcasted_iota(jnp.int32, (1, SEQ), 1) // BLOCK
    half = first_half()
    last = SEQ // BLOCK - 2
    qp, kp, vp = q[rows, lanes], k[rows, lanes], v[rows, lanes]
    outs = []
    for j in range(2):
        head = g * (2 * pairs) + pair * 2 + j
        keys = pl.ds(pl.multiple_of((pair * 2 + j) * SEQ, SEQ), SEQ)
        mine = half if j == 0 else jnp.logical_not(half)
        s_s[j] = dot_nt(jnp.where(mine, qp * 0.125, 0).astype(BF), kp)
        miss1, miss6 = 18 - rb(head, 0), 10 - rb(head, 5)
        skip1 = jnp.where(lane_block == miss1, LOW, 0.0)
        skip6 = jnp.where(lane_block == miss6, LOW, 0.0)
        tops = None
        for c in range(SEQ // BLOCK):
            cr = slice(c * BLOCK, (c + 1) * BLOCK)
            sv = s_s[j, cr, :] + bias[s, cr, :]
            if c == 1:
                sv = sv + skip1
            if c == last:
                sv = sv + skip6
            top = jnp.max(sv, axis=1, keepdims=True)
            live = top > -1e29
            e = jnp.exp(sv - jnp.where(live, top, 0.0))
            total = jnp.sum(e, axis=1, keepdims=True) + jnp.where(live, 0.0, 1.0)
            p[pl.ds(pl.multiple_of(s * SEQ + c * BLOCK, BLOCK), BLOCK), keys] = (e * (1.0 / total)).astype(BF)
            tops = top if tops is None else jnp.maximum(tops, top)
        top = jnp.max(tops, axis=0, keepdims=True)
        hm[pl.ds(head, 1), :] = jnp.maximum(hm[pl.ds(head, 1), :], top)
        outs.append(dot(p[rows, keys], vp))
    ctx[rows, lanes] = jnp.where(half, outs[0], outs[1]).astype(BF)


def pair_backward(it, q, k, v, p, dc, dq, dk, dv, dp_s, ds_s):
    pairs = GW // 128
    s, pair = it // pairs, it % pairs
    rows = pl.ds(pl.multiple_of(s * SEQ, SEQ), SEQ)
    lanes = pl.ds(pl.multiple_of(pair * 128, 128), 128)
    half = first_half()
    qp, kp, vp, dcp = q[rows, lanes], k[rows, lanes], v[rows, lanes], dc[rows, lanes]
    dqs, dks, dvs = [], [], []
    for j in range(2):
        mine = half if j == 0 else jnp.logical_not(half)
        keys = pl.ds(pl.multiple_of((pair * 2 + j) * SEQ, SEQ), SEQ)
        dp_s[j][...] = dot_nt(jnp.where(mine, dcp, 0).astype(BF), vp)
        for c in range(SEQ // BLOCK):
            cr = slice(c * BLOCK, (c + 1) * BLOCK)
            pv = p[pl.ds(pl.multiple_of(s * SEQ + c * BLOCK, BLOCK), BLOCK), keys].astype(F32)
            sl = dp_s[j][cr, :]
            mean = jnp.sum(pv * sl, axis=1, keepdims=True)
            ds_s[j][cr, :] = (pv * (sl - mean)).astype(BF)
        dqs.append(dot(ds_s[j][...], kp))
        dks.append(dot_tn(ds_s[j][...], qp))
        dvs.append(dot_tn(p[rows, keys], dcp))
    dq[rows, lanes] = (jnp.where(half, dqs[0], dqs[1]) * 0.125).astype(BF)
    dk[rows, lanes] = (jnp.where(half, dks[0], dks[1]) * 0.125).astype(BF)
    dv[rows, lanes] = jnp.where(half, dvs[0], dvs[1]).astype(BF)


def unit_rows(z):
    mean = jnp.mean(z, axis=-1, keepdims=True)
    c = z - mean
    inv = lax.rsqrt(jnp.mean(c * c, axis=-1, keepdims=True) + 1e-12)
    return c * inv, inv


def norm_back(up, unit, inv, gain):
    e = up * gain
    spread = jnp.mean(e, axis=-1, keepdims=True)
    along = jnp.mean(e * unit, axis=-1, keepdims=True)
    return inv * (e - spread - unit * along)


def ffn_body(z, cot, wi, wo, vecs, out, dsum, db, dwi, dwo, small, fl, act, gp, acc, do):
    rows, d = z.shape
    ff = wi.shape[1]
    rt, et = 512, 128
    k0, k1 = math.sqrt(2.0 / math.pi), 0.044715
    row = lambda i: vecs[i:i + 1, :]
    small[...] = jnp.zeros(small.shape, F32)

    def prep(i, _):
        r = pl.ds(pl.multiple_of(i * et, et), et)
        unit, _inv = unit_rows(z[r, :])
        first = unit * row(AG) + row(ASH)
        fl[r, :] = first.astype(BF)
        acc[r, :] = first + row(BO)
        return 0

    lax.fori_loop(0, rows // et, prep, 0)

    def up(i, _):
        j = i // (rows // rt)
        r = pl.ds(pl.multiple_of((i % (rows // rt)) * rt, rt), rt)
        c = pl.ds(pl.multiple_of(j * d, d), d)
        u = dot(fl[r, :], wi[:, c]) + vecs[pl.ds(BI + j, 1), :]
        u2 = u * u
        t = jnp.tanh(u * (k0 + (k0 * k1) * u2))
        h = 0.5 + 0.5 * t
        a = (u * h).astype(BF)
        act[r, c] = a
        gp[r, c] = (h + (0.5 * u) * (1.0 - t * t) * (k0 + (3.0 * k0 * k1) * u2)).astype(gp.dtype)
        acc[r, :] += dot(a, wo[c, :])
        return 0

    lax.fori_loop(0, (ff // d) * (rows // rt), up, 0)

    def mid(i, _):
        r = pl.ds(pl.multiple_of(i * et, et), et)
        unit, inv = unit_rows(acc[r, :])
        out[r, :] = (unit * row(FG) + row(FS)).astype(BF)
        upv = cot[r, :].astype(F32)
        small[FG:FG + 1, :] += col_sum(upv * unit)
        small[FS:FS + 1, :] += col_sum(upv)
        ds = norm_back(upv, unit, inv, row(FG))
        dsl = ds.astype(BF)
        do[r, :] = dsl
        acc[r, :] = ds
        small[BO:BO + 1, :] += col_sum(dsl.astype(F32))
        return 0

    lax.fori_loop(0, rows // et, mid, 0)

    def down(j, _):
        c = pl.ds(pl.multiple_of(j * d, d), d)
        dwo[c, :] = dot_tn(act[:, c], do[...]).astype(dwo.dtype)
        sums = None
        for i in range(rows // rt):
            r = slice(i * rt, (i + 1) * rt)
            di = dot_nt(do[r, :], wo[c, :]) * gp[r, c].astype(F32)
            dil = di.astype(BF)
            act[r, c] = dil
            s = col_sum(dil.astype(F32))
            sums = s if sums is None else sums + s
            acc[r, :] += dot_nt(dil, wi[:, c])
        small[pl.ds(BI + j, 1), :] = sums
        dwi[:, c] = dot_tn(fl[...], act[:, c]).astype(dwi.dtype)
        return 0

    lax.fori_loop(0, ff // d, down, 0)

    def tail(i, _):
        r = pl.ds(pl.multiple_of(i * et, et), et)
        unit, inv = unit_rows(z[r, :])
        df = acc[r, :]
        small[AG:AG + 1, :] += col_sum(df * unit)
        small[ASH:ASH + 1, :] += col_sum(df)
        ds = norm_back(df, unit, inv, row(AG))
        dsum[r, :] = ds
        dsl = ds.astype(BF)
        db[r, :] = dsl
        small[OB:OB + 1, :] += col_sum(dsl.astype(F32))
        return 0

    lax.fori_loop(0, rows // et, tail, 0)


def ffn(z, cot, wi, wo, vecs, gdt):
    rows, d = z.shape
    ff = wi.shape[1]
    sd = jax.ShapeDtypeStruct
    vm = pl.BlockSpec(memory_space=pltpu.VMEM)
    return pl.pallas_call(
        ffn_body,
        in_specs=[vm] * 5,
        out_specs=[vm] * 6,
        out_shape=[sd((rows, d), BF), sd((rows, d), F32), sd((rows, d), BF), sd((d, ff), gdt), sd((ff, d), gdt),
                   sd((16, d), F32)],
        scratch_shapes=[pltpu.VMEM((rows, d), BF), pltpu.VMEM((rows, ff), BF), pltpu.VMEM((rows, ff), BF),
                        pltpu.VMEM((rows, d), F32), pltpu.VMEM((rows, d), BF)],
        compiler_params=pltpu.CompilerParams(vmem_limit_bytes=VMEM_MAX),
        name="ffn",
    )(z, cot, wi, wo, vecs)


def place():
    me = lax.axis_index("dp")
    c, x, y, z = me % 2, (me // 2) % 2, (me // 4) % 2, me // 8
    fc, fx, fy = 1 - 2 * c, 2 * (1 - 2 * x), 4 * (1 - 2 * y)
    d1 = fx * (1 - c) + fy * c
    d2 = fy * (1 - c) + fx * c
    zs = (0, 8 * (1 - 2 * (z % 2)), 16 * (1 - 2 * (z // 2)), 8 * (3 - 2 * z))
    return me, fc, d1, d2, zs


def greet(me, fc, d1, d2, zs):
    for off in (fc, d1, d2) + zs[1:]:
        pl.semaphore_signal(pltpu.get_barrier_semaphore(), inc=1, device_id=(me + off,), device_id_type=MESH_ID)


def meet():
    pl.semaphore_wait(pltpu.get_barrier_semaphore(), 6)


def unit_of(ref, unit):
    return ref.at[:, unit] if len(ref.shape) == 4 else ref.at[unit]


class Gather:
    ORDER = (1, 4, 2, 5, 8, 3, 6, 9, 7, 12, 10, 13, 11, 14, 15)

    def __init__(self, where, own, out, send, recv):
        self.where, self.own, self.out, self.send, self.recv = where, own, out, send, recv

    def copy(self, slot, unit, dest, own=False):
        return pltpu.make_async_remote_copy(
            src_ref=self.own if own else unit_of(self.out, unit), dst_ref=unit_of(self.out, unit),
            send_sem=self.send.at[slot], recv_sem=self.recv.at[slot], device_id=(dest,), device_id_type=MESH_ID)

    def begin_z(self):
        me, fc, d1, d2, zs = self.where
        for k in (1, 2, 3):
            self.copy(k, me, me + zs[k], True).start()

    def begin_xy(self):
        me, fc, d1, d2, zs = self.where
        self.copy(4, me, me + d1, True).start()
        self.copy(8, me, me + d2, True).start()
        self.copy(16, me, me + fc, True).start()

    def landed(self, slot):
        me, fc, d1, d2, zs = self.where
        unit = me + zs[slot % 4] + (0, d1, d2, d1 + d2, fc, fc + d2, fc + d1, fc + d1 + d2)[slot // 4]
        self.copy(slot, unit, me).wait_recv()
        return unit

    def step(self, slot):
        me, fc, d1, d2, zs = self.where
        k, group = slot % 4, slot // 4
        unit = self.landed(slot)
        if group == 0:
            self.copy(4 + k, unit, me + d1).start()
            self.copy(8 + k, unit, me + d2).start()
        if group == 1:
            self.copy(12 + k, unit, me + d2).start()
        self.copy(16 + slot, unit, me + fc).start()

    def finish(self):
        for slot in range(16, 32):
            self.landed(slot)

    def drain(self):
        me = self.where[0]
        for slot in range(1, 32):
            self.copy(slot, me, me, slot in (1, 2, 3, 4, 8, 16)).wait_send()


LATE = ((1, 0), (4, 1), (2, 2), (5, 3), (8, 4), (3, 5), (6, 6), (9, 7), (7, 8), (12, 9), (10, 10), (13, 11))


def front_body(rb, x, seg, wq, wk, wv, wo, vpart, wis, wus,
               wall_o, wi_o, wu_o, vec_o, q_o, k_o, v_o, p_o, c_o, z_o, hm_o,
               wall, vg, bias, s_s, q_s, k_s, v_s, p_s, c_s, send, recv, local, outs):
    where = place()
    me = where[0]
    rows, d = x.shape
    groups = d // GW
    steps = (rows // SEQ) * (GW // 128)
    owns, targets = (wall.at[:, me], vpart, wis, wus), (wall, vg, wi_o, wu_o)
    mine = [pltpu.make_async_copy(o, unit_of(t, me), local.at[i]) for i, (o, t) in enumerate(zip(owns[1:], targets[1:]))]
    four = [pltpu.make_async_copy(w, wall.at[i, me], local.at[3 + i]) for i, w in enumerate((wq, wk, wv, wo))]
    for m in four + mine:
        m.start()
    greet(*where)
    for m in four:
        m.wait()
    meet()
    flows = [Gather(where, o, t, send.at[i], recv.at[i]) for i, (o, t) in enumerate(zip(owns, targets))]
    early, late = flows[:2], flows[2:]
    for f in early:
        f.begin_z()
    for f in early:
        f.begin_xy()
    same_document_flat(seg, bias)
    for slot in Gather.ORDER:
        for f in early:
            f.step(slot)
        if slot == 3:
            for f in late:
                f.begin_z()
    for f in late:
        f.begin_xy()
    for f in early:
        f.finish()
    mine[0].wait()
    keep = pltpu.make_async_copy(wall, wall_o, outs.at[5])
    keep.start()
    whole_vectors(vg, vec_o, wus.shape[0])
    hm_o[...] = jnp.full(hm_o.shape, LOW, F32)
    z_o[...] = x[...].astype(F32) + vec_o[OB:OB + 1, :]

    def put(g, i):
        src = (q_s, k_s, v_s, c_s)[i].at[g] if i < 4 else p_s.at[g]
        return pltpu.make_async_copy(src, (q_o, k_o, v_o, c_o, p_o)[i].at[g], outs.at[i])

    def group(g, _):
        cols = pl.ds(pl.multiple_of(g * GW, GW), GW)
        weight = lambda i: wall[i, :, :, cols].reshape(d, GW)
        xv = x[...]
        q_s[g] = (dot(xv, weight(0)) + vec_o[QB:QB + 1, cols]).astype(BF)
        k_s[g] = dot(xv, weight(1)).astype(BF)
        v_s[g] = (dot(xv, weight(2)) + vec_o[VB:VB + 1, cols]).astype(BF)

        def one_pair(it, _):
            pair_forward(g, it, lambda h, i: jnp.sum(rb[h].astype(F32)[i:i + 1, :], axis=1, keepdims=True).astype(jnp.int32),
                         q_s.at[g], k_s.at[g], v_s.at[g], p_s.at[g], c_s.at[g], hm_o, bias, s_s)
            for slot, when in LATE:
                @pl.when(g * steps + it == when)
                def _():
                    for f in late:
                        f.step(slot)
            return 0

        lax.fori_loop(0, steps, one_pair, 0)
        for i in range(5):
            put(g, i).start()
        return 0

    lax.fori_loop(0, groups, group, 0)
    wo = wall[3].reshape(d, d)
    for g in range(groups):
        z_o[...] += dot(c_s[g], wo[g * GW:(g + 1) * GW, :])
    done = [slot for slot, _ in LATE]
    for slot in Gather.ORDER:
        if slot not in done:
            for f in late:
                f.step(slot)
    for f in late:
        f.finish()
    mine[1].wait()
    mine[2].wait()
    for f in flows:
        f.drain()
    keep.wait()
    for g in range(groups):
        for i in range(5):
            put(g, i).wait()


def front(rb, x, seg, wq, wk, wv, wo, vpart, wis, wus, n):
    rows, d = x.shape
    groups = d // GW
    maps = (groups, rows, GW // HD * SEQ)
    sd = jax.ShapeDtypeStruct
    vm, hbm = pl.BlockSpec(memory_space=pltpu.VMEM), pl.BlockSpec(memory_space=pl.ANY)
    whole = lambda a: (n,) + a.shape
    four = (4, n) + wq.shape
    act = (groups, rows, GW)
    return pl.pallas_call(
        front_body,
        in_specs=[vm] * 3 + [hbm] * 4 + [vm] * 3,
        out_specs=[hbm] * 3 + [vm] + [hbm] * 5 + [vm] * 2,
        out_shape=[sd(four, BF), sd(whole(wis), BF), sd(whole(wus), BF), sd((16, d), F32),
                   sd(act, BF), sd(act, BF), sd(act, BF), sd(maps, BF), sd(act, BF),
                   sd((rows, d), F32), sd((16, 128), F32)],
        scratch_shapes=[pltpu.VMEM(four, BF), pltpu.VMEM(whole(vpart), F32),
                        pltpu.VMEM((rows // SEQ, SEQ, SEQ), F32), pltpu.VMEM((2, SEQ, SEQ), F32),
                        pltpu.VMEM(act, BF), pltpu.VMEM(act, BF), pltpu.VMEM(act, BF),
                        pltpu.VMEM(maps, BF), pltpu.VMEM(act, BF),
                        pltpu.SemaphoreType.DMA((4, 32)), pltpu.SemaphoreType.DMA((4, 32)),
                        pltpu.SemaphoreType.DMA((7,)), pltpu.SemaphoreType.DMA((6,))],
        compiler_params=pltpu.CompilerParams(collective_id=0, has_side_effects=True, vmem_limit_bytes=VMEM_MAX),
        name="front",
    )(rb, x, seg, wq, wk, wv, wo, vpart, wis, wus)


class Scatter:
    def __init__(self, where, grad, rp, r1, r2, rz, sems):
        self.where, self.grad, self.rp, self.r1, self.r2, self.rz, self.sems = where, grad, rp, r1, r2, rz, sems

    def remote(self, src, dst, slot, off):
        return pltpu.make_async_remote_copy(
            src_ref=src, dst_ref=dst, send_sem=self.sems.at[0, slot], recv_sem=self.sems.at[1, slot],
            device_id=(self.where[0] + off,), device_id_type=MESH_ID)

    def begin(self):
        me, fc, d1, d2, zs = self.where
        for a in (1, 0):
            for b in (1, 0):
                for k in range(4):
                    self.remote(unit_of(self.grad, me + fc + a * d2 + b * d1 + zs[k]), self.rp.at[a, b, k], a, fc).start()

    def pair(self, a):
        me, fc, d1, d2, zs = self.where
        self.remote(self.rp.at[a], self.rp.at[a], a, fc).wait_recv()
        for b in (1, 0):
            for k in range(4):
                held = unit_of(self.grad, me + a * d1 + b * d2 + zs[k])[...]
                self.rp[a, b, k] = held + self.rp[a, b, k]
            if a == 1:
                self.remote(self.rp.at[1, b], self.r1.at[b], 2 + b, d1).start()

    def first(self, b):
        me, fc, d1, d2, zs = self.where
        self.remote(self.rp.at[1, b], self.r1.at[b], 2 + b, d1).wait_recv()
        self.rp[0, b] = self.rp[0, b] + self.r1[b]
        if b == 1:
            self.remote(self.rp.at[0, 1], self.r2, 4, d2).start()

    def second(self):
        me, fc, d1, d2, zs = self.where
        self.remote(self.rp.at[0, 1], self.r2, 4, d2).wait_recv()
        for k in (1, 2, 3):
            self.rp[0, 0, k] = self.rp[0, 0, k] + self.r2[k]
            self.remote(self.rp.at[0, 0, k], self.rz.at[k - 1], 4 + k, zs[k]).start()

    def near(self):
        return self.rp[0, 0, 0].astype(F32) + self.r2[0].astype(F32)

    def far(self, k):
        self.remote(self.rp.at[0, 0, k], self.rz.at[k - 1], 4 + k, self.where[4][k]).wait_recv()
        return self.rz[k - 1].astype(F32)

    def last(self):
        return self.near() + self.far(1) + self.far(2) + self.far(3)

    def core_sent(self):
        for a in (1, 0):
            self.remote(self.rp.at[a], self.rp.at[a], a, self.where[1]).wait_send()

    def drain(self):
        me, fc, d1, d2, zs = self.where
        for b in (1, 0):
            self.remote(self.rp.at[1, b], self.r1.at[b], 2 + b, d1).wait_send()
        self.remote(self.rp.at[0, 1], self.r2, 4, d2).wait_send()
        for k in (1, 2, 3):
            self.remote(self.rp.at[0, 0, k], self.rz.at[k - 1], 4 + k, zs[k]).wait_send()


class Plane(Scatter):
    def __init__(self, k, *rest):
        Scatter.__init__(self, *rest)
        self.k = k

    def begin(self):
        me, fc, d1, d2, zs = self.where
        for a in (1, 0):
            for b in (1, 0):
                self.remote(self.grad.at[lax.rem(me, 8) + fc + a * d2 + b * d1], self.rp.at[a, b], a, fc).start()

    def pair(self, a):
        me, fc, d1, d2, zs = self.where
        self.remote(self.rp.at[a], self.rp.at[a], a, fc).wait_recv()
        for b in (1, 0):
            held = self.grad[lax.rem(me, 8) + a * d1 + b * d2]
            self.rp[a, b] = held + self.rp[a, b]
            if a == 1:
                self.remote(self.rp.at[1, b], self.r1.at[b], 2 + b, d1).start()

    def along(self):
        return self.remote(self.rp.at[0, 0], self.rz.at[self.k - 1], 4 + self.k, self.where[4][self.k])

    def second(self):
        self.remote(self.rp.at[0, 1], self.r2, 4, self.where[3]).wait_recv()
        if self.k:
            self.rp[0, 0] = self.rp[0, 0] + self.r2[...]
            self.along().start()

    def near(self):
        return self.rp[0, 0].astype(F32) + self.r2[...].astype(F32)

    def far(self):
        self.along().wait_recv()
        return self.rz[self.k - 1].astype(F32)

    def drain(self):
        me, fc, d1, d2, zs = self.where
        for b in (1, 0):
            self.remote(self.rp.at[1, b], self.r1.at[b], 2 + b, d1).wait_send()
        self.remote(self.rp.at[0, 1], self.r2, 4, d2).wait_send()
        if self.k:
            self.along().wait_send()


def scatter_buffers(lead, shape):
    return [pltpu.VMEM(lead + (2, 2, 4) + shape, BF), pltpu.VMEM(lead + (2, 4) + shape, BF),
            pltpu.VMEM(lead + (4,) + shape, BF), pltpu.VMEM(lead + (3,) + shape, BF)]


class Vectors:
    def __init__(self, where, held, got, sems):
        self.where, self.held, self.got, self.sems = where, held, got, sems

    def remote(self, src, slot, off):
        return pltpu.make_async_remote_copy(
            src_ref=self.held.at[src], dst_ref=self.got.at[slot], send_sem=self.sems.at[0, slot],
            recv_sem=self.sems.at[1, slot], device_id=(self.where[0] + off,), device_id_type=MESH_ID)

    def merge(self, a, b):
        row = lax.broadcasted_iota(jnp.int32, a.shape, 0)
        return jnp.where(row == TOP, jnp.maximum(a, b), a + b)

    def step(self, i):
        me, fc, d1, d2, zs = self.where
        offs = (fc, d1, d2)
        if i > 0:
            self.remote(i - 1, i - 1, offs[i - 1]).wait_recv()
            self.held[i] = self.merge(self.held[i - 1], self.got[i - 1])
        if i < 3:
            self.remote(i, i, offs[i]).start()
        else:
            for k in (1, 2, 3):
                self.remote(3, 2 + k, zs[k]).start()

    def last(self):
        me, fc, d1, d2, zs = self.where
        total = self.held[3]
        for k in (1, 2, 3):
            self.remote(3, 2 + k, zs[k]).wait_recv()
            total = self.merge(total, self.got[2 + k])
        for i, off in enumerate((fc, d1, d2)):
            self.remote(i, i, off).wait_send()
        for k in (1, 2, 3):
            self.remote(3, 2 + k, zs[k]).wait_send()
        return total


def rear_body(z_h, cot_h, wi_h, wu_h, x_h, wall_h, q_h, k_h, v_h, c_h, p_h, vecs, hm,
              out_h, dx_h, o_q, o_k, o_v, o_o, o_i, o_u, vout,
              wi, wu, ag, z, dx, fl, do, db, gu, gi, gg, held, got, usems, nsems, sems, vsems, isem, osem, *bufs):
    where = place()
    zi = where[0] // 8
    rows, d = z.shape
    ff = wi.shape[1]
    groups, n = gg.shape[0], gi.shape[1]
    rt, et = 512, 128
    k0, k1 = math.sqrt(2.0 / math.pi), 0.044715
    act, gp, small = ag.at[0], ag.at[1], held.at[0]
    row = lambda i: vecs[i:i + 1, :]
    part = lambda j: pl.ds(pl.multiple_of(j * d, d), d)
    beside = lambda k: (zi % 2 + k % 2 - 2 * (zi % 2) * (k % 2)) + 2 * (zi // 2 + k // 2 - 2 * (zi // 2) * (k // 2))

    def up_flow(it):
        k = (it + 1) % 4 if isinstance(it, int) else None
        return Plane(k, where, gu.at[lax.rem(it, 2)], bufs[0].at[it], bufs[1].at[it], bufs[2].at[it], bufs[3], usems.at[it])

    def in_flow(it):
        return Scatter(where, gi.at[lax.rem(it, 2)], *(b.at[it] for b in bufs[4:8]), nsems.at[it])

    small_flow = Vectors(where, held, got, vsems)
    out_flow = Scatter(where, gi.at[0], *bufs[8:12], sems.at[0])
    group_flow = [Scatter(where, gg.at[g], *bufs[12 + 4 * g:16 + 4 * g], sems.at[1 + g]) for g in range(groups)]

    def get_up(j):
        return pltpu.make_async_copy(wi_h.at[:, part(j)], wi.at[:, part(j)], isem.at[j])

    def get_down(j):
        return pltpu.make_async_copy(wu_h.at[part(j)], wu.at[part(j)], isem.at[4 + j])

    def get_wall(i):
        return pltpu.make_async_copy(wall_h.at[i], wi.at[:, pl.ds(i * d, d)], isem.at[i])

    def get_ctx(g):
        return pltpu.make_async_copy(c_h.at[g], fl.at[:, pl.ds(g * GW, GW)], isem.at[4 + g])

    get_z = pltpu.make_async_copy(z_h, z, isem.at[8])
    get_cot = pltpu.make_async_copy(cot_h, do, isem.at[9])
    get_x = pltpu.make_async_copy(x_h, do, isem.at[9])
    put_out = pltpu.make_async_copy(db, out_h, osem)
    put_dx = pltpu.make_async_copy(dx, dx_h, osem)
    mid_cols = pl.ds(0, GW // HD * SEQ)

    def get_group(g, i):
        cols = pl.ds(pl.multiple_of(g * GW, GW), GW)
        src = (v_h, q_h, k_h, p_h)[i].at[g]
        dst = wu.at[pl.ds((2, 0, 1)[i] * rows, rows), cols] if i < 3 else ag.at[lax.rem(g, 2), :, mid_cols]
        return pltpu.make_async_copy(src, dst, isem.at[10 + 4 * lax.rem(g, 2) + i])

    get_z.start()
    for j in range(ff // d):
        get_up(j).start()
        get_down(j).start()
    get_cot.start()
    greet(*where)
    small[...] = jnp.zeros(small.shape, F32)
    get_z.wait()

    def prep(i, _):
        r = pl.ds(pl.multiple_of(i * et, et), et)
        unit, _inv = unit_rows(z[r, :])
        first = unit * row(AG) + row(ASH)
        fl[r, :] = first.astype(BF)
        dx[r, :] = first + row(BO)
        return 0

    lax.fori_loop(0, rows // et, prep, 0)

    def up(j, _):
        c = part(j)
        get_up(j).wait()
        get_down(j).wait()
        for i in range(rows // rt):
            r = slice(i * rt, (i + 1) * rt)
            u = dot(fl[r, :], wi[:, c]) + vecs[pl.ds(BI + j, 1), :]
            u2 = u * u
            t = jnp.tanh(u * (k0 + (k0 * k1) * u2))
            h = 0.5 + 0.5 * t
            a = (u * h).astype(BF)
            act[r, c] = a
            gp[r, c] = (h + (0.5 * u) * (1.0 - t * t) * (k0 + (3.0 * k0 * k1) * u2)).astype(BF)
            dx[r, :] += dot(a, wu[c, :])
        return 0

    lax.fori_loop(0, ff // d, up, 0)
    get_cot.wait()

    def mid(i, _):
        r = pl.ds(pl.multiple_of(i * et, et), et)
        unit, inv = unit_rows(dx[r, :])
        db[r, :] = (unit * row(FG) + row(FS)).astype(BF)
        upv = do[r, :].astype(F32)
        small[FG:FG + 1, :] += col_sum(upv * unit)
        small[FS:FS + 1, :] += col_sum(upv)
        ds = norm_back(upv, unit, inv, row(FG))
        dsl = ds.astype(BF)
        do[r, :] = dsl
        dx[r, :] = ds
        small[BO:BO + 1, :] += col_sum(dsl.astype(F32))
        return 0

    lax.fori_loop(0, rows // et, mid, 0)
    put_out.start()
    meet()

    def down(it, _):
        j = beside((it + 1) % 4)
        c = part(j)
        slot = lax.rem(it, 2)

        @pl.when(it >= 2)
        def _():
            up_flow(it - 2).core_sent()

        gu[slot] = dot_tn(act[:, c], do[...]).astype(BF).reshape(gu.shape[1:])
        up_flow(it).begin()
        sums = None
        for i in range(rows // rt):
            r = slice(i * rt, (i + 1) * rt)
            di = dot_nt(do[r, :], wu[c, :]) * gp[r, c].astype(F32)
            dil = di.astype(BF)
            act[r, c] = dil
            s = col_sum(dil.astype(F32))
            sums = s if sums is None else sums + s
            dx[r, :] += dot_nt(dil, wi[:, c])
            if i == 0:
                @pl.when(it >= 1)
                def _():
                    in_flow(it - 1).pair(1)
                    in_flow(it - 1).pair(0)
        small[pl.ds(BI + j, 1), :] = sums
        up_flow(it).pair(1)
        up_flow(it).pair(0)

        @pl.when(it >= 2)
        def _():
            in_flow(it - 2).core_sent()

        gi[slot] = dot_tn(fl[...], act[:, c]).reshape(gi.shape[1:]).astype(BF)
        in_flow(it).begin()

        @pl.when(it >= 2)
        def _():
            for f in (up_flow(it - 2), in_flow(it - 2)):
                f.first(1)
                f.first(0)

        return 0

    lax.fori_loop(0, ff // d, down, 0)
    get_wall(3).start()
    for i in range(4):
        get_group(0, i).start()
    for g in range(groups):
        get_ctx(g).start()
    get_x.start()
    for i in range(3):
        get_wall(i).start()
    put_out.wait()

    def tail(i, _):
        r = pl.ds(pl.multiple_of(i * et, et), et)
        unit, inv = unit_rows(z[r, :])
        df = dx[r, :]
        small[AG:AG + 1, :] += col_sum(df * unit)
        small[ASH:ASH + 1, :] += col_sum(df)
        ds = norm_back(df, unit, inv, row(AG))
        dx[r, :] = ds
        dsl = ds.astype(BF)
        db[r, :] = dsl
        small[OB:OB + 1, :] += col_sum(dsl.astype(F32))
        return 0

    lax.fori_loop(0, rows // et, tail, 0)
    in_flow(3).pair(1)
    in_flow(3).pair(0)
    for g in range(groups):
        get_ctx(g).wait()
    in_flow(2).core_sent()
    gi[0] = dot_tn(fl[...], db[...]).reshape(gi.shape[1:]).astype(BF)
    out_flow.begin()
    get_wall(3).wait()

    steps = (rows // SEQ) * (GW // 128)
    edge = GW // HD * SEQ
    dc = act.at[:, pl.ds(edge, GW)]
    dp_s = [z.at[pl.ds(j * SEQ, SEQ), pl.ds(0, SEQ)] for j in range(2)]
    ds_s = [gp.at[pl.ds(j * SEQ, SEQ), pl.ds(edge, SEQ)] for j in range(2)]
    both = lambda f: [(f.first, 1), (f.first, 0)]
    g0, g1, g2 = group_flow
    events = {
        0: [(up_flow(0).second,), (in_flow(0).second,), (out_flow.pair, 1)],
        1: [(out_flow.pair, 0)] + both(up_flow(2)),
        2: both(in_flow(2)) + [(up_flow(1).second,)],
        3: [(in_flow(1).second,)],
        4: both(up_flow(3)),
        5: both(in_flow(3)) + [(g0.pair, 1)],
        6: [(g0.pair, 0), (up_flow(2).second,), (out_flow.first, 1)],
        7: [(out_flow.first, 0), (in_flow(2).second,)],
        8: [(up_flow(3).second,), (in_flow(3).second,), (g0.first, 1)],
        9: [(g0.first, 0), (g1.pair, 1)],
        10: [(g1.pair, 0), (out_flow.second,)],
        11: [(g0.second,), (g1.first, 1)],
    }

    def group(g, _):
        cols = pl.ds(pl.multiple_of(g * GW, GW), GW)
        for i in range(4):
            get_group(g, i).wait()

        @pl.when(g + 1 < groups)
        def _():
            for i in range(4):
                get_group(g + 1, i).start()

        dc[...] = dot_nt(db[...], wi[cols, 3 * d:4 * d]).astype(BF)
        heads = [wu.at[pl.ds(i * rows, rows), cols] for i in range(3)]

        def one_pair(it, _):
            pair_backward(it, *heads, ag.at[lax.rem(g, 2)], dc, *heads, dp_s, ds_s)
            for when, todo in events.items():
                @pl.when(g * steps + it == when)
                def _():
                    for fn, *a in todo:
                        fn(*a)
            return 0

        lax.fori_loop(0, steps, one_pair, 0)

        @pl.when(g == 0)
        def _():
            get_x.wait()

        xv = do[...]
        for i, grad in enumerate(heads):
            gg[g, i] = dot_tn(xv, grad[...]).reshape(n, d // n, GW).astype(BF)
        for i in range(groups):
            @pl.when(g == i)
            def _():
                group_flow[i].begin()
        small[QB:QB + 1, cols] = col_sum(heads[0][...].astype(F32))
        small[VB:VB + 1, cols] = col_sum(heads[2][...].astype(F32))
        return 0

    lax.fori_loop(0, groups, group, 0)
    diag = lax.broadcasted_iota(jnp.int32, hm.shape, 0) == lax.broadcasted_iota(jnp.int32, hm.shape, 1)
    small[TOP:TOP + 1, 0:128] = jnp.sum(jnp.where(diag, hm[...], 0.0), axis=0, keepdims=True)
    small_flow.step(0)
    for i in range(3):
        get_wall(i).wait()
    quarter = rows // 4

    def inputs_part(t):
        grads = (wu[i * rows + t * quarter:i * rows + (t + 1) * quarter, :] for i in range(3))
        dx[t * quarter:(t + 1) * quarter, :] += sum(dot_nt(v, wi[:, i * d:(i + 1) * d]) for i, v in enumerate(grads))

    inputs_part(0)
    g2.pair(1)
    g2.pair(0)
    small_flow.step(1)
    inputs_part(1)
    g1.first(0)
    inputs_part(2)
    small_flow.step(2)
    g2.first(1)
    g1.second()
    g2.first(0)
    inputs_part(3)
    put_dx.start()
    small_flow.step(3)
    o_u[...] = up_flow(3).near() + up_flow(0).far() + up_flow(1).far() + up_flow(2).far()
    g2.second()
    for it in range(4):
        k = (it + 1) % 4
        total = in_flow(it).near()
        for m in (1, 2, 3):
            total = total + in_flow(((k ^ m) - 1) % 4).far(m)
        o_i[:, part(beside(k))] = total
    o_o[...] = out_flow.last()
    for g, f in enumerate(group_flow):
        t = f.last()
        for i, o in enumerate((o_q, o_k, o_v)):
            o[:, g * GW:(g + 1) * GW] = t[i]
    vout[...] = small_flow.last()
    put_dx.wait()
    up_flow(2).core_sent()
    up_flow(3).core_sent()
    in_flow(3).core_sent()
    for f in [out_flow] + group_flow:
        f.core_sent()
    for f in [up_flow(i) for i in range(4)] + [in_flow(i) for i in range(4)] + [out_flow] + group_flow:
        f.drain()


def rear(n, z, cot, wi, wu, x, wall, q, k, v, c, p, vecs, hm):
    rows, d = x.shape
    ff = wi.shape[1]
    groups = d // GW
    r, ru = d // n, ff // n
    sd = jax.ShapeDtypeStruct
    vm, hbm = pl.BlockSpec(memory_space=pltpu.VMEM), pl.BlockSpec(memory_space=pl.ANY)
    flat = pltpu.VMEM((rows, d), BF)
    bufs = [pltpu.VMEM((4, 2, 2, ru, d), BF), pltpu.VMEM((4, 2, ru, d), BF), pltpu.VMEM((4, ru, d), BF),
            pltpu.VMEM((3, ru, d), BF)]
    bufs += scatter_buffers((4,), (r, d)) + scatter_buffers((), (r, d))
    for _ in range(groups):
        bufs += scatter_buffers((), (3, r, GW))
    return pl.pallas_call(
        rear_body,
        in_specs=[hbm] * 11 + [vm] * 2,
        out_specs=[hbm] * 2 + [vm] * 7,
        out_shape=[sd((rows, d), BF), sd((rows, d), F32)] + [sd((r, d), F32)] * 4
        + [sd((r, ff), F32), sd((ru, d), F32), sd((16, d), F32)],
        scratch_shapes=[pltpu.VMEM((d, ff), BF), pltpu.VMEM((ff, d), BF), pltpu.VMEM((2, rows, ff), BF),
                        pltpu.VMEM((rows, d), F32), pltpu.VMEM((rows, d), F32), flat, flat, flat,
                        pltpu.VMEM((2, 8, ru, d), BF),
                        pltpu.VMEM((2, n, r, d), BF), pltpu.VMEM((groups, 3, n, r, GW), BF),
                        pltpu.VMEM((4, 16, d), F32), pltpu.VMEM((6, 16, d), F32),
                        pltpu.SemaphoreType.DMA((4, 2, 8)), pltpu.SemaphoreType.DMA((4, 2, 8)),
                        pltpu.SemaphoreType.DMA((1 + groups, 2, 8)), pltpu.SemaphoreType.DMA((2, 6)),
                        pltpu.SemaphoreType.DMA((18,)), pltpu.SemaphoreType.DMA] + bufs,
        compiler_params=pltpu.CompilerParams(collective_id=1, has_side_effects=True, vmem_limit_bytes=VMEM_MAX),
        name="rear",
    )(z, cot, wi, wu, x, wall, q, k, v, c, p, vecs, hm)


def attn_fwd_body(rb, x, segr, segc, wq, wk, wv, wo, vecs, q, k, v, p, c, z, hm, bias, s_s):
    g = pl.program_id(0)

    @pl.when(g == 0)
    def _():
        same_document(lambda s: segr[s:s + 1, :], lambda s, c: segc[s * SEQ + c * BLOCK:s * SEQ + (c + 1) * BLOCK, :], bias)
        hm[...] = jnp.full(hm.shape, LOW, F32)
        z[...] = x[...].astype(F32) + vecs[OB:OB + 1, :]

    cols = pl.ds(pl.multiple_of(g * GW, GW), GW)
    xv = x[...]
    q[...] = (dot(xv, wq[...]) + vecs[QB:QB + 1, cols]).astype(BF)
    k[...] = dot(xv, wk[...]).astype(BF)
    v[...] = (dot(xv, wv[...]) + vecs[VB:VB + 1, cols]).astype(BF)

    def one_pair(it, _):
        pair_forward(g, it, lambda h, i: rb[h * 18 + i * 3] + rb[h * 18 + i * 3 + 1] + rb[h * 18 + i * 3 + 2], q, k, v, p, c, hm, bias, s_s)
        return 0

    lax.fori_loop(0, x.shape[0] // SEQ * (GW // 128), one_pair, 0)
    z[...] += dot(c[...], wo[...])


def attn_fwd(rb, x, segr, segc, wall, vecs):
    rows, d = x.shape
    groups, seqs = d // GW, rows // SEQ
    keys = GW // HD * SEQ
    full = lambda shape: pl.BlockSpec(shape, lambda g, *_: (0,) * len(shape))
    col = lambda i: pl.BlockSpec((None, d, GW), lambda g, *_: (i, 0, g))
    act = pl.BlockSpec((None, rows, GW), lambda g, *_: (g, 0, 0))
    sd = jax.ShapeDtypeStruct
    return pl.pallas_call(
        attn_fwd_body,
        grid_spec=pltpu.PrefetchScalarGridSpec(
            num_scalar_prefetch=1, grid=(groups,),
            in_specs=[full((rows, d)), full((seqs, SEQ)), full((rows, 1)), col(0), col(1), col(2),
                      pl.BlockSpec((None, GW, d), lambda g, *_: (3, g, 0)), full((16, d))],
            out_specs=[act, act, act, pl.BlockSpec((None, rows, keys), lambda g, *_: (g, 0, 0)), act,
                       full((rows, d)), full((16, 128))],
            scratch_shapes=[pltpu.VMEM((seqs, SEQ, SEQ), F32), pltpu.VMEM((2, SEQ, SEQ), F32)]),
        out_shape=[sd((groups, rows, GW), BF)] * 3
        + [sd((groups, rows, keys), BF), sd((groups, rows, GW), BF), sd((rows, d), F32), sd((16, 128), F32)],
        compiler_params=pltpu.CompilerParams(vmem_limit_bytes=VMEM_MAX),
        name="attn_fwd",
    )(rb, x, segr, segc, wall, wall, wall, wall, vecs)


def attn_bwd_body(x, db, wq, wk, wv, wo, q, k, v, p, c, dsum, dw, dqb, dvb, dx, dc, dq, dk, dv, dp_s, ds_s):
    g = pl.program_id(0)

    @pl.when(g == 0)
    def _():
        dx[...] = dsum[...]

    dbv = db[...]
    cols = pl.ds(pl.multiple_of(g * GW, GW), GW)
    dc[...] = dot_nt(dbv, wo[...]).astype(BF)
    dw[3, cols, :] = dot_tn(c[...], dbv).astype(dw.dtype)

    def one_pair(it, _):
        pair_backward(it, q, k, v, p, dc, dq, dk, dv, [dp_s.at[0], dp_s.at[1]], [ds_s.at[0], ds_s.at[1]])
        return 0

    lax.fori_loop(0, x.shape[0] // SEQ * (GW // 128), one_pair, 0)
    dqb[...] = col_sum(dq[...].astype(F32))
    dvb[...] = col_sum(dv[...].astype(F32))
    xv = x[...]
    for i, part in enumerate((dq, dk, dv)):
        dw[i, :, cols] = dot_tn(xv, part[...]).astype(dw.dtype)
    dx[...] += dot_nt(dq[...], wq[...]) + dot_nt(dk[...], wk[...]) + dot_nt(dv[...], wv[...])


def attn_bwd(x, db, wall, q, k, v, p, c, dsum, gdt):
    rows, d = x.shape
    groups = d // GW
    keys = GW // HD * SEQ
    full = lambda shape: pl.BlockSpec(shape, lambda g: (0,) * len(shape), pipeline_mode=pl.Buffered(1))
    col = lambda i: pl.BlockSpec((None, d, GW), lambda g: (i, 0, g))
    vec = pl.BlockSpec((1, GW), lambda g: (0, g))
    act = pl.BlockSpec((None, rows, GW), lambda g: (g, 0, 0))
    sd = jax.ShapeDtypeStruct
    return pl.pallas_call(
        attn_bwd_body,
        grid=(groups,),
        in_specs=[full((rows, d)), full((rows, d)), col(0), col(1), col(2),
                  pl.BlockSpec((None, GW, d), lambda g: (3, g, 0)), act, act, act,
                  pl.BlockSpec((None, rows, keys), lambda g: (g, 0, 0)), act, full((rows, d))],
        out_specs=[full((4, d, d)), vec, vec, full((rows, d))],
        out_shape=[sd((4, d, d), gdt)] + [sd((1, d), F32)] * 2 + [sd((rows, d), F32)],
        scratch_shapes=[pltpu.VMEM((rows, GW), BF)] * 4
        + [pltpu.VMEM((2, SEQ, SEQ), F32), pltpu.VMEM((2, SEQ, SEQ), BF)],
        compiler_params=pltpu.CompilerParams(vmem_limit_bytes=VMEM_MAX),
        name="attn_bwd",
    )(x, db, wall, wall, wall, wall, q, k, v, p, c, dsum)


def far_layer(me, n, random_blocks, tokens, segment_ids, cot, weights, vecs, inner_weight, inner_bias, outer_weight, limit):
    d, ff = tokens.shape[1], inner_weight.shape[1]
    heads, part, wide = random_blocks.shape[0], vecs[0].shape[0], inner_bias.shape[0]
    wall = lax.all_gather(jnp.stack(weights), "dp", axis=1, tiled=True)
    wi, wu = (lax.all_gather(a, "dp", axis=0, tiled=True) for a in (inner_weight, outer_weight))
    vecs = lax.psum(vectors_part(me, n, vecs, inner_bias).astype(F32), "dp")
    q, k, v, p, c, z, hm = attn_fwd(random_blocks.reshape(-1), tokens, segment_ids.reshape(-1, SEQ),
                                    segment_ids.reshape(-1, 1), wall, vecs)
    out, dsum, db, dwi, dwu, small = ffn(z, cot, wi, wu, vecs, F32)
    dwall, dqb, dvb, dx = attn_bwd(tokens, db, wall, q, k, v, p, c, dsum, F32)
    mine = small.at[QB:QB + 1].set(dqb).at[VB:VB + 1].set(dvb).at[TOP, :hm.shape[0]].set(hm[:, 0])
    scatter = lambda a, at: lax.psum_scatter(a, "dp", scatter_dimension=at, tiled=True)
    dwu, dwi, dwall = scatter(dwu, 0), scatter(dwi, 0), scatter(dwall, 1)
    row = lax.broadcasted_iota(jnp.int32, mine.shape, 0)
    total = jnp.where(row == TOP, lax.pmax(mine, "dp"), lax.psum(mine, "dp"))
    vec8 = lax.dynamic_slice(total, (0, me * part), (8, part))
    dbi = lax.dynamic_slice(total[BI:BI + ff // d].reshape(-1), (me * wide,), (wide,))
    head_maxima = total[TOP, :heads]
    factor = jnp.sqrt(jnp.minimum(1.0, limit[0].astype(F32) / jnp.maximum(head_maxima, 1.0)))
    columns = jnp.repeat(factor, HD)[None, :]
    cq, ck = ((w.astype(F32) * columns).astype(BF) for w in weights[:2])
    return out, dx, dwall[0], dwall[1], dwall[2], dwall[3], dwi, dwu, [vec8[i] for i in range(8)], dbi, cq, ck, head_maxima


def near_layer(me, n, random_blocks, tokens, segment_ids, cot, weights, vecs, inner_weight, inner_bias, outer_weight, limit):
    d, ff = tokens.shape[1], inner_weight.shape[1]
    heads, part, wide = random_blocks.shape[0], vecs[0].shape[0], inner_bias.shape[0]
    pieces = jnp.concatenate([jnp.pad(jnp.stack(vecs), ((0, 0), (0, 128 - part))),
                              jnp.pad(inner_bias[None, :], ((0, 7), (0, 128 - wide)))]).astype(F32)
    wall, wi, wu, vec, q, k, v, p, c, z, hm = front(random_blocks, tokens, segment_ids.reshape(-1, 128), *weights, pieces,
                                                    inner_weight, outer_weight, n)
    raw = rear(n, z, cot, wi.reshape(d, ff), wu.reshape(ff, d), tokens, wall.reshape(4, d, d), q, k, v, c, p, vec, hm)
    out, dx, dwq, dwk, dwv, dwo, dwi, dwu, cq, ck, *fins = finish(n, heads, limit, weights[0], weights[1], *raw)
    fins = [a.reshape(-1) for a in fins]
    return out, dx, dwq, dwk, dwv, dwo, dwi, dwu, fins[:8], fins[8], cq, ck, fins[9]


def finish_body(n, heads, limit, wq, wk, total, *refs):
    count = 8
    srcs, dsts, refs = refs[:count], refs[count:2 * count], refs[2 * count:]
    (cq, ck), fins, held, sems = refs[:2], refs[2:12], refs[12:-1], refs[-1]
    jobs = []
    for src, dst, tmp in zip(srcs, dsts, held):
        cut = 4 if src.shape[0] >= 512 else 1
        step = src.shape[0] // cut
        for i in range(cut):
            at = pl.ds(i * step, step)
            slot = len(jobs)
            jobs.append((pltpu.make_async_copy(src.at[at], tmp.at[at], sems.at[0, slot]),
                         pltpu.make_async_copy(tmp.at[at], dst.at[at], sems.at[1, slot])))
    for get, _ in jobs:
        get.start()
    me = lax.axis_index("dp")
    d = total.shape[1]
    part, wide = d // n, held[7].shape[0]
    top = total[TOP:TOP + 1, 0:128]
    head = lax.broadcasted_iota(jnp.int32, (1, d), 1) // HD
    columns = jnp.zeros((1, d), F32)
    for h in range(heads):
        columns = jnp.where(head == h, top[:, h:h + 1], columns)
    factor = jnp.sqrt(jnp.minimum(1.0, limit[0].astype(F32) / jnp.maximum(columns, 1.0)))
    cq[...] = (wq[...].astype(F32) * factor).astype(BF)
    ck[...] = (wk[...].astype(F32) * factor).astype(BF)
    mine = pltpu.roll(total[0:8, :], d - me * part, 1)
    for i in range(8):
        fins[i][...] = mine[i:i + 1, 0:part]
    per = d // wide
    inner = jnp.broadcast_to(total[pl.ds(BI + me // per, 1), :], (8, d))
    fins[8][...] = pltpu.roll(inner, d - (me % per) * wide, 1)[0:1, 0:wide]
    fins[9][...] = top[:, 0:heads]
    for get, put in jobs:
        get.wait()
        put.start()
    for _, put in jobs:
        put.wait()


def finish(n, heads, limit, wq, wk, *raw):
    mats, total = raw[:8], raw[8]
    vm, hbm = pl.BlockSpec(memory_space=pltpu.VMEM), pl.BlockSpec(memory_space=pl.ANY)
    sd = jax.ShapeDtypeStruct
    return pl.pallas_call(
        partial(finish_body, n, heads),
        in_specs=[pl.BlockSpec(memory_space=pltpu.SMEM)] + [vm] * 3 + [hbm] * 8,
        out_specs=[hbm] * 8 + [vm] * 12,
        out_shape=[sd(a.shape, a.dtype) for a in mats] + [sd(wq.shape, BF)] * 2 + [sd((1, mats[2].shape[0]), F32)] * 8
        + [sd((1, mats[7].shape[0]), F32), sd((1, heads), F32)],
        scratch_shapes=[pltpu.VMEM(a.shape, a.dtype) for a in mats] + [pltpu.SemaphoreType.DMA((2, 16))],
        compiler_params=pltpu.CompilerParams(vmem_limit_bytes=VMEM_MAX),
        name="finish",
    )(limit, wq, wk, total, *mats)


def vectors_part(me, n, vecs, inner_bias):
    part = vecs[0].shape[0]
    d = part * n
    rows = jnp.tile(jnp.stack(vecs), (1, n))
    rows = jnp.where(lax.broadcasted_iota(jnp.int32, rows.shape, 1) // part == me, rows, 0)
    flat = jnp.tile(inner_bias, n)
    flat = jnp.where(lax.broadcasted_iota(jnp.int32, flat.shape, 0) // inner_bias.shape[0] == me, flat, 0)
    flat = flat.reshape(-1, d)
    rest = jnp.zeros((16 - rows.shape[0] - flat.shape[0], d), BF)
    return jnp.concatenate([rows, flat, rest], axis=0)


def per_device(n, tokens, segment_ids, random_blocks, clip_limit, query_weight, query_bias, key_weight, value_weight,
               value_bias, output_weight, output_bias, attn_gain, attn_shift, inner_weight, inner_bias,
               outer_weight, outer_bias, final_gain, final_shift, out_cotangent):
    rows, d = tokens.shape
    near = n == 32 and (rows, d, inner_weight.shape[1]) == (2 * SEQ, 3 * GW, 6 * SEQ)
    weights = (query_weight, key_weight, value_weight, output_weight)
    vecs = (query_bias, value_bias, output_bias, attn_gain, attn_shift, outer_bias, final_gain, final_shift)
    out, dx, dwq, dwk, dwv, dwo, dwi, dwu, vec8, dbi, cq, ck, head_maxima = (near_layer if near else far_layer)(
        lax.axis_index("dp"), n, random_blocks, tokens, segment_ids, out_cotangent, weights, vecs, inner_weight, inner_bias,
        outer_weight, clip_limit)
    dqb, dvb, dob, dag, dash, dbo, dfg, dfs = vec8
    return (out, dx, dwq, dqb, dwk, dwv, dvb, dwo, dob, dag, dash, dwi, dbi, dwu, dbo, dfg, dfs, cq, ck, head_maxima)


def solution(mesh):
    mat, vec, rep = P("dp", None), P("dp"), P()
    in_specs = (mat, vec, rep, rep, mat, vec, mat, mat, vec, mat, vec, vec, vec, mat, vec, mat, vec, vec, vec, mat)
    out_specs = (mat, mat, mat, vec, mat, mat, vec, mat, vec, vec, vec, mat, vec, mat, vec, vec, vec, mat, mat, rep)
    return jax.shard_map(partial(per_device, mesh.shape["dp"]), mesh=mesh, in_specs=in_specs, out_specs=out_specs,
                         check_vma=False)
```

```python
from functools import partial
import math

import jax
import jax.numpy as jnp
from jax import lax
from jax.experimental import pallas as pl
from jax.experimental.pallas import tpu as pltpu
from jax.sharding import PartitionSpec as P

HD = 64
BLOCK = 64
SEQ = 512
GW = 256
BF = jnp.bfloat16
F32 = jnp.float32
LOW = -1e30
VMEM_MAX = 67043328
MESH_ID = pl.DeviceIdType.MESH
QB, VB, OB, AG, ASH, BO, FG, FS, BI, TOP = 0, 1, 2, 3, 4, 5, 6, 7, 8, 12


def dot(a, b):
    return jnp.dot(a, b, preferred_element_type=F32)


def dot_nt(a, b):
    return lax.dot_general(a, b, (((1,), (1,)), ((), ())), preferred_element_type=F32)


def dot_tn(a, b):
    return lax.dot_general(a, b, (((0,), (0,)), ((), ())), preferred_element_type=F32)


def col_sum(v):
    return jnp.sum(v, axis=0, keepdims=True)


def first_half():
    return lax.broadcasted_iota(jnp.int32, (1, 128), 1) < HD


def same_document(key_ids, query_ids, bias):
    for s in range(bias.shape[0]):
        kseg = key_ids(s)
        for c in range(SEQ // BLOCK):
            bias[s, c * BLOCK:(c + 1) * BLOCK, :] = jnp.where((query_ids(s, c) == kseg) & (kseg != 0), 0.0, LOW)


def same_document_flat(seg, bias):
    ids = seg[...].astype(F32)
    turned = jnp.transpose(ids)
    per = SEQ // 128
    key_ids = lambda s: jnp.concatenate([ids[s * per + i:s * per + i + 1, :] for i in range(per)], axis=1)

    def query_ids(s, c):
        i, r = s * per + c * BLOCK // 128, c * BLOCK % 128
        return turned[r:r + BLOCK, i:i + 1]

    same_document(key_ids, query_ids, bias)


def whole_vectors(pieces, vec, wide):
    n, d = pieces.shape[0], vec.shape[1]
    lane = lax.broadcasted_iota(jnp.int32, (1, 128), 1)

    def spread(values, width):
        tiles = [0.0] * (d // 128)
        for i, value in enumerate(values):
            t, at = i * width // 128, i * width % 128
            moved = pltpu.roll(value, at, 1) if at else value
            tiles[t] = tiles[t] + (jnp.where(lane >= at, moved, 0.0) if at + width > 128 else moved)
            if at + width > 128:
                tiles[t + 1] = tiles[t + 1] + jnp.where(lane < at, moved, 0.0)
        return jnp.concatenate(tiles, axis=1)

    vec[0:8, :] = spread([pieces[u, 0:8, :] for u in range(n)], d // n)
    per = d // wide
    inner = [spread([pieces[j * per + i, 8:16, :] for i in range(per)], wide) for j in range(n // per)]
    for j, v in enumerate(inner):
        vec[8 + j:9 + j, :] = v[0:1, :]
    vec[8 + len(inner):16, :] = jnp.zeros((8 - len(inner), d), F32)


def pair_forward(g, it, rb, q, k, v, p, ctx, hm, bias, s_s):
    pairs = GW // 128
    s, pair = it // pairs, it % pairs
    rows = pl.ds(pl.multiple_of(s * SEQ, SEQ), SEQ)
    lanes = pl.ds(pl.multiple_of(pair * 128, 128), 128)
    lane_block = lax.broadcasted_iota(jnp.int32, (1, SEQ), 1) // BLOCK
    half = first_half()
    last = SEQ // BLOCK - 2
    qp, kp, vp = q[rows, lanes], k[rows, lanes], v[rows, lanes]
    outs = []
    for j in range(2):
        head = g * (2 * pairs) + pair * 2 + j
        keys = pl.ds(pl.multiple_of((pair * 2 + j) * SEQ, SEQ), SEQ)
        mine = half if j == 0 else jnp.logical_not(half)
        s_s[j] = dot_nt(jnp.where(mine, qp * 0.125, 0).astype(BF), kp)
        miss1, miss6 = 18 - rb(head, 0), 10 - rb(head, 5)
        skip1 = jnp.where(lane_block == miss1, LOW, 0.0)
        skip6 = jnp.where(lane_block == miss6, LOW, 0.0)
        tops = None
        for c in range(SEQ // BLOCK):
            cr = slice(c * BLOCK, (c + 1) * BLOCK)
            sv = s_s[j, cr, :] + bias[s, cr, :]
            if c == 1:
                sv = sv + skip1
            if c == last:
                sv = sv + skip6
            top = jnp.max(sv, axis=1, keepdims=True)
            live = top > -1e29
            e = jnp.exp(sv - jnp.where(live, top, 0.0))
            total = jnp.sum(e, axis=1, keepdims=True) + jnp.where(live, 0.0, 1.0)
            p[pl.ds(pl.multiple_of(s * SEQ + c * BLOCK, BLOCK), BLOCK), keys] = (e * (1.0 / total)).astype(BF)
            tops = top if tops is None else jnp.maximum(tops, top)
        top = jnp.max(tops, axis=0, keepdims=True)
        hm[pl.ds(head, 1), :] = jnp.maximum(hm[pl.ds(head, 1), :], top)
        outs.append(dot(p[rows, keys], vp))
    ctx[rows, lanes] = jnp.where(half, outs[0], outs[1]).astype(BF)


def pair_backward(it, q, k, v, p, dc, dq, dk, dv, dp_s, ds_s):
    pairs = GW // 128
    s, pair = it // pairs, it % pairs
    rows = pl.ds(pl.multiple_of(s * SEQ, SEQ), SEQ)
    lanes = pl.ds(pl.multiple_of(pair * 128, 128), 128)
    half = first_half()
    qp, kp, vp, dcp = q[rows, lanes], k[rows, lanes], v[rows, lanes], dc[rows, lanes]
    dqs, dks, dvs = [], [], []
    for j in range(2):
        mine = half if j == 0 else jnp.logical_not(half)
        keys = pl.ds(pl.multiple_of((pair * 2 + j) * SEQ, SEQ), SEQ)
        dp_s[j][...] = dot_nt(jnp.where(mine, dcp, 0).astype(BF), vp)
        for c in range(SEQ // BLOCK):
            cr = slice(c * BLOCK, (c + 1) * BLOCK)
            pv = p[pl.ds(pl.multiple_of(s * SEQ + c * BLOCK, BLOCK), BLOCK), keys].astype(F32)
            sl = dp_s[j][cr, :]
            mean = jnp.sum(pv * sl, axis=1, keepdims=True)
            ds_s[j][cr, :] = (pv * (sl - mean)).astype(BF)
        dqs.append(dot(ds_s[j][...], kp))
        dks.append(dot_tn(ds_s[j][...], qp))
        dvs.append(dot_tn(p[rows, keys], dcp))
    dq[rows, lanes] = (jnp.where(half, dqs[0], dqs[1]) * 0.125).astype(BF)
    dk[rows, lanes] = (jnp.where(half, dks[0], dks[1]) * 0.125).astype(BF)
    dv[rows, lanes] = jnp.where(half, dvs[0], dvs[1]).astype(BF)


def unit_rows(z):
    mean = jnp.mean(z, axis=-1, keepdims=True)
    c = z - mean
    inv = lax.rsqrt(jnp.mean(c * c, axis=-1, keepdims=True) + 1e-12)
    return c * inv, inv


def norm_back(up, unit, inv, gain):
    e = up * gain
    spread = jnp.mean(e, axis=-1, keepdims=True)
    along = jnp.mean(e * unit, axis=-1, keepdims=True)
    return inv * (e - spread - unit * along)


def ffn_body(z, cot, wi, wo, vecs, out, dsum, db, dwi, dwo, small, fl, act, gp, acc, do):
    rows, d = z.shape
    ff = wi.shape[1]
    rt, et = 512, 128
    k0, k1 = math.sqrt(2.0 / math.pi), 0.044715
    row = lambda i: vecs[i:i + 1, :]
    small[...] = jnp.zeros(small.shape, F32)

    def prep(i, _):
        r = pl.ds(pl.multiple_of(i * et, et), et)
        unit, _inv = unit_rows(z[r, :])
        first = unit * row(AG) + row(ASH)
        fl[r, :] = first.astype(BF)
        acc[r, :] = first + row(BO)
        return 0

    lax.fori_loop(0, rows // et, prep, 0)

    def up(i, _):
        j = i // (rows // rt)
        r = pl.ds(pl.multiple_of((i % (rows // rt)) * rt, rt), rt)
        c = pl.ds(pl.multiple_of(j * d, d), d)
        u = dot(fl[r, :], wi[:, c]) + vecs[pl.ds(BI + j, 1), :]
        u2 = u * u
        t = jnp.tanh(u * (k0 + (k0 * k1) * u2))
        h = 0.5 + 0.5 * t
        a = (u * h).astype(BF)
        act[r, c] = a
        gp[r, c] = (h + (0.5 * u) * (1.0 - t * t) * (k0 + (3.0 * k0 * k1) * u2)).astype(gp.dtype)
        acc[r, :] += dot(a, wo[c, :])
        return 0

    lax.fori_loop(0, (ff // d) * (rows // rt), up, 0)

    def mid(i, _):
        r = pl.ds(pl.multiple_of(i * et, et), et)
        unit, inv = unit_rows(acc[r, :])
        out[r, :] = (unit * row(FG) + row(FS)).astype(BF)
        upv = cot[r, :].astype(F32)
        small[FG:FG + 1, :] += col_sum(upv * unit)
        small[FS:FS + 1, :] += col_sum(upv)
        ds = norm_back(upv, unit, inv, row(FG))
        dsl = ds.astype(BF)
        do[r, :] = dsl
        acc[r, :] = ds
        small[BO:BO + 1, :] += col_sum(dsl.astype(F32))
        return 0

    lax.fori_loop(0, rows // et, mid, 0)

    def down(j, _):
        c = pl.ds(pl.multiple_of(j * d, d), d)
        dwo[c, :] = dot_tn(act[:, c], do[...]).astype(dwo.dtype)
        sums = None
        for i in range(rows // rt):
            r = slice(i * rt, (i + 1) * rt)
            di = dot_nt(do[r, :], wo[c, :]) * gp[r, c].astype(F32)
            dil = di.astype(BF)
            act[r, c] = dil
            s = col_sum(dil.astype(F32))
            sums = s if sums is None else sums + s
            acc[r, :] += dot_nt(dil, wi[:, c])
        small[pl.ds(BI + j, 1), :] = sums
        dwi[:, c] = dot_tn(fl[...], act[:, c]).astype(dwi.dtype)
        return 0

    lax.fori_loop(0, ff // d, down, 0)

    def tail(i, _):
        r = pl.ds(pl.multiple_of(i * et, et), et)
        unit, inv = unit_rows(z[r, :])
        df = acc[r, :]
        small[AG:AG + 1, :] += col_sum(df * unit)
        small[ASH:ASH + 1, :] += col_sum(df)
        ds = norm_back(df, unit, inv, row(AG))
        dsum[r, :] = ds
        dsl = ds.astype(BF)
        db[r, :] = dsl
        small[OB:OB + 1, :] += col_sum(dsl.astype(F32))
        return 0

    lax.fori_loop(0, rows // et, tail, 0)


def ffn(z, cot, wi, wo, vecs, gdt):
    rows, d = z.shape
    ff = wi.shape[1]
    sd = jax.ShapeDtypeStruct
    vm = pl.BlockSpec(memory_space=pltpu.VMEM)
    return pl.pallas_call(
        ffn_body,
        in_specs=[vm] * 5,
        out_specs=[vm] * 6,
        out_shape=[sd((rows, d), BF), sd((rows, d), F32), sd((rows, d), BF), sd((d, ff), gdt), sd((ff, d), gdt),
                   sd((16, d), F32)],
        scratch_shapes=[pltpu.VMEM((rows, d), BF), pltpu.VMEM((rows, ff), BF), pltpu.VMEM((rows, ff), BF),
                        pltpu.VMEM((rows, d), F32), pltpu.VMEM((rows, d), BF)],
        compiler_params=pltpu.CompilerParams(vmem_limit_bytes=VMEM_MAX),
        name="ffn",
    )(z, cot, wi, wo, vecs)


def place():
    me = lax.axis_index("dp")
    c, x, y, z = me % 2, (me // 2) % 2, (me // 4) % 2, me // 8
    fc, fx, fy = 1 - 2 * c, 2 * (1 - 2 * x), 4 * (1 - 2 * y)
    d1 = fx * (1 - c) + fy * c
    d2 = fy * (1 - c) + fx * c
    zs = (0, 8 * (1 - 2 * (z % 2)), 16 * (1 - 2 * (z // 2)), 8 * (3 - 2 * z))
    return me, fc, d1, d2, zs


def greet(me, fc, d1, d2, zs):
    for off in (fc, d1, d2) + zs[1:]:
        pl.semaphore_signal(pltpu.get_barrier_semaphore(), inc=1, device_id=(me + off,), device_id_type=MESH_ID)


def meet():
    pl.semaphore_wait(pltpu.get_barrier_semaphore(), 6)


def unit_of(ref, unit):
    return ref.at[:, unit] if len(ref.shape) == 4 else ref.at[unit]


class Gather:
    ORDER = (1, 4, 2, 5, 8, 3, 6, 9, 7, 12, 10, 13, 11, 14, 15)

    def __init__(self, where, own, out, send, recv):
        self.where, self.own, self.out, self.send, self.recv = where, own, out, send, recv

    def copy(self, slot, unit, dest, own=False):
        return pltpu.make_async_remote_copy(
            src_ref=self.own if own else unit_of(self.out, unit), dst_ref=unit_of(self.out, unit),
            send_sem=self.send.at[slot], recv_sem=self.recv.at[slot], device_id=(dest,), device_id_type=MESH_ID)

    def begin_z(self):
        me, fc, d1, d2, zs = self.where
        for k in (1, 2, 3):
            self.copy(k, me, me + zs[k], True).start()

    def begin_xy(self):
        me, fc, d1, d2, zs = self.where
        self.copy(4, me, me + d1, True).start()
        self.copy(8, me, me + d2, True).start()
        self.copy(16, me, me + fc, True).start()

    def landed(self, slot):
        me, fc, d1, d2, zs = self.where
        unit = me + zs[slot % 4] + (0, d1, d2, d1 + d2, fc, fc + d2, fc + d1, fc + d1 + d2)[slot // 4]
        self.copy(slot, unit, me).wait_recv()
        return unit

    def step(self, slot):
        me, fc, d1, d2, zs = self.where
        k, group = slot % 4, slot // 4
        unit = self.landed(slot)
        if group == 0:
            self.copy(4 + k, unit, me + d1).start()
            self.copy(8 + k, unit, me + d2).start()
        if group == 1:
            self.copy(12 + k, unit, me + d2).start()
        self.copy(16 + slot, unit, me + fc).start()

    def finish(self):
        for slot in range(16, 32):
            self.landed(slot)

    def drain(self):
        me = self.where[0]
        for slot in range(1, 32):
            self.copy(slot, me, me, slot in (1, 2, 3, 4, 8, 16)).wait_send()


LATE = ((1, 0), (4, 1), (2, 2), (5, 3), (8, 4), (3, 5), (6, 6), (9, 7), (7, 8), (12, 9), (10, 10), (13, 11))


def front_body(rb, x, seg, wq, wk, wv, wo, vpart, wis, wus,
               wall_o, wi_o, wu_o, vec_o, q_o, k_o, v_o, p_o, c_o, z_o, hm_o,
               wall, vg, bias, s_s, q_s, k_s, v_s, p_s, c_s, send, recv, local, outs):
    where = place()
    me = where[0]
    rows, d = x.shape
    groups = d // GW
    steps = (rows // SEQ) * (GW // 128)
    owns, targets = (wall.at[:, me], vpart, wis, wus), (wall, vg, wi_o, wu_o)
    mine = [pltpu.make_async_copy(o, unit_of(t, me), local.at[i]) for i, (o, t) in enumerate(zip(owns[1:], targets[1:]))]
    four = [pltpu.make_async_copy(w, wall.at[i, me], local.at[3 + i]) for i, w in enumerate((wq, wk, wv, wo))]
    for m in four + mine:
        m.start()
    greet(*where)
    for m in four:
        m.wait()
    meet()
    flows = [Gather(where, o, t, send.at[i], recv.at[i]) for i, (o, t) in enumerate(zip(owns, targets))]
    early, late = flows[:2], flows[2:]
    for f in early:
        f.begin_z()
    for f in early:
        f.begin_xy()
    same_document_flat(seg, bias)
    for slot in Gather.ORDER:
        for f in early:
            f.step(slot)
        if slot == 3:
            for f in late:
                f.begin_z()
    for f in late:
        f.begin_xy()
    for f in early:
        f.finish()
    mine[0].wait()
    keep = pltpu.make_async_copy(wall, wall_o, outs.at[5])
    keep.start()
    whole_vectors(vg, vec_o, wus.shape[0])
    hm_o[...] = jnp.full(hm_o.shape, LOW, F32)
    z_o[...] = x[...].astype(F32) + vec_o[OB:OB + 1, :]

    def put(g, i):
        src = (q_s, k_s, v_s, c_s)[i].at[g] if i < 4 else p_s.at[g]
        return pltpu.make_async_copy(src, (q_o, k_o, v_o, c_o, p_o)[i].at[g], outs.at[i])

    def group(g, _):
        cols = pl.ds(pl.multiple_of(g * GW, GW), GW)
        weight = lambda i: wall[i, :, :, cols].reshape(d, GW)
        xv = x[...]
        q_s[g] = (dot(xv, weight(0)) + vec_o[QB:QB + 1, cols]).astype(BF)
        k_s[g] = dot(xv, weight(1)).astype(BF)
        v_s[g] = (dot(xv, weight(2)) + vec_o[VB:VB + 1, cols]).astype(BF)

        def one_pair(it, _):
            pair_forward(g, it, lambda h, i: jnp.sum(rb[h].astype(F32)[i:i + 1, :], axis=1, keepdims=True).astype(jnp.int32),
                         q_s.at[g], k_s.at[g], v_s.at[g], p_s.at[g], c_s.at[g], hm_o, bias, s_s)
            for slot, when in LATE:
                @pl.when(g * steps + it == when)
                def _():
                    for f in late:
                        f.step(slot)
            return 0

        lax.fori_loop(0, steps, one_pair, 0)
        for i in range(5):
            put(g, i).start()
        return 0

    lax.fori_loop(0, groups, group, 0)
    wo = wall[3].reshape(d, d)
    for g in range(groups):
        z_o[...] += dot(c_s[g], wo[g * GW:(g + 1) * GW, :])
    done = [slot for slot, _ in LATE]
    for slot in Gather.ORDER:
        if slot not in done:
            for f in late:
                f.step(slot)
    for f in late:
        f.finish()
    mine[1].wait()
    mine[2].wait()
    for f in flows:
        f.drain()
    keep.wait()
    for g in range(groups):
        for i in range(5):
            put(g, i).wait()


def front(rb, x, seg, wq, wk, wv, wo, vpart, wis, wus, n):
    rows, d = x.shape
    groups = d // GW
    maps = (groups, rows, GW // HD * SEQ)
    sd = jax.ShapeDtypeStruct
    vm, hbm = pl.BlockSpec(memory_space=pltpu.VMEM), pl.BlockSpec(memory_space=pl.ANY)
    whole = lambda a: (n,) + a.shape
    four = (4, n) + wq.shape
    act = (groups, rows, GW)
    return pl.pallas_call(
        front_body,
        in_specs=[vm] * 3 + [hbm] * 4 + [vm] * 3,
        out_specs=[hbm] * 3 + [vm] + [hbm] * 5 + [vm] * 2,
        out_shape=[sd(four, BF), sd(whole(wis), BF), sd(whole(wus), BF), sd((16, d), F32),
                   sd(act, BF), sd(act, BF), sd(act, BF), sd(maps, BF), sd(act, BF),
                   sd((rows, d), F32), sd((16, 128), F32)],
        scratch_shapes=[pltpu.VMEM(four, BF), pltpu.VMEM(whole(vpart), F32),
                        pltpu.VMEM((rows // SEQ, SEQ, SEQ), F32), pltpu.VMEM((2, SEQ, SEQ), F32),
                        pltpu.VMEM(act, BF), pltpu.VMEM(act, BF), pltpu.VMEM(act, BF),
                        pltpu.VMEM(maps, BF), pltpu.VMEM(act, BF),
                        pltpu.SemaphoreType.DMA((4, 32)), pltpu.SemaphoreType.DMA((4, 32)),
                        pltpu.SemaphoreType.DMA((7,)), pltpu.SemaphoreType.DMA((6,))],
        compiler_params=pltpu.CompilerParams(collective_id=0, has_side_effects=True, vmem_limit_bytes=VMEM_MAX),
        name="front",
    )(rb, x, seg, wq, wk, wv, wo, vpart, wis, wus)


class Scatter:
    def __init__(self, where, grad, rp, r1, r2, rz, sems):
        self.where, self.grad, self.rp, self.r1, self.r2, self.rz, self.sems = where, grad, rp, r1, r2, rz, sems

    def remote(self, src, dst, slot, off):
        return pltpu.make_async_remote_copy(
            src_ref=src, dst_ref=dst, send_sem=self.sems.at[0, slot], recv_sem=self.sems.at[1, slot],
            device_id=(self.where[0] + off,), device_id_type=MESH_ID)

    def begin(self):
        me, fc, d1, d2, zs = self.where
        for a in (1, 0):
            for b in (1, 0):
                for k in range(4):
                    self.remote(unit_of(self.grad, me + fc + a * d2 + b * d1 + zs[k]), self.rp.at[a, b, k], a, fc).start()

    def pair(self, a):
        me, fc, d1, d2, zs = self.where
        self.remote(self.rp.at[a], self.rp.at[a], a, fc).wait_recv()
        for b in (1, 0):
            for k in range(4):
                held = unit_of(self.grad, me + a * d1 + b * d2 + zs[k])[...]
                self.rp[a, b, k] = held + self.rp[a, b, k]
            if a == 1:
                self.remote(self.rp.at[1, b], self.r1.at[b], 2 + b, d1).start()

    def first(self, b):
        me, fc, d1, d2, zs = self.where
        self.remote(self.rp.at[1, b], self.r1.at[b], 2 + b, d1).wait_recv()
        self.rp[0, b] = self.rp[0, b] + self.r1[b]
        if b == 1:
            self.remote(self.rp.at[0, 1], self.r2, 4, d2).start()

    def second(self):
        me, fc, d1, d2, zs = self.where
        self.remote(self.rp.at[0, 1], self.r2, 4, d2).wait_recv()
        for k in (1, 2, 3):
            self.rp[0, 0, k] = self.rp[0, 0, k] + self.r2[k]
            self.remote(self.rp.at[0, 0, k], self.rz.at[k - 1], 4 + k, zs[k]).start()

    def near(self):
        return self.rp[0, 0, 0].astype(F32) + self.r2[0].astype(F32)

    def far(self, k):
        self.remote(self.rp.at[0, 0, k], self.rz.at[k - 1], 4 + k, self.where[4][k]).wait_recv()
        return self.rz[k - 1].astype(F32)

    def last(self):
        return self.near() + self.far(1) + self.far(2) + self.far(3)

    def core_sent(self):
        for a in (1, 0):
            self.remote(self.rp.at[a], self.rp.at[a], a, self.where[1]).wait_send()

    def drain(self):
        me, fc, d1, d2, zs = self.where
        for b in (1, 0):
            self.remote(self.rp.at[1, b], self.r1.at[b], 2 + b, d1).wait_send()
        self.remote(self.rp.at[0, 1], self.r2, 4, d2).wait_send()
        for k in (1, 2, 3):
            self.remote(self.rp.at[0, 0, k], self.rz.at[k - 1], 4 + k, zs[k]).wait_send()


class Plane(Scatter):
    def __init__(self, k, *rest):
        Scatter.__init__(self, *rest)
        self.k = k

    def begin(self):
        me, fc, d1, d2, zs = self.where
        for a in (1, 0):
            for b in (1, 0):
                self.remote(self.grad.at[lax.rem(me, 8) + fc + a * d2 + b * d1], self.rp.at[a, b], a, fc).start()

    def pair(self, a):
        me, fc, d1, d2, zs = self.where
        self.remote(self.rp.at[a], self.rp.at[a], a, fc).wait_recv()
        for b in (1, 0):
            held = self.grad[lax.rem(me, 8) + a * d1 + b * d2]
            self.rp[a, b] = held + self.rp[a, b]
            if a == 1:
                self.remote(self.rp.at[1, b], self.r1.at[b], 2 + b, d1).start()

    def along(self):
        return self.remote(self.rp.at[0, 0], self.rz.at[self.k - 1], 4 + self.k, self.where[4][self.k])

    def second(self):
        self.remote(self.rp.at[0, 1], self.r2, 4, self.where[3]).wait_recv()
        if self.k:
            self.rp[0, 0] = self.rp[0, 0] + self.r2[...]
            self.along().start()

    def near(self):
        return self.rp[0, 0].astype(F32) + self.r2[...].astype(F32)

    def far(self):
        self.along().wait_recv()
        return self.rz[self.k - 1].astype(F32)

    def drain(self):
        me, fc, d1, d2, zs = self.where
        for b in (1, 0):
            self.remote(self.rp.at[1, b], self.r1.at[b], 2 + b, d1).wait_send()
        self.remote(self.rp.at[0, 1], self.r2, 4, d2).wait_send()
        if self.k:
            self.along().wait_send()


def scatter_buffers(lead, shape):
    return [pltpu.VMEM(lead + (2, 2, 4) + shape, BF), pltpu.VMEM(lead + (2, 4) + shape, BF),
            pltpu.VMEM(lead + (4,) + shape, BF), pltpu.VMEM(lead + (3,) + shape, BF)]


class Vectors:
    def __init__(self, where, held, got, sems):
        self.where, self.held, self.got, self.sems = where, held, got, sems

    def remote(self, src, slot, off):
        return pltpu.make_async_remote_copy(
            src_ref=self.held.at[src], dst_ref=self.got.at[slot], send_sem=self.sems.at[0, slot],
            recv_sem=self.sems.at[1, slot], device_id=(self.where[0] + off,), device_id_type=MESH_ID)

    def merge(self, a, b):
        row = lax.broadcasted_iota(jnp.int32, a.shape, 0)
        return jnp.where(row == TOP, jnp.maximum(a, b), a + b)

    def step(self, i):
        me, fc, d1, d2, zs = self.where
        offs = (fc, d1, d2)
        if i > 0:
            self.remote(i - 1, i - 1, offs[i - 1]).wait_recv()
            self.held[i] = self.merge(self.held[i - 1], self.got[i - 1])
        if i < 3:
            self.remote(i, i, offs[i]).start()
        else:
            for k in (1, 2, 3):
                self.remote(3, 2 + k, zs[k]).start()

    def last(self):
        me, fc, d1, d2, zs = self.where
        total = self.held[3]
        for k in (1, 2, 3):
            self.remote(3, 2 + k, zs[k]).wait_recv()
            total = self.merge(total, self.got[2 + k])
        for i, off in enumerate((fc, d1, d2)):
            self.remote(i, i, off).wait_send()
        for k in (1, 2, 3):
            self.remote(3, 2 + k, zs[k]).wait_send()
        return total


def rear_body(z_h, cot_h, wi_h, wu_h, x_h, wall_h, q_h, k_h, v_h, c_h, p_h, vecs, hm,
              out_h, dx_h, o_q, o_k, o_v, o_o, o_i, o_u, vout,
              wi, wu, ag, ds_s, dil_s, z, dx, fl, do, db, gu, gi, gg, held, got, usems, nsems, sems, vsems, isem, osem, *bufs):
    where = place()
    zi = where[0] // 8
    rows, d = z.shape
    ff = wi.shape[1]
    groups, n = gg.shape[0], gi.shape[1]
    rt, et = 512, 128
    k0, k1 = math.sqrt(2.0 / math.pi), 0.044715
    act, gp, small = ag.at[0], ag.at[1], held.at[0]
    row = lambda i: vecs[i:i + 1, :]
    part = lambda j: pl.ds(pl.multiple_of(j * d, d), d)
    beside = lambda k: (zi % 2 + k % 2 - 2 * (zi % 2) * (k % 2)) + 2 * (zi // 2 + k // 2 - 2 * (zi // 2) * (k // 2))

    def up_flow(it):
        k = (it + 1) % 4 if isinstance(it, int) else None
        return Plane(k, where, gu.at[lax.rem(it, 2)], bufs[0].at[it], bufs[1].at[it], bufs[2].at[it], bufs[3], usems.at[it])

    def in_flow(it):
        return Scatter(where, gi.at[lax.rem(it, 2)], *(b.at[it] for b in bufs[4:8]), nsems.at[it])

    small_flow = Vectors(where, held, got, vsems)
    out_flow = Scatter(where, gi.at[0], *bufs[8:12], sems.at[0])
    group_flow = [Scatter(where, gg.at[g], *bufs[12 + 4 * g:16 + 4 * g], sems.at[1 + g]) for g in range(groups)]

    def get_up(j):
        return pltpu.make_async_copy(wi_h.at[:, part(j)], wi.at[:, part(j)], isem.at[j])

    def get_down(j):
        return pltpu.make_async_copy(wu_h.at[part(j)], wu.at[part(j)], isem.at[4 + j])

    def get_wall(i):
        return pltpu.make_async_copy(wall_h.at[i], wi.at[:, pl.ds(i * d, d)], isem.at[i])

    def get_ctx(g):
        return pltpu.make_async_copy(c_h.at[g], fl.at[:, pl.ds(g * GW, GW)], isem.at[4 + g])

    get_z = pltpu.make_async_copy(z_h, z, isem.at[8])
    get_cot = pltpu.make_async_copy(cot_h, do, isem.at[9])
    get_x = pltpu.make_async_copy(x_h, do, isem.at[9])
    put_out = pltpu.make_async_copy(db, out_h, osem)
    put_dx = pltpu.make_async_copy(dx, dx_h, osem)
    mid_cols = pl.ds(0, GW // HD * SEQ)

    def get_group(g, i):
        cols = pl.ds(pl.multiple_of(g * GW, GW), GW)
        src = (v_h, q_h, k_h, p_h)[i].at[g]
        dst = wu.at[pl.ds((2, 0, 1)[i] * rows, rows), cols] if i < 3 else ag.at[lax.rem(g, 2), :, mid_cols]
        return pltpu.make_async_copy(src, dst, isem.at[10 + 4 * lax.rem(g, 2) + i])

    get_z.start()
    for j in range(ff // d):
        get_up(j).start()
        get_down(j).start()
    get_cot.start()
    greet(*where)
    small[...] = jnp.zeros(small.shape, F32)
    get_z.wait()

    def prep(i, _):
        r = pl.ds(pl.multiple_of(i * et, et), et)
        unit, _inv = unit_rows(z[r, :])
        first = unit * row(AG) + row(ASH)
        fl[r, :] = first.astype(BF)
        dx[r, :] = first + row(BO)
        return 0

    lax.fori_loop(0, rows // et, prep, 0)

    def up(j, _):
        c = part(j)
        get_up(j).wait()
        get_down(j).wait()
        for i in range(rows // rt):
            r = slice(i * rt, (i + 1) * rt)
            u = dot(fl[r, :], wi[:, c]) + vecs[pl.ds(BI + j, 1), :]
            u2 = u * u
            t = jnp.tanh(u * (k0 + (k0 * k1) * u2))
            h = 0.5 + 0.5 * t
            a = (u * h).astype(BF)
            act[r, c] = a
            gp[r, c] = (h + (0.5 * u) * (1.0 - t * t) * (k0 + (3.0 * k0 * k1) * u2)).astype(BF)
            dx[r, :] += dot(a, wu[c, :])
        return 0

    lax.fori_loop(0, ff // d, up, 0)
    get_cot.wait()

    def mid(i, _):
        r = pl.ds(pl.multiple_of(i * et, et), et)
        unit, inv = unit_rows(dx[r, :])
        db[r, :] = (unit * row(FG) + row(FS)).astype(BF)
        upv = do[r, :].astype(F32)
        small[FG:FG + 1, :] += col_sum(upv * unit)
        small[FS:FS + 1, :] += col_sum(upv)
        ds = norm_back(upv, unit, inv, row(FG))
        dsl = ds.astype(BF)
        do[r, :] = dsl
        dx[r, :] = ds
        small[BO:BO + 1, :] += col_sum(dsl.astype(F32))
        return 0

    lax.fori_loop(0, rows // et, mid, 0)
    put_out.start()
    meet()

    def down(it, _):
        j = beside((it + 1) % 4)
        c = part(j)
        slot = lax.rem(it, 2)

        @pl.when(it >= 2)
        def _():
            up_flow(it - 2).core_sent()

        gu[slot] = dot_tn(act[:, c], do[...]).astype(BF).reshape(gu.shape[1:])
        up_flow(it).begin()
        sums = None
        for i in range(rows // rt):
            r = slice(i * rt, (i + 1) * rt)
            di = dot_nt(do[r, :], wu[c, :]) * gp[r, c].astype(F32)
            dil = di.astype(BF)
            dil_s[r, :] = dil
            s = col_sum(dil.astype(F32))
            sums = s if sums is None else sums + s
            dx[r, :] += dot_nt(dil, wi[:, c])
            if i == 0:
                @pl.when(it >= 1)
                def _():
                    in_flow(it - 1).pair(1)
                    in_flow(it - 1).pair(0)
        small[pl.ds(BI + j, 1), :] = sums
        up_flow(it).pair(1)
        up_flow(it).pair(0)

        @pl.when(it >= 2)
        def _():
            in_flow(it - 2).core_sent()

        gi[slot] = dot_tn(fl[...], dil_s[...]).reshape(gi.shape[1:]).astype(BF)
        in_flow(it).begin()

        @pl.when(it >= 2)
        def _():
            for f in (up_flow(it - 2), in_flow(it - 2)):
                f.first(1)
                f.first(0)

        return 0

    lax.fori_loop(0, ff // d, down, 0)
    get_wall(3).start()
    for i in range(4):
        get_group(0, i).start()
    for g in range(groups):
        get_ctx(g).start()
    get_x.start()
    for i in range(3):
        get_wall(i).start()
    put_out.wait()

    def tail(i, _):
        r = pl.ds(pl.multiple_of(i * et, et), et)
        unit, inv = unit_rows(z[r, :])
        df = dx[r, :]
        small[AG:AG + 1, :] += col_sum(df * unit)
        small[ASH:ASH + 1, :] += col_sum(df)
        ds = norm_back(df, unit, inv, row(AG))
        dx[r, :] = ds
        dsl = ds.astype(BF)
        db[r, :] = dsl
        small[OB:OB + 1, :] += col_sum(dsl.astype(F32))
        return 0

    lax.fori_loop(0, rows // et, tail, 0)
    in_flow(3).pair(1)
    in_flow(3).pair(0)
    for g in range(groups):
        get_ctx(g).wait()
    in_flow(2).core_sent()
    gi[0] = dot_tn(fl[...], db[...]).reshape(gi.shape[1:]).astype(BF)
    out_flow.begin()
    get_wall(3).wait()

    steps = (rows // SEQ) * (GW // 128)
    edge = GW // HD * SEQ
    dc = act.at[:, pl.ds(edge, GW)]
    dp_s = [z.at[pl.ds(j * SEQ, SEQ), pl.ds(0, SEQ)] for j in range(2)]
    slopes = [ds_s.at[0], ds_s.at[1]]
    both = lambda f: [(f.first, 1), (f.first, 0)]
    g0, g1, g2 = group_flow
    events = {
        0: [(up_flow(0).second,), (in_flow(0).second,), (out_flow.pair, 1)],
        1: [(out_flow.pair, 0)] + both(up_flow(2)),
        2: both(in_flow(2)) + [(up_flow(1).second,)],
        3: [(in_flow(1).second,)],
        4: both(up_flow(3)),
        5: both(in_flow(3)) + [(g0.pair, 1)],
        6: [(g0.pair, 0), (up_flow(2).second,), (out_flow.first, 1)],
        7: [(out_flow.first, 0), (in_flow(2).second,)],
        8: [(up_flow(3).second,), (in_flow(3).second,), (g0.first, 1)],
        9: [(g0.first, 0), (g1.pair, 1)],
        10: [(g1.pair, 0), (out_flow.second,)],
        11: [(g0.second,), (g1.first, 1)],
    }

    def group(g, _):
        cols = pl.ds(pl.multiple_of(g * GW, GW), GW)
        for i in range(4):
            get_group(g, i).wait()

        @pl.when(g + 1 < groups)
        def _():
            for i in range(4):
                get_group(g + 1, i).start()

        dc[...] = dot_nt(db[...], wi[cols, 3 * d:4 * d]).astype(BF)
        heads = [wu.at[pl.ds(i * rows, rows), cols] for i in range(3)]

        def one_pair(it, _):
            pair_backward(it, *heads, ag.at[lax.rem(g, 2)], dc, *heads, dp_s, slopes)
            for when, todo in events.items():
                @pl.when(g * steps + it == when)
                def _():
                    for fn, *a in todo:
                        fn(*a)
            return 0

        lax.fori_loop(0, steps, one_pair, 0)

        @pl.when(g == 0)
        def _():
            get_x.wait()

        xv = do[...]
        for i, grad in enumerate(heads):
            gg[g, i] = dot_tn(xv, grad[...]).reshape(n, d // n, GW).astype(BF)
        for i in range(groups):
            @pl.when(g == i)
            def _():
                group_flow[i].begin()
        small[QB:QB + 1, cols] = col_sum(heads[0][...].astype(F32))
        small[VB:VB + 1, cols] = col_sum(heads[2][...].astype(F32))
        return 0

    lax.fori_loop(0, groups, group, 0)
    diag = lax.broadcasted_iota(jnp.int32, hm.shape, 0) == lax.broadcasted_iota(jnp.int32, hm.shape, 1)
    small[TOP:TOP + 1, 0:128] = jnp.sum(jnp.where(diag, hm[...], 0.0), axis=0, keepdims=True)
    small_flow.step(0)
    for i in range(3):
        get_wall(i).wait()
    quarter = rows // 4

    def inputs_part(t):
        grads = (wu[i * rows + t * quarter:i * rows + (t + 1) * quarter, :] for i in range(3))
        dx[t * quarter:(t + 1) * quarter, :] += sum(dot_nt(v, wi[:, i * d:(i + 1) * d]) for i, v in enumerate(grads))

    inputs_part(0)
    g2.pair(1)
    g2.pair(0)
    small_flow.step(1)
    inputs_part(1)
    g1.first(0)
    inputs_part(2)
    small_flow.step(2)
    g2.first(1)
    g1.second()
    g2.first(0)
    inputs_part(3)
    put_dx.start()
    small_flow.step(3)
    o_u[...] = up_flow(3).near() + up_flow(0).far() + up_flow(1).far() + up_flow(2).far()
    g2.second()
    for it in range(4):
        k = (it + 1) % 4
        total = in_flow(it).near()
        for m in (1, 2, 3):
            total = total + in_flow(((k ^ m) - 1) % 4).far(m)
        o_i[:, part(beside(k))] = total
    o_o[...] = out_flow.last()
    for g, f in enumerate(group_flow):
        t = f.last()
        for i, o in enumerate((o_q, o_k, o_v)):
            o[:, g * GW:(g + 1) * GW] = t[i]
    vout[...] = small_flow.last()
    put_dx.wait()
    up_flow(2).core_sent()
    up_flow(3).core_sent()
    in_flow(3).core_sent()
    for f in [out_flow] + group_flow:
        f.core_sent()
    for f in [up_flow(i) for i in range(4)] + [in_flow(i) for i in range(4)] + [out_flow] + group_flow:
        f.drain()


def rear(n, z, cot, wi, wu, x, wall, q, k, v, c, p, vecs, hm):
    rows, d = x.shape
    ff = wi.shape[1]
    groups = d // GW
    r, ru = d // n, ff // n
    sd = jax.ShapeDtypeStruct
    vm, hbm = pl.BlockSpec(memory_space=pltpu.VMEM), pl.BlockSpec(memory_space=pl.ANY)
    flat = pltpu.VMEM((rows, d), BF)
    bufs = [pltpu.VMEM((4, 2, 2, ru, d), BF), pltpu.VMEM((4, 2, ru, d), BF), pltpu.VMEM((4, ru, d), BF),
            pltpu.VMEM((3, ru, d), BF)]
    bufs += scatter_buffers((4,), (r, d)) + scatter_buffers((), (r, d))
    for _ in range(groups):
        bufs += scatter_buffers((), (3, r, GW))
    return pl.pallas_call(
        rear_body,
        in_specs=[hbm] * 11 + [vm] * 2,
        out_specs=[hbm] * 2 + [vm] * 7,
        out_shape=[sd((rows, d), BF), sd((rows, d), F32)] + [sd((r, d), F32)] * 4
        + [sd((r, ff), F32), sd((ru, d), F32), sd((16, d), F32)],
        scratch_shapes=[pltpu.VMEM((d, ff), BF), pltpu.VMEM((ff, d), BF), pltpu.VMEM((2, rows, ff), BF), pltpu.VMEM((2, SEQ, SEQ), BF), flat,
                        pltpu.VMEM((rows, d), F32), pltpu.VMEM((rows, d), F32), flat, flat, flat,
                        pltpu.VMEM((2, 8, ru, d), BF),
                        pltpu.VMEM((2, n, r, d), BF), pltpu.VMEM((groups, 3, n, r, GW), BF),
                        pltpu.VMEM((4, 16, d), F32), pltpu.VMEM((6, 16, d), F32),
                        pltpu.SemaphoreType.DMA((4, 2, 8)), pltpu.SemaphoreType.DMA((4, 2, 8)),
                        pltpu.SemaphoreType.DMA((1 + groups, 2, 8)), pltpu.SemaphoreType.DMA((2, 6)),
                        pltpu.SemaphoreType.DMA((18,)), pltpu.SemaphoreType.DMA] + bufs,
        compiler_params=pltpu.CompilerParams(collective_id=1, has_side_effects=True, vmem_limit_bytes=VMEM_MAX),
        name="rear",
    )(z, cot, wi, wu, x, wall, q, k, v, c, p, vecs, hm)


def attn_fwd_body(rb, x, segr, segc, wq, wk, wv, wo, vecs, q, k, v, p, c, z, hm, bias, s_s):
    g = pl.program_id(0)

    @pl.when(g == 0)
    def _():
        same_document(lambda s: segr[s:s + 1, :], lambda s, c: segc[s * SEQ + c * BLOCK:s * SEQ + (c + 1) * BLOCK, :], bias)
        hm[...] = jnp.full(hm.shape, LOW, F32)
        z[...] = x[...].astype(F32) + vecs[OB:OB + 1, :]

    cols = pl.ds(pl.multiple_of(g * GW, GW), GW)
    xv = x[...]
    q[...] = (dot(xv, wq[...]) + vecs[QB:QB + 1, cols]).astype(BF)
    k[...] = dot(xv, wk[...]).astype(BF)
    v[...] = (dot(xv, wv[...]) + vecs[VB:VB + 1, cols]).astype(BF)

    def one_pair(it, _):
        pair_forward(g, it, lambda h, i: rb[h * 18 + i * 3] + rb[h * 18 + i * 3 + 1] + rb[h * 18 + i * 3 + 2], q, k, v, p, c, hm, bias, s_s)
        return 0

    lax.fori_loop(0, x.shape[0] // SEQ * (GW // 128), one_pair, 0)
    z[...] += dot(c[...], wo[...])


def attn_fwd(rb, x, segr, segc, wall, vecs):
    rows, d = x.shape
    groups, seqs = d // GW, rows // SEQ
    keys = GW // HD * SEQ
    full = lambda shape: pl.BlockSpec(shape, lambda g, *_: (0,) * len(shape))
    col = lambda i: pl.BlockSpec((None, d, GW), lambda g, *_: (i, 0, g))
    act = pl.BlockSpec((None, rows, GW), lambda g, *_: (g, 0, 0))
    sd = jax.ShapeDtypeStruct
    return pl.pallas_call(
        attn_fwd_body,
        grid_spec=pltpu.PrefetchScalarGridSpec(
            num_scalar_prefetch=1, grid=(groups,),
            in_specs=[full((rows, d)), full((seqs, SEQ)), full((rows, 1)), col(0), col(1), col(2),
                      pl.BlockSpec((None, GW, d), lambda g, *_: (3, g, 0)), full((16, d))],
            out_specs=[act, act, act, pl.BlockSpec((None, rows, keys), lambda g, *_: (g, 0, 0)), act,
                       full((rows, d)), full((16, 128))],
            scratch_shapes=[pltpu.VMEM((seqs, SEQ, SEQ), F32), pltpu.VMEM((2, SEQ, SEQ), F32)]),
        out_shape=[sd((groups, rows, GW), BF)] * 3
        + [sd((groups, rows, keys), BF), sd((groups, rows, GW), BF), sd((rows, d), F32), sd((16, 128), F32)],
        compiler_params=pltpu.CompilerParams(vmem_limit_bytes=VMEM_MAX),
        name="attn_fwd",
    )(rb, x, segr, segc, wall, wall, wall, wall, vecs)


def attn_bwd_body(x, db, wq, wk, wv, wo, q, k, v, p, c, dsum, dw, dqb, dvb, dx, dc, dq, dk, dv, dp_s, ds_s):
    g = pl.program_id(0)

    @pl.when(g == 0)
    def _():
        dx[...] = dsum[...]

    dbv = db[...]
    cols = pl.ds(pl.multiple_of(g * GW, GW), GW)
    dc[...] = dot_nt(dbv, wo[...]).astype(BF)
    dw[3, cols, :] = dot_tn(c[...], dbv).astype(dw.dtype)

    def one_pair(it, _):
        pair_backward(it, q, k, v, p, dc, dq, dk, dv, [dp_s.at[0], dp_s.at[1]], [ds_s.at[0], ds_s.at[1]])
        return 0

    lax.fori_loop(0, x.shape[0] // SEQ * (GW // 128), one_pair, 0)
    dqb[...] = col_sum(dq[...].astype(F32))
    dvb[...] = col_sum(dv[...].astype(F32))
    xv = x[...]
    for i, part in enumerate((dq, dk, dv)):
        dw[i, :, cols] = dot_tn(xv, part[...]).astype(dw.dtype)
    dx[...] += dot_nt(dq[...], wq[...]) + dot_nt(dk[...], wk[...]) + dot_nt(dv[...], wv[...])


def attn_bwd(x, db, wall, q, k, v, p, c, dsum, gdt):
    rows, d = x.shape
    groups = d // GW
    keys = GW // HD * SEQ
    full = lambda shape: pl.BlockSpec(shape, lambda g: (0,) * len(shape), pipeline_mode=pl.Buffered(1))
    col = lambda i: pl.BlockSpec((None, d, GW), lambda g: (i, 0, g))
    vec = pl.BlockSpec((1, GW), lambda g: (0, g))
    act = pl.BlockSpec((None, rows, GW), lambda g: (g, 0, 0))
    sd = jax.ShapeDtypeStruct
    return pl.pallas_call(
        attn_bwd_body,
        grid=(groups,),
        in_specs=[full((rows, d)), full((rows, d)), col(0), col(1), col(2),
                  pl.BlockSpec((None, GW, d), lambda g: (3, g, 0)), act, act, act,
                  pl.BlockSpec((None, rows, keys), lambda g: (g, 0, 0)), act, full((rows, d))],
        out_specs=[full((4, d, d)), vec, vec, full((rows, d))],
        out_shape=[sd((4, d, d), gdt)] + [sd((1, d), F32)] * 2 + [sd((rows, d), F32)],
        scratch_shapes=[pltpu.VMEM((rows, GW), BF)] * 4
        + [pltpu.VMEM((2, SEQ, SEQ), F32), pltpu.VMEM((2, SEQ, SEQ), BF)],
        compiler_params=pltpu.CompilerParams(vmem_limit_bytes=VMEM_MAX),
        name="attn_bwd",
    )(x, db, wall, wall, wall, wall, q, k, v, p, c, dsum)


def far_layer(me, n, random_blocks, tokens, segment_ids, cot, weights, vecs, inner_weight, inner_bias, outer_weight, limit):
    d, ff = tokens.shape[1], inner_weight.shape[1]
    heads, part, wide = random_blocks.shape[0], vecs[0].shape[0], inner_bias.shape[0]
    wall = lax.all_gather(jnp.stack(weights), "dp", axis=1, tiled=True)
    wi, wu = (lax.all_gather(a, "dp", axis=0, tiled=True) for a in (inner_weight, outer_weight))
    vecs = lax.psum(vectors_part(me, n, vecs, inner_bias).astype(F32), "dp")
    q, k, v, p, c, z, hm = attn_fwd(random_blocks.reshape(-1), tokens, segment_ids.reshape(-1, SEQ),
                                    segment_ids.reshape(-1, 1), wall, vecs)
    out, dsum, db, dwi, dwu, small = ffn(z, cot, wi, wu, vecs, F32)
    dwall, dqb, dvb, dx = attn_bwd(tokens, db, wall, q, k, v, p, c, dsum, F32)
    mine = small.at[QB:QB + 1].set(dqb).at[VB:VB + 1].set(dvb).at[TOP, :hm.shape[0]].set(hm[:, 0])
    scatter = lambda a, at: lax.psum_scatter(a, "dp", scatter_dimension=at, tiled=True)
    dwu, dwi, dwall = scatter(dwu, 0), scatter(dwi, 0), scatter(dwall, 1)
    row = lax.broadcasted_iota(jnp.int32, mine.shape, 0)
    total = jnp.where(row == TOP, lax.pmax(mine, "dp"), lax.psum(mine, "dp"))
    vec8 = lax.dynamic_slice(total, (0, me * part), (8, part))
    dbi = lax.dynamic_slice(total[BI:BI + ff // d].reshape(-1), (me * wide,), (wide,))
    head_maxima = total[TOP, :heads]
    factor = jnp.sqrt(jnp.minimum(1.0, limit[0].astype(F32) / jnp.maximum(head_maxima, 1.0)))
    columns = jnp.repeat(factor, HD)[None, :]
    cq, ck = ((w.astype(F32) * columns).astype(BF) for w in weights[:2])
    return out, dx, dwall[0], dwall[1], dwall[2], dwall[3], dwi, dwu, [vec8[i] for i in range(8)], dbi, cq, ck, head_maxima


def near_layer(me, n, random_blocks, tokens, segment_ids, cot, weights, vecs, inner_weight, inner_bias, outer_weight, limit):
    d, ff = tokens.shape[1], inner_weight.shape[1]
    heads, part, wide = random_blocks.shape[0], vecs[0].shape[0], inner_bias.shape[0]
    pieces = jnp.concatenate([jnp.pad(jnp.stack(vecs), ((0, 0), (0, 128 - part))),
                              jnp.pad(inner_bias[None, :], ((0, 7), (0, 128 - wide)))]).astype(F32)
    wall, wi, wu, vec, q, k, v, p, c, z, hm = front(random_blocks, tokens, segment_ids.reshape(-1, 128), *weights, pieces,
                                                    inner_weight, outer_weight, n)
    raw = rear(n, z, cot, wi.reshape(d, ff), wu.reshape(ff, d), tokens, wall.reshape(4, d, d), q, k, v, c, p, vec, hm)
    out, dx, dwq, dwk, dwv, dwo, dwi, dwu, cq, ck, *fins = finish(n, heads, limit, weights[0], weights[1], *raw)
    fins = [a.reshape(-1) for a in fins]
    return out, dx, dwq, dwk, dwv, dwo, dwi, dwu, fins[:8], fins[8], cq, ck, fins[9]


def finish_body(n, heads, limit, wq, wk, total, *refs):
    count = 8
    srcs, dsts, refs = refs[:count], refs[count:2 * count], refs[2 * count:]
    (cq, ck), fins, held, sems = refs[:2], refs[2:12], refs[12:-1], refs[-1]
    jobs = []
    for src, dst, tmp in zip(srcs, dsts, held):
        cut = 4 if src.shape[0] >= 512 else 1
        step = src.shape[0] // cut
        for i in range(cut):
            at = pl.ds(i * step, step)
            slot = len(jobs)
            jobs.append((pltpu.make_async_copy(src.at[at], tmp.at[at], sems.at[0, slot]),
                         pltpu.make_async_copy(tmp.at[at], dst.at[at], sems.at[1, slot])))
    for get, _ in jobs:
        get.start()
    me = lax.axis_index("dp")
    d = total.shape[1]
    part, wide = d // n, held[7].shape[0]
    top = total[TOP:TOP + 1, 0:128]
    head = lax.broadcasted_iota(jnp.int32, (1, d), 1) // HD
    columns = jnp.zeros((1, d), F32)
    for h in range(heads):
        columns = jnp.where(head == h, top[:, h:h + 1], columns)
    factor = jnp.sqrt(jnp.minimum(1.0, limit[0].astype(F32) / jnp.maximum(columns, 1.0)))
    cq[...] = (wq[...].astype(F32) * factor).astype(BF)
    ck[...] = (wk[...].astype(F32) * factor).astype(BF)
    mine = pltpu.roll(total[0:8, :], d - me * part, 1)
    for i in range(8):
        fins[i][...] = mine[i:i + 1, 0:part]
    per = d // wide
    inner = jnp.broadcast_to(total[pl.ds(BI + me // per, 1), :], (8, d))
    fins[8][...] = pltpu.roll(inner, d - (me % per) * wide, 1)[0:1, 0:wide]
    fins[9][...] = top[:, 0:heads]
    for get, put in jobs:
        get.wait()
        put.start()
    for _, put in jobs:
        put.wait()


def finish(n, heads, limit, wq, wk, *raw):
    mats, total = raw[:8], raw[8]
    vm, hbm = pl.BlockSpec(memory_space=pltpu.VMEM), pl.BlockSpec(memory_space=pl.ANY)
    sd = jax.ShapeDtypeStruct
    return pl.pallas_call(
        partial(finish_body, n, heads),
        in_specs=[pl.BlockSpec(memory_space=pltpu.SMEM)] + [vm] * 3 + [hbm] * 8,
        out_specs=[hbm] * 8 + [vm] * 12,
        out_shape=[sd(a.shape, a.dtype) for a in mats] + [sd(wq.shape, BF)] * 2 + [sd((1, mats[2].shape[0]), F32)] * 8
        + [sd((1, mats[7].shape[0]), F32), sd((1, heads), F32)],
        scratch_shapes=[pltpu.VMEM(a.shape, a.dtype) for a in mats] + [pltpu.SemaphoreType.DMA((2, 16))],
        compiler_params=pltpu.CompilerParams(vmem_limit_bytes=VMEM_MAX),
        name="finish",
    )(limit, wq, wk, total, *mats)


def vectors_part(me, n, vecs, inner_bias):
    part = vecs[0].shape[0]
    d = part * n
    rows = jnp.tile(jnp.stack(vecs), (1, n))
    rows = jnp.where(lax.broadcasted_iota(jnp.int32, rows.shape, 1) // part == me, rows, 0)
    flat = jnp.tile(inner_bias, n)
    flat = jnp.where(lax.broadcasted_iota(jnp.int32, flat.shape, 0) // inner_bias.shape[0] == me, flat, 0)
    flat = flat.reshape(-1, d)
    rest = jnp.zeros((16 - rows.shape[0] - flat.shape[0], d), BF)
    return jnp.concatenate([rows, flat, rest], axis=0)


def per_device(n, tokens, segment_ids, random_blocks, clip_limit, query_weight, query_bias, key_weight, value_weight,
               value_bias, output_weight, output_bias, attn_gain, attn_shift, inner_weight, inner_bias,
               outer_weight, outer_bias, final_gain, final_shift, out_cotangent):
    rows, d = tokens.shape
    near = n == 32 and (rows, d, inner_weight.shape[1]) == (2 * SEQ, 3 * GW, 6 * SEQ)
    weights = (query_weight, key_weight, value_weight, output_weight)
    vecs = (query_bias, value_bias, output_bias, attn_gain, attn_shift, outer_bias, final_gain, final_shift)
    out, dx, dwq, dwk, dwv, dwo, dwi, dwu, vec8, dbi, cq, ck, head_maxima = (near_layer if near else far_layer)(
        lax.axis_index("dp"), n, random_blocks, tokens, segment_ids, out_cotangent, weights, vecs, inner_weight, inner_bias,
        outer_weight, clip_limit)
    dqb, dvb, dob, dag, dash, dbo, dfg, dfs = vec8
    return (out, dx, dwq, dqb, dwk, dwv, dvb, dwo, dob, dag, dash, dwi, dbi, dwu, dbo, dfg, dfs, cq, ck, head_maxima)


def solution(mesh):
    mat, vec, rep = P("dp", None), P("dp"), P()
    in_specs = (mat, vec, rep, rep, mat, vec, mat, mat, vec, mat, vec, vec, vec, mat, vec, mat, vec, vec, vec, mat)
    out_specs = (mat, mat, mat, vec, mat, mat, vec, mat, vec, vec, vec, mat, vec, mat, vec, vec, vec, mat, mat, rep)
    return jax.shard_map(partial(per_device, mesh.shape["dp"]), mesh=mesh, in_specs=in_specs, out_specs=out_specs,
                         check_vma=False)
```

```python
from functools import partial
import math

import jax
import jax.numpy as jnp
from jax import lax
from jax.experimental import pallas as pl
from jax.experimental.pallas import tpu as pltpu
from jax.sharding import PartitionSpec as P

HD = 64
BLOCK = 64
SEQ = 512
GW = 256
BF = jnp.bfloat16
F32 = jnp.float32
LOW = -1e30
VMEM_MAX = 67043328
MESH_ID = pl.DeviceIdType.MESH
QB, VB, OB, AG, ASH, BO, FG, FS, BI, TOP = 0, 1, 2, 3, 4, 5, 6, 7, 8, 12


def dot(a, b):
    return jnp.dot(a, b, preferred_element_type=F32)


def dot_nt(a, b):
    return lax.dot_general(a, b, (((1,), (1,)), ((), ())), preferred_element_type=F32)


def dot_tn(a, b):
    return lax.dot_general(a, b, (((0,), (0,)), ((), ())), preferred_element_type=F32)


def col_sum(v):
    return jnp.sum(v, axis=0, keepdims=True)


def first_half():
    return lax.broadcasted_iota(jnp.int32, (1, 128), 1) < HD


def same_document(key_ids, query_ids, bias):
    for s in range(bias.shape[0]):
        kseg = key_ids(s)
        for c in range(SEQ // BLOCK):
            bias[s, c * BLOCK:(c + 1) * BLOCK, :] = jnp.where((query_ids(s, c) == kseg) & (kseg != 0), 0.0, LOW)


def same_document_flat(seg, bias):
    ids = seg[...].astype(F32)
    turned = jnp.transpose(ids)
    per = SEQ // 128
    key_ids = lambda s: jnp.concatenate([ids[s * per + i:s * per + i + 1, :] for i in range(per)], axis=1)

    def query_ids(s, c):
        i, r = s * per + c * BLOCK // 128, c * BLOCK % 128
        return turned[r:r + BLOCK, i:i + 1]

    same_document(key_ids, query_ids, bias)


def whole_vectors(pieces, vec, wide):
    n, d = pieces.shape[0], vec.shape[1]
    lane = lax.broadcasted_iota(jnp.int32, (1, 128), 1)

    def spread(values, width):
        tiles = [0.0] * (d // 128)
        for i, value in enumerate(values):
            t, at = i * width // 128, i * width % 128
            moved = pltpu.roll(value, at, 1) if at else value
            tiles[t] = tiles[t] + (jnp.where(lane >= at, moved, 0.0) if at + width > 128 else moved)
            if at + width > 128:
                tiles[t + 1] = tiles[t + 1] + jnp.where(lane < at, moved, 0.0)
        return jnp.concatenate(tiles, axis=1)

    vec[0:8, :] = spread([pieces[u, 0:8, :] for u in range(n)], d // n)
    per = d // wide
    inner = [spread([pieces[j * per + i, 8:16, :] for i in range(per)], wide) for j in range(n // per)]
    for j, v in enumerate(inner):
        vec[8 + j:9 + j, :] = v[0:1, :]
    vec[8 + len(inner):16, :] = jnp.zeros((8 - len(inner), d), F32)


def pair_forward(g, it, rb, q, k, v, p, ctx, hm, bias, s_s):
    pairs = GW // 128
    s, pair = it // pairs, it % pairs
    rows = pl.ds(pl.multiple_of(s * SEQ, SEQ), SEQ)
    lanes = pl.ds(pl.multiple_of(pair * 128, 128), 128)
    lane_block = lax.broadcasted_iota(jnp.int32, (1, SEQ), 1) // BLOCK
    half = first_half()
    last = SEQ // BLOCK - 2
    qp, kp, vp = q[rows, lanes], k[rows, lanes], v[rows, lanes]
    outs = []
    for j in range(2):
        head = g * (2 * pairs) + pair * 2 + j
        keys = pl.ds(pl.multiple_of((pair * 2 + j) * SEQ, SEQ), SEQ)
        mine = half if j == 0 else jnp.logical_not(half)
        s_s[j] = dot_nt(jnp.where(mine, qp * 0.125, 0).astype(BF), kp)
        miss1, miss6 = 18 - rb(head, 0), 10 - rb(head, 5)
        skip1 = jnp.where(lane_block == miss1, LOW, 0.0)
        skip6 = jnp.where(lane_block == miss6, LOW, 0.0)
        tops = None
        for c in range(SEQ // BLOCK):
            cr = slice(c * BLOCK, (c + 1) * BLOCK)
            sv = s_s[j, cr, :] + bias[s, cr, :]
            if c == 1:
                sv = sv + skip1
            if c == last:
                sv = sv + skip6
            top = jnp.max(sv, axis=1, keepdims=True)
            live = top > -1e29
            e = jnp.exp(sv - jnp.where(live, top, 0.0))
            total = jnp.sum(e, axis=1, keepdims=True) + jnp.where(live, 0.0, 1.0)
            p[pl.ds(pl.multiple_of(s * SEQ + c * BLOCK, BLOCK), BLOCK), keys] = (e * (1.0 / total)).astype(BF)
            tops = top if tops is None else jnp.maximum(tops, top)
        top = jnp.max(tops, axis=0, keepdims=True)
        hm[pl.ds(head, 1), :] = jnp.maximum(hm[pl.ds(head, 1), :], top)
        outs.append(dot(p[rows, keys], vp))
    ctx[rows, lanes] = jnp.where(half, outs[0], outs[1]).astype(BF)


def pair_backward(it, q, k, v, p, dc, dq, dk, dv, dp_s, ds_s):
    pairs = GW // 128
    s, pair = it // pairs, it % pairs
    rows = pl.ds(pl.multiple_of(s * SEQ, SEQ), SEQ)
    lanes = pl.ds(pl.multiple_of(pair * 128, 128), 128)
    half = first_half()
    qp, kp, vp, dcp = q[rows, lanes], k[rows, lanes], v[rows, lanes], dc[rows, lanes]
    dqs, dks, dvs = [], [], []
    for j in range(2):
        mine = half if j == 0 else jnp.logical_not(half)
        keys = pl.ds(pl.multiple_of((pair * 2 + j) * SEQ, SEQ), SEQ)
        dp_s[j][...] = dot_nt(jnp.where(mine, dcp, 0).astype(BF), vp)
        for c in range(SEQ // BLOCK):
            cr = slice(c * BLOCK, (c + 1) * BLOCK)
            pv = p[pl.ds(pl.multiple_of(s * SEQ + c * BLOCK, BLOCK), BLOCK), keys].astype(F32)
            sl = dp_s[j][cr, :]
            mean = jnp.sum(pv * sl, axis=1, keepdims=True)
            ds_s[j][cr, :] = (pv * (sl - mean)).astype(BF)
        dqs.append(dot(ds_s[j][...], kp))
        dks.append(dot_tn(ds_s[j][...], qp))
        dvs.append(dot_tn(p[rows, keys], dcp))
    dq[rows, lanes] = (jnp.where(half, dqs[0], dqs[1]) * 0.125).astype(BF)
    dk[rows, lanes] = (jnp.where(half, dks[0], dks[1]) * 0.125).astype(BF)
    dv[rows, lanes] = jnp.where(half, dvs[0], dvs[1]).astype(BF)


def unit_rows(z):
    mean = jnp.mean(z, axis=-1, keepdims=True)
    c = z - mean
    inv = lax.rsqrt(jnp.mean(c * c, axis=-1, keepdims=True) + 1e-12)
    return c * inv, inv


def norm_back(up, unit, inv, gain):
    e = up * gain
    spread = jnp.mean(e, axis=-1, keepdims=True)
    along = jnp.mean(e * unit, axis=-1, keepdims=True)
    return inv * (e - spread - unit * along)


def ffn_body(z, cot, wi, wo, vecs, out, dsum, db, dwi, dwo, small, fl, act, gp, acc, do):
    rows, d = z.shape
    ff = wi.shape[1]
    rt, et = 512, 128
    k0, k1 = math.sqrt(2.0 / math.pi), 0.044715
    row = lambda i: vecs[i:i + 1, :]
    small[...] = jnp.zeros(small.shape, F32)

    def prep(i, _):
        r = pl.ds(pl.multiple_of(i * et, et), et)
        unit, _inv = unit_rows(z[r, :])
        first = unit * row(AG) + row(ASH)
        fl[r, :] = first.astype(BF)
        acc[r, :] = first + row(BO)
        return 0

    lax.fori_loop(0, rows // et, prep, 0)

    def up(i, _):
        j = i // (rows // rt)
        r = pl.ds(pl.multiple_of((i % (rows // rt)) * rt, rt), rt)
        c = pl.ds(pl.multiple_of(j * d, d), d)
        u = dot(fl[r, :], wi[:, c]) + vecs[pl.ds(BI + j, 1), :]
        u2 = u * u
        t = jnp.tanh(u * (k0 + (k0 * k1) * u2))
        h = 0.5 + 0.5 * t
        a = (u * h).astype(BF)
        act[r, c] = a
        gp[r, c] = (h + (0.5 * u) * (1.0 - t * t) * (k0 + (3.0 * k0 * k1) * u2)).astype(gp.dtype)
        acc[r, :] += dot(a, wo[c, :])
        return 0

    lax.fori_loop(0, (ff // d) * (rows // rt), up, 0)

    def mid(i, _):
        r = pl.ds(pl.multiple_of(i * et, et), et)
        unit, inv = unit_rows(acc[r, :])
        out[r, :] = (unit * row(FG) + row(FS)).astype(BF)
        upv = cot[r, :].astype(F32)
        small[FG:FG + 1, :] += col_sum(upv * unit)
        small[FS:FS + 1, :] += col_sum(upv)
        ds = norm_back(upv, unit, inv, row(FG))
        dsl = ds.astype(BF)
        do[r, :] = dsl
        acc[r, :] = ds
        small[BO:BO + 1, :] += col_sum(dsl.astype(F32))
        return 0

    lax.fori_loop(0, rows // et, mid, 0)

    def down(j, _):
        c = pl.ds(pl.multiple_of(j * d, d), d)
        dwo[c, :] = dot_tn(act[:, c], do[...]).astype(dwo.dtype)
        sums = None
        for i in range(rows // rt):
            r = slice(i * rt, (i + 1) * rt)
            di = dot_nt(do[r, :], wo[c, :]) * gp[r, c].astype(F32)
            dil = di.astype(BF)
            act[r, c] = dil
            s = col_sum(dil.astype(F32))
            sums = s if sums is None else sums + s
            acc[r, :] += dot_nt(dil, wi[:, c])
        small[pl.ds(BI + j, 1), :] = sums
        dwi[:, c] = dot_tn(fl[...], act[:, c]).astype(dwi.dtype)
        return 0

    lax.fori_loop(0, ff // d, down, 0)

    def tail(i, _):
        r = pl.ds(pl.multiple_of(i * et, et), et)
        unit, inv = unit_rows(z[r, :])
        df = acc[r, :]
        small[AG:AG + 1, :] += col_sum(df * unit)
        small[ASH:ASH + 1, :] += col_sum(df)
        ds = norm_back(df, unit, inv, row(AG))
        dsum[r, :] = ds
        dsl = ds.astype(BF)
        db[r, :] = dsl
        small[OB:OB + 1, :] += col_sum(dsl.astype(F32))
        return 0

    lax.fori_loop(0, rows // et, tail, 0)


def ffn(z, cot, wi, wo, vecs, gdt):
    rows, d = z.shape
    ff = wi.shape[1]
    sd = jax.ShapeDtypeStruct
    vm = pl.BlockSpec(memory_space=pltpu.VMEM)
    return pl.pallas_call(
        ffn_body,
        in_specs=[vm] * 5,
        out_specs=[vm] * 6,
        out_shape=[sd((rows, d), BF), sd((rows, d), F32), sd((rows, d), BF), sd((d, ff), gdt), sd((ff, d), gdt),
                   sd((16, d), F32)],
        scratch_shapes=[pltpu.VMEM((rows, d), BF), pltpu.VMEM((rows, ff), BF), pltpu.VMEM((rows, ff), BF),
                        pltpu.VMEM((rows, d), F32), pltpu.VMEM((rows, d), BF)],
        compiler_params=pltpu.CompilerParams(vmem_limit_bytes=VMEM_MAX),
        name="ffn",
    )(z, cot, wi, wo, vecs)


def place():
    me = lax.axis_index("dp")
    c, x, y, z = me % 2, (me // 2) % 2, (me // 4) % 2, me // 8
    fc, fx, fy = 1 - 2 * c, 2 * (1 - 2 * x), 4 * (1 - 2 * y)
    d1 = fx * (1 - c) + fy * c
    d2 = fy * (1 - c) + fx * c
    zs = (0, 8 * (1 - 2 * (z % 2)), 16 * (1 - 2 * (z // 2)), 8 * (3 - 2 * z))
    return me, fc, d1, d2, zs


def greet(me, fc, d1, d2, zs):
    for off in (fc, d1, d2) + zs[1:]:
        pl.semaphore_signal(pltpu.get_barrier_semaphore(), inc=1, device_id=(me + off,), device_id_type=MESH_ID)


def meet():
    pl.semaphore_wait(pltpu.get_barrier_semaphore(), 6)


def unit_of(ref, unit):
    return ref.at[:, unit] if len(ref.shape) == 4 else ref.at[unit]


class Gather:
    ORDER = (1, 4, 2, 5, 8, 3, 6, 9, 7, 12, 10, 13, 11, 14, 15)

    def __init__(self, where, own, out, send, recv):
        self.where, self.own, self.out, self.send, self.recv = where, own, out, send, recv

    def copy(self, slot, unit, dest, own=False):
        return pltpu.make_async_remote_copy(
            src_ref=self.own if own else unit_of(self.out, unit), dst_ref=unit_of(self.out, unit),
            send_sem=self.send.at[slot], recv_sem=self.recv.at[slot], device_id=(dest,), device_id_type=MESH_ID)

    def begin_z(self):
        me, fc, d1, d2, zs = self.where
        for k in (1, 2, 3):
            self.copy(k, me, me + zs[k], True).start()

    def begin_xy(self):
        me, fc, d1, d2, zs = self.where
        self.copy(4, me, me + d1, True).start()
        self.copy(8, me, me + d2, True).start()
        self.copy(16, me, me + fc, True).start()

    def landed(self, slot):
        me, fc, d1, d2, zs = self.where
        unit = me + zs[slot % 4] + (0, d1, d2, d1 + d2, fc, fc + d2, fc + d1, fc + d1 + d2)[slot // 4]
        self.copy(slot, unit, me).wait_recv()
        return unit

    def step(self, slot):
        me, fc, d1, d2, zs = self.where
        k, group = slot % 4, slot // 4
        unit = self.landed(slot)
        if group == 0:
            self.copy(4 + k, unit, me + d1).start()
            self.copy(8 + k, unit, me + d2).start()
        if group == 1:
            self.copy(12 + k, unit, me + d2).start()
        self.copy(16 + slot, unit, me + fc).start()

    def finish(self):
        for slot in range(16, 32):
            self.landed(slot)

    def drain(self):
        me = self.where[0]
        for slot in range(1, 32):
            self.copy(slot, me, me, slot in (1, 2, 3, 4, 8, 16)).wait_send()


LATE = ((1, 0), (4, 1), (2, 2), (5, 3), (8, 4), (3, 5), (6, 6), (9, 7), (7, 8), (12, 9), (10, 10), (13, 11))


def front_body(rb, x, seg, wq, wk, wv, wo, vpart, wis, wus,
               wall_o, wi_o, wu_o, vec_o, q_o, k_o, v_o, p_o, c_o, z_o, hm_o,
               wall, vg, bias, s_s, q_s, k_s, v_s, p_s, c_s, send, recv, local, outs):
    where = place()
    me = where[0]
    rows, d = x.shape
    groups = d // GW
    steps = (rows // SEQ) * (GW // 128)
    owns, targets = (wall.at[:, me], vpart, wis, wus), (wall, vg, wi_o, wu_o)
    mine = [pltpu.make_async_copy(o, unit_of(t, me), local.at[i]) for i, (o, t) in enumerate(zip(owns[1:], targets[1:]))]
    four = [pltpu.make_async_copy(w, wall.at[i, me], local.at[3 + i]) for i, w in enumerate((wq, wk, wv, wo))]
    for m in four + mine:
        m.start()
    greet(*where)
    for m in four:
        m.wait()
    meet()
    flows = [Gather(where, o, t, send.at[i], recv.at[i]) for i, (o, t) in enumerate(zip(owns, targets))]
    early, late = flows[:2], flows[2:]
    for f in early:
        f.begin_z()
    for f in early:
        f.begin_xy()
    same_document_flat(seg, bias)
    for slot in Gather.ORDER:
        for f in early:
            f.step(slot)
        if slot == 3:
            for f in late:
                f.begin_z()
    for f in late:
        f.begin_xy()
    for f in early:
        f.finish()
    mine[0].wait()
    keep = pltpu.make_async_copy(wall, wall_o, outs.at[5])
    keep.start()
    whole_vectors(vg, vec_o, wus.shape[0])
    hm_o[...] = jnp.full(hm_o.shape, LOW, F32)
    z_o[...] = x[...].astype(F32) + vec_o[OB:OB + 1, :]

    def put(g, i):
        src = (q_s, k_s, v_s, c_s)[i].at[g] if i < 4 else p_s.at[g]
        return pltpu.make_async_copy(src, (q_o, k_o, v_o, c_o, p_o)[i].at[g], outs.at[i])

    def group(g, _):
        cols = pl.ds(pl.multiple_of(g * GW, GW), GW)
        weight = lambda i: wall[i, :, :, cols].reshape(d, GW)
        xv = x[...]
        q_s[g] = (dot(xv, weight(0)) + vec_o[QB:QB + 1, cols]).astype(BF)
        k_s[g] = dot(xv, weight(1)).astype(BF)
        v_s[g] = (dot(xv, weight(2)) + vec_o[VB:VB + 1, cols]).astype(BF)

        def one_pair(it, _):
            pair_forward(g, it, lambda h, i: jnp.sum(rb[h].astype(F32)[i:i + 1, :], axis=1, keepdims=True).astype(jnp.int32),
                         q_s.at[g], k_s.at[g], v_s.at[g], p_s.at[g], c_s.at[g], hm_o, bias, s_s)
            for slot, when in LATE:
                @pl.when(g * steps + it == when)
                def _():
                    for f in late:
                        f.step(slot)
            return 0

        lax.fori_loop(0, steps, one_pair, 0)
        for i in range(5):
            put(g, i).start()
        return 0

    lax.fori_loop(0, groups, group, 0)
    wo = wall[3].reshape(d, d)
    for g in range(groups):
        z_o[...] += dot(c_s[g], wo[g * GW:(g + 1) * GW, :])
    done = [slot for slot, _ in LATE]
    for slot in Gather.ORDER:
        if slot not in done:
            for f in late:
                f.step(slot)
    for f in late:
        f.finish()
    mine[1].wait()
    mine[2].wait()
    for f in flows:
        f.drain()
    keep.wait()
    for g in range(groups):
        for i in range(5):
            put(g, i).wait()


def front(rb, x, seg, wq, wk, wv, wo, vpart, wis, wus, n):
    rows, d = x.shape
    groups = d // GW
    maps = (groups, rows, GW // HD * SEQ)
    sd = jax.ShapeDtypeStruct
    vm, hbm = pl.BlockSpec(memory_space=pltpu.VMEM), pl.BlockSpec(memory_space=pl.ANY)
    whole = lambda a: (n,) + a.shape
    four = (4, n) + wq.shape
    act = (groups, rows, GW)
    return pl.pallas_call(
        front_body,
        in_specs=[vm] * 3 + [hbm] * 4 + [vm] * 3,
        out_specs=[hbm] * 3 + [vm] + [hbm] * 5 + [vm] * 2,
        out_shape=[sd(four, BF), sd(whole(wis), BF), sd(whole(wus), BF), sd((16, d), F32),
                   sd(act, BF), sd(act, BF), sd(act, BF), sd(maps, BF), sd(act, BF),
                   sd((rows, d), F32), sd((16, 128), F32)],
        scratch_shapes=[pltpu.VMEM(four, BF), pltpu.VMEM(whole(vpart), F32),
                        pltpu.VMEM((rows // SEQ, SEQ, SEQ), F32), pltpu.VMEM((2, SEQ, SEQ), F32),
                        pltpu.VMEM(act, BF), pltpu.VMEM(act, BF), pltpu.VMEM(act, BF),
                        pltpu.VMEM(maps, BF), pltpu.VMEM(act, BF),
                        pltpu.SemaphoreType.DMA((4, 32)), pltpu.SemaphoreType.DMA((4, 32)),
                        pltpu.SemaphoreType.DMA((7,)), pltpu.SemaphoreType.DMA((6,))],
        compiler_params=pltpu.CompilerParams(collective_id=0, has_side_effects=True, vmem_limit_bytes=VMEM_MAX),
        name="front",
    )(rb, x, seg, wq, wk, wv, wo, vpart, wis, wus)


class Scatter:
    def __init__(self, where, grad, rp, r1, r2, rz, sems):
        self.where, self.grad, self.rp, self.r1, self.r2, self.rz, self.sems = where, grad, rp, r1, r2, rz, sems

    def remote(self, src, dst, slot, off):
        return pltpu.make_async_remote_copy(
            src_ref=src, dst_ref=dst, send_sem=self.sems.at[0, slot], recv_sem=self.sems.at[1, slot],
            device_id=(self.where[0] + off,), device_id_type=MESH_ID)

    def begin(self):
        me, fc, d1, d2, zs = self.where
        for a in (1, 0):
            for b in (1, 0):
                for k in range(4):
                    self.remote(unit_of(self.grad, me + fc + a * d2 + b * d1 + zs[k]), self.rp.at[a, b, k], a, fc).start()

    def pair(self, a):
        me, fc, d1, d2, zs = self.where
        self.remote(self.rp.at[a], self.rp.at[a], a, fc).wait_recv()
        for b in (1, 0):
            for k in range(4):
                held = unit_of(self.grad, me + a * d1 + b * d2 + zs[k])[...]
                self.rp[a, b, k] = held + self.rp[a, b, k]
            if a == 1:
                self.remote(self.rp.at[1, b], self.r1.at[b], 2 + b, d1).start()

    def first(self, b):
        me, fc, d1, d2, zs = self.where
        self.remote(self.rp.at[1, b], self.r1.at[b], 2 + b, d1).wait_recv()
        self.rp[0, b] = self.rp[0, b] + self.r1[b]
        if b == 1:
            self.remote(self.rp.at[0, 1], self.r2, 4, d2).start()

    def second(self):
        me, fc, d1, d2, zs = self.where
        self.remote(self.rp.at[0, 1], self.r2, 4, d2).wait_recv()
        for k in (1, 2, 3):
            self.rp[0, 0, k] = self.rp[0, 0, k] + self.r2[k]
            self.remote(self.rp.at[0, 0, k], self.rz.at[k - 1], 4 + k, zs[k]).start()

    def near(self):
        return self.rp[0, 0, 0].astype(F32) + self.r2[0].astype(F32)

    def far(self, k):
        self.remote(self.rp.at[0, 0, k], self.rz.at[k - 1], 4 + k, self.where[4][k]).wait_recv()
        return self.rz[k - 1].astype(F32)

    def last(self):
        return self.near() + self.far(1) + self.far(2) + self.far(3)

    def core_sent(self):
        for a in (1, 0):
            self.remote(self.rp.at[a], self.rp.at[a], a, self.where[1]).wait_send()

    def drain(self):
        me, fc, d1, d2, zs = self.where
        for b in (1, 0):
            self.remote(self.rp.at[1, b], self.r1.at[b], 2 + b, d1).wait_send()
        self.remote(self.rp.at[0, 1], self.r2, 4, d2).wait_send()
        for k in (1, 2, 3):
            self.remote(self.rp.at[0, 0, k], self.rz.at[k - 1], 4 + k, zs[k]).wait_send()


class Plane(Scatter):
    def __init__(self, k, *rest):
        Scatter.__init__(self, *rest)
        self.k = k

    def begin(self):
        me, fc, d1, d2, zs = self.where
        for a in (1, 0):
            for b in (1, 0):
                self.remote(self.grad.at[lax.rem(me, 8) + fc + a * d2 + b * d1], self.rp.at[a, b], a, fc).start()

    def pair(self, a):
        me, fc, d1, d2, zs = self.where
        self.remote(self.rp.at[a], self.rp.at[a], a, fc).wait_recv()
        for b in (1, 0):
            held = self.grad[lax.rem(me, 8) + a * d1 + b * d2]
            self.rp[a, b] = held + self.rp[a, b]
            if a == 1:
                self.remote(self.rp.at[1, b], self.r1.at[b], 2 + b, d1).start()

    def along(self):
        return self.remote(self.rp.at[0, 0], self.rz.at[self.k - 1], 4 + self.k, self.where[4][self.k])

    def second(self):
        self.remote(self.rp.at[0, 1], self.r2, 4, self.where[3]).wait_recv()
        if self.k:
            self.rp[0, 0] = self.rp[0, 0] + self.r2[...]
            self.along().start()

    def near(self):
        return self.rp[0, 0].astype(F32) + self.r2[...].astype(F32)

    def far(self):
        self.along().wait_recv()
        return self.rz[self.k - 1].astype(F32)

    def drain(self):
        me, fc, d1, d2, zs = self.where
        for b in (1, 0):
            self.remote(self.rp.at[1, b], self.r1.at[b], 2 + b, d1).wait_send()
        self.remote(self.rp.at[0, 1], self.r2, 4, d2).wait_send()
        if self.k:
            self.along().wait_send()


def scatter_buffers(lead, shape):
    return [pltpu.VMEM(lead + (2, 2, 4) + shape, BF), pltpu.VMEM(lead + (2, 4) + shape, BF),
            pltpu.VMEM(lead + (4,) + shape, BF), pltpu.VMEM(lead + (3,) + shape, BF)]


class Vectors:
    def __init__(self, where, held, got, sems):
        self.where, self.held, self.got, self.sems = where, held, got, sems

    def remote(self, src, slot, off):
        return pltpu.make_async_remote_copy(
            src_ref=self.held.at[src], dst_ref=self.got.at[slot], send_sem=self.sems.at[0, slot],
            recv_sem=self.sems.at[1, slot], device_id=(self.where[0] + off,), device_id_type=MESH_ID)

    def merge(self, a, b):
        row = lax.broadcasted_iota(jnp.int32, a.shape, 0)
        return jnp.where(row == TOP, jnp.maximum(a, b), a + b)

    def step(self, i):
        me, fc, d1, d2, zs = self.where
        offs = (fc, d1, d2)
        if i > 0:
            self.remote(i - 1, i - 1, offs[i - 1]).wait_recv()
            self.held[i] = self.merge(self.held[i - 1], self.got[i - 1])
        if i < 3:
            self.remote(i, i, offs[i]).start()
        else:
            for k in (1, 2, 3):
                self.remote(3, 2 + k, zs[k]).start()

    def last(self):
        me, fc, d1, d2, zs = self.where
        total = self.held[3]
        for k in (1, 2, 3):
            self.remote(3, 2 + k, zs[k]).wait_recv()
            total = self.merge(total, self.got[2 + k])
        for i, off in enumerate((fc, d1, d2)):
            self.remote(i, i, off).wait_send()
        for k in (1, 2, 3):
            self.remote(3, 2 + k, zs[k]).wait_send()
        return total


def rear_body(z_h, cot_h, wi_h, wu_h, x_h, wall_h, q_h, k_h, v_h, c_h, p_h, vecs, hm,
              out_h, dx_h, o_q, o_k, o_v, o_o, o_i, o_u, vout,
              wi, wu, ag, ds_s, dil_s, z, dx, fl, do, db, gu, gi, gg, held, got, usems, nsems, sems, vsems, isem, osem, *bufs):
    where = place()
    zi = where[0] // 8
    rows, d = z.shape
    ff = wi.shape[1]
    groups, n = gg.shape[0], gi.shape[1]
    rt, et = 512, 128
    k0, k1 = math.sqrt(2.0 / math.pi), 0.044715
    act, gp, small = ag.at[0], ag.at[1], held.at[0]
    row = lambda i: vecs[i:i + 1, :]
    part = lambda j: pl.ds(pl.multiple_of(j * d, d), d)
    beside = lambda k: (zi % 2 + k % 2 - 2 * (zi % 2) * (k % 2)) + 2 * (zi // 2 + k // 2 - 2 * (zi // 2) * (k // 2))

    def up_flow(it):
        k = (it + 1) % 4 if isinstance(it, int) else None
        return Plane(k, where, gu.at[lax.rem(it, 2)], bufs[0].at[it], bufs[1].at[it], bufs[2].at[it], bufs[3], usems.at[it])

    def in_flow(it):
        return Scatter(where, gi.at[lax.rem(it, 2)], *(b.at[it] for b in bufs[4:8]), nsems.at[it])

    small_flow = Vectors(where, held, got, vsems)
    out_flow = Scatter(where, gi.at[0], *bufs[8:12], sems.at[0])
    group_flow = [Scatter(where, gg.at[g], *bufs[12 + 4 * g:16 + 4 * g], sems.at[1 + g]) for g in range(groups)]

    def get_up(j):
        return pltpu.make_async_copy(wi_h.at[:, part(j)], wi.at[:, part(j)], isem.at[j])

    def get_down(j):
        return pltpu.make_async_copy(wu_h.at[part(j)], wu.at[part(j)], isem.at[4 + j])

    def get_wall(i):
        return pltpu.make_async_copy(wall_h.at[i], wi.at[:, pl.ds(i * d, d)], isem.at[i])

    def get_ctx(g):
        return pltpu.make_async_copy(c_h.at[g], fl.at[:, pl.ds(g * GW, GW)], isem.at[4 + g])

    get_z = pltpu.make_async_copy(z_h, z, isem.at[8])
    get_cot = pltpu.make_async_copy(cot_h, do, isem.at[9])
    get_x = pltpu.make_async_copy(x_h, do, isem.at[9])
    put_out = pltpu.make_async_copy(db, out_h, osem)
    put_dx = pltpu.make_async_copy(dx, dx_h, osem)
    mid_cols = pl.ds(0, GW // HD * SEQ)

    def get_group(g, i):
        cols = pl.ds(pl.multiple_of(g * GW, GW), GW)
        src = (v_h, q_h, k_h, p_h)[i].at[g]
        dst = wu.at[pl.ds((2, 0, 1)[i] * rows, rows), cols] if i < 3 else ag.at[lax.rem(g, 2), :, mid_cols]
        return pltpu.make_async_copy(src, dst, isem.at[10 + 4 * lax.rem(g, 2) + i])

    get_z.start()
    for j in range(ff // d):
        get_up(j).start()
        get_down(j).start()
    get_cot.start()
    greet(*where)
    small[...] = jnp.zeros(small.shape, F32)
    get_z.wait()

    def prep(i, _):
        r = pl.ds(pl.multiple_of(i * et, et), et)
        unit, _inv = unit_rows(z[r, :])
        first = unit * row(AG) + row(ASH)
        fl[r, :] = first.astype(BF)
        dx[r, :] = first + row(BO)
        return 0

    lax.fori_loop(0, rows // et, prep, 0)

    def up(j, _):
        c = part(j)
        get_up(j).wait()
        get_down(j).wait()
        for i in range(rows // rt):
            r = slice(i * rt, (i + 1) * rt)
            u = dot(fl[r, :], wi[:, c]) + vecs[pl.ds(BI + j, 1), :]
            u2 = u * u
            t = jnp.tanh(u * (k0 + (k0 * k1) * u2))
            h = 0.5 + 0.5 * t
            a = (u * h).astype(BF)
            act[r, c] = a
            gp[r, c] = (h + (0.5 * u) * (1.0 - t * t) * (k0 + (3.0 * k0 * k1) * u2)).astype(BF)
            dx[r, :] += dot(a, wu[c, :])
        return 0

    lax.fori_loop(0, ff // d, up, 0)
    get_cot.wait()

    def mid(i, _):
        r = pl.ds(pl.multiple_of(i * et, et), et)
        unit, inv = unit_rows(dx[r, :])
        db[r, :] = (unit * row(FG) + row(FS)).astype(BF)
        upv = do[r, :].astype(F32)
        small[FG:FG + 1, :] += col_sum(upv * unit)
        small[FS:FS + 1, :] += col_sum(upv)
        ds = norm_back(upv, unit, inv, row(FG))
        dsl = ds.astype(BF)
        do[r, :] = dsl
        dx[r, :] = ds
        small[BO:BO + 1, :] += col_sum(dsl.astype(F32))
        return 0

    lax.fori_loop(0, rows // et, mid, 0)
    put_out.start()
    meet()

    def down(it, _):
        j = beside((it + 1) % 4)
        c = part(j)
        slot = lax.rem(it, 2)

        @pl.when(it >= 2)
        def _():
            up_flow(it - 2).core_sent()

        gu[slot] = dot_tn(act[:, c], do[...]).astype(BF).reshape(gu.shape[1:])
        up_flow(it).begin()
        sums = None
        for i in range(rows // rt):
            r = slice(i * rt, (i + 1) * rt)
            di = dot_nt(do[r, :], wu[c, :]) * gp[r, c].astype(F32)
            dil = di.astype(BF)
            dil_s[r, :] = dil
            s = col_sum(dil.astype(F32))
            sums = s if sums is None else sums + s
            dx[r, :] += dot_nt(dil, wi[:, c])
            if i == 0:
                @pl.when(it >= 1)
                def _():
                    in_flow(it - 1).pair(1)
                    in_flow(it - 1).pair(0)
        small[pl.ds(BI + j, 1), :] = sums
        up_flow(it).pair(1)
        up_flow(it).pair(0)

        @pl.when(it >= 2)
        def _():
            in_flow(it - 2).core_sent()

        gi[slot] = dot_tn(fl[...], dil_s[...]).reshape(gi.shape[1:]).astype(BF)
        in_flow(it).begin()

        @pl.when(it >= 2)
        def _():
            for f in (up_flow(it - 2), in_flow(it - 2)):
                f.first(1)
                f.first(0)

        return 0

    lax.fori_loop(0, ff // d, down, 0)
    get_wall(3).start()
    for i in range(4):
        get_group(0, i).start()
    for g in range(groups):
        get_ctx(g).start()
    get_x.start()
    for i in range(3):
        get_wall(i).start()
    put_out.wait()

    def tail(i, _):
        r = pl.ds(pl.multiple_of(i * et, et), et)
        unit, inv = unit_rows(z[r, :])
        df = dx[r, :]
        small[AG:AG + 1, :] += col_sum(df * unit)
        small[ASH:ASH + 1, :] += col_sum(df)
        ds = norm_back(df, unit, inv, row(AG))
        dx[r, :] = ds
        dsl = ds.astype(BF)
        db[r, :] = dsl
        small[OB:OB + 1, :] += col_sum(dsl.astype(F32))
        return 0

    lax.fori_loop(0, rows // et, tail, 0)
    in_flow(3).pair(1)
    in_flow(3).pair(0)
    for g in range(groups):
        get_ctx(g).wait()
    in_flow(2).core_sent()
    gi[0] = dot_tn(fl[...], db[...]).reshape(gi.shape[1:]).astype(BF)
    out_flow.begin()
    get_wall(3).wait()

    steps = (rows // SEQ) * (GW // 128)
    edge = GW // HD * SEQ
    dc = act.at[:, pl.ds(edge, GW)]
    dp_s = [z.at[pl.ds(j * SEQ, SEQ), pl.ds(0, SEQ)] for j in range(2)]
    slopes = [ds_s.at[0], ds_s.at[1]]
    both = lambda f: [(f.first, 1), (f.first, 0)]
    g0, g1, g2 = group_flow
    events = {
        0: [(up_flow(0).second,), (in_flow(0).second,), (out_flow.pair, 1)],
        1: [(out_flow.pair, 0)] + both(up_flow(2)),
        2: both(in_flow(2)) + [(up_flow(1).second,)],
        3: [(in_flow(1).second,)],
        4: both(up_flow(3)),
        5: both(in_flow(3)) + [(g0.pair, 1)],
        6: [(g0.pair, 0), (up_flow(2).second,), (out_flow.first, 1)],
        7: [(out_flow.first, 0), (in_flow(2).second,)],
        8: [(up_flow(3).second,), (in_flow(3).second,), (g0.first, 1)],
        9: [(g0.first, 0), (g1.pair, 1)],
        10: [(g1.pair, 0), (out_flow.second,)],
        11: [(g0.second,), (g1.first, 1)],
    }

    def group(g, _):
        cols = pl.ds(pl.multiple_of(g * GW, GW), GW)
        for i in range(4):
            get_group(g, i).wait()

        @pl.when(g + 1 < groups)
        def _():
            for i in range(4):
                get_group(g + 1, i).start()

        dc[...] = dot_nt(db[...], wi[cols, 3 * d:4 * d]).astype(BF)
        heads = [wu.at[pl.ds(i * rows, rows), cols] for i in range(3)]

        def one_pair(it, _):
            pair_backward(it, *heads, ag.at[lax.rem(g, 2)], dc, *heads, dp_s, slopes)
            for when, todo in events.items():
                @pl.when(g * steps + it == when)
                def _():
                    for fn, *a in todo:
                        fn(*a)
            return 0

        lax.fori_loop(0, steps, one_pair, 0)

        @pl.when(g == 0)
        def _():
            get_x.wait()

        xv = do[...]
        for i, grad in enumerate(heads):
            gg[g, i] = dot_tn(xv, grad[...]).reshape(n, d // n, GW).astype(BF)
        for i in range(groups):
            @pl.when(g == i)
            def _():
                group_flow[i].begin()
        small[QB:QB + 1, cols] = col_sum(heads[0][...].astype(F32))
        small[VB:VB + 1, cols] = col_sum(heads[2][...].astype(F32))
        return 0

    lax.fori_loop(0, groups, group, 0)
    diag = lax.broadcasted_iota(jnp.int32, hm.shape, 0) == lax.broadcasted_iota(jnp.int32, hm.shape, 1)
    small[TOP:TOP + 1, 0:128] = jnp.sum(jnp.where(diag, hm[...], 0.0), axis=0, keepdims=True)
    small_flow.step(0)
    for i in range(3):
        get_wall(i).wait()
    quarter = rows // 4

    def inputs_part(t):
        grads = (wu[i * rows + t * quarter:i * rows + (t + 1) * quarter, :] for i in range(3))
        dx[t * quarter:(t + 1) * quarter, :] += sum(dot_nt(v, wi[:, i * d:(i + 1) * d]) for i, v in enumerate(grads))

    inputs_part(0)
    g2.pair(1)
    g2.pair(0)
    small_flow.step(1)
    inputs_part(1)
    g1.first(0)
    inputs_part(2)
    small_flow.step(2)
    g2.first(1)
    g1.second()
    g2.first(0)
    inputs_part(3)
    put_dx.start()
    small_flow.step(3)
    o_u[...] = up_flow(3).near() + up_flow(0).far() + up_flow(1).far() + up_flow(2).far()
    g2.second()
    for it in range(4):
        k = (it + 1) % 4
        total = in_flow(it).near()
        for m in (1, 2, 3):
            total = total + in_flow(((k ^ m) - 1) % 4).far(m)
        o_i[:, part(beside(k))] = total
    o_o[...] = out_flow.last()
    for g, f in enumerate(group_flow):
        t = f.last()
        for i, o in enumerate((o_q, o_k, o_v)):
            o[:, g * GW:(g + 1) * GW] = t[i]
    vout[...] = small_flow.last()
    put_dx.wait()
    up_flow(2).core_sent()
    up_flow(3).core_sent()
    in_flow(3).core_sent()
    for f in [out_flow] + group_flow:
        f.core_sent()
    for f in [up_flow(i) for i in range(4)] + [in_flow(i) for i in range(4)] + [out_flow] + group_flow:
        f.drain()


def rear(n, z, cot, wi, wu, x, wall, q, k, v, c, p, vecs, hm):
    rows, d = x.shape
    ff = wi.shape[1]
    groups = d // GW
    r, ru = d // n, ff // n
    sd = jax.ShapeDtypeStruct
    vm, hbm = pl.BlockSpec(memory_space=pltpu.VMEM), pl.BlockSpec(memory_space=pl.ANY)
    flat = pltpu.VMEM((rows, d), BF)
    bufs = [pltpu.VMEM((4, 2, 2, ru, d), BF), pltpu.VMEM((4, 2, ru, d), BF), pltpu.VMEM((4, ru, d), BF),
            pltpu.VMEM((3, ru, d), BF)]
    bufs += scatter_buffers((4,), (r, d)) + scatter_buffers((), (r, d))
    for _ in range(groups):
        bufs += scatter_buffers((), (3, r, GW))
    return pl.pallas_call(
        rear_body,
        in_specs=[hbm] * 11 + [vm] * 2,
        out_specs=[hbm] * 2 + [vm] * 7,
        out_shape=[sd((rows, d), BF), sd((rows, d), F32)] + [sd((r, d), F32)] * 4
        + [sd((r, ff), F32), sd((ru, d), F32), sd((16, d), F32)],
        scratch_shapes=[pltpu.VMEM((d, ff), BF), pltpu.VMEM((ff, d), BF), pltpu.VMEM((2, rows, ff), BF), pltpu.VMEM((2, SEQ, SEQ), BF), flat,
                        pltpu.VMEM((rows, d), F32), pltpu.VMEM((rows, d), F32), flat, flat, flat,
                        pltpu.VMEM((2, 8, ru, d), BF),
                        pltpu.VMEM((2, n, r, d), BF), pltpu.VMEM((groups, 3, n, r, GW), BF),
                        pltpu.VMEM((4, 16, d), F32), pltpu.VMEM((6, 16, d), F32),
                        pltpu.SemaphoreType.DMA((4, 2, 8)), pltpu.SemaphoreType.DMA((4, 2, 8)),
                        pltpu.SemaphoreType.DMA((1 + groups, 2, 8)), pltpu.SemaphoreType.DMA((2, 6)),
                        pltpu.SemaphoreType.DMA((18,)), pltpu.SemaphoreType.DMA] + bufs,
        compiler_params=pltpu.CompilerParams(collective_id=1, has_side_effects=True, vmem_limit_bytes=VMEM_MAX),
        name="rear",
    )(z, cot, wi, wu, x, wall, q, k, v, c, p, vecs, hm)


def attn_fwd_body(rb, x, segr, segc, wq, wk, wv, wo, vecs, q, k, v, p, c, z, hm, bias, s_s):
    g = pl.program_id(0)

    @pl.when(g == 0)
    def _():
        same_document(lambda s: segr[s:s + 1, :], lambda s, c: segc[s * SEQ + c * BLOCK:s * SEQ + (c + 1) * BLOCK, :], bias)
        hm[...] = jnp.full(hm.shape, LOW, F32)
        z[...] = x[...].astype(F32) + vecs[OB:OB + 1, :]

    cols = pl.ds(pl.multiple_of(g * GW, GW), GW)
    xv = x[...]
    q[...] = (dot(xv, wq[...]) + vecs[QB:QB + 1, cols]).astype(BF)
    k[...] = dot(xv, wk[...]).astype(BF)
    v[...] = (dot(xv, wv[...]) + vecs[VB:VB + 1, cols]).astype(BF)

    def one_pair(it, _):
        pair_forward(g, it, lambda h, i: rb[h * 18 + i * 3] + rb[h * 18 + i * 3 + 1] + rb[h * 18 + i * 3 + 2], q, k, v, p, c, hm, bias, s_s)
        return 0

    lax.fori_loop(0, x.shape[0] // SEQ * (GW // 128), one_pair, 0)
    z[...] += dot(c[...], wo[...])


def attn_fwd(rb, x, segr, segc, wall, vecs):
    rows, d = x.shape
    groups, seqs = d // GW, rows // SEQ
    keys = GW // HD * SEQ
    full = lambda shape: pl.BlockSpec(shape, lambda g, *_: (0,) * len(shape))
    col = lambda i: pl.BlockSpec((None, d, GW), lambda g, *_: (i, 0, g))
    act = pl.BlockSpec((None, rows, GW), lambda g, *_: (g, 0, 0))
    sd = jax.ShapeDtypeStruct
    return pl.pallas_call(
        attn_fwd_body,
        grid_spec=pltpu.PrefetchScalarGridSpec(
            num_scalar_prefetch=1, grid=(groups,),
            in_specs=[full((rows, d)), full((seqs, SEQ)), full((rows, 1)), col(0), col(1), col(2),
                      pl.BlockSpec((None, GW, d), lambda g, *_: (3, g, 0)), full((16, d))],
            out_specs=[act, act, act, pl.BlockSpec((None, rows, keys), lambda g, *_: (g, 0, 0)), act,
                       full((rows, d)), full((16, 128))],
            scratch_shapes=[pltpu.VMEM((seqs, SEQ, SEQ), F32), pltpu.VMEM((2, SEQ, SEQ), F32)]),
        out_shape=[sd((groups, rows, GW), BF)] * 3
        + [sd((groups, rows, keys), BF), sd((groups, rows, GW), BF), sd((rows, d), F32), sd((16, 128), F32)],
        compiler_params=pltpu.CompilerParams(vmem_limit_bytes=VMEM_MAX),
        name="attn_fwd",
    )(rb, x, segr, segc, wall, wall, wall, wall, vecs)


def attn_bwd_body(x, db, wq, wk, wv, wo, q, k, v, p, c, dsum, dw, dqb, dvb, dx, dc, dq, dk, dv, dp_s, ds_s):
    g = pl.program_id(0)

    @pl.when(g == 0)
    def _():
        dx[...] = dsum[...]

    dbv = db[...]
    cols = pl.ds(pl.multiple_of(g * GW, GW), GW)
    dc[...] = dot_nt(dbv, wo[...]).astype(BF)
    dw[3, cols, :] = dot_tn(c[...], dbv).astype(dw.dtype)

    def one_pair(it, _):
        pair_backward(it, q, k, v, p, dc, dq, dk, dv, [dp_s.at[0], dp_s.at[1]], [ds_s.at[0], ds_s.at[1]])
        return 0

    lax.fori_loop(0, x.shape[0] // SEQ * (GW // 128), one_pair, 0)
    dqb[...] = col_sum(dq[...].astype(F32))
    dvb[...] = col_sum(dv[...].astype(F32))
    xv = x[...]
    for i, part in enumerate((dq, dk, dv)):
        dw[i, :, cols] = dot_tn(xv, part[...]).astype(dw.dtype)
    dx[...] += dot_nt(dq[...], wq[...]) + dot_nt(dk[...], wk[...]) + dot_nt(dv[...], wv[...])


def attn_bwd(x, db, wall, q, k, v, p, c, dsum, gdt):
    rows, d = x.shape
    groups = d // GW
    keys = GW // HD * SEQ
    full = lambda shape: pl.BlockSpec(shape, lambda g: (0,) * len(shape), pipeline_mode=pl.Buffered(1))
    col = lambda i: pl.BlockSpec((None, d, GW), lambda g: (i, 0, g))
    vec = pl.BlockSpec((1, GW), lambda g: (0, g))
    act = pl.BlockSpec((None, rows, GW), lambda g: (g, 0, 0))
    sd = jax.ShapeDtypeStruct
    return pl.pallas_call(
        attn_bwd_body,
        grid=(groups,),
        in_specs=[full((rows, d)), full((rows, d)), col(0), col(1), col(2),
                  pl.BlockSpec((None, GW, d), lambda g: (3, g, 0)), act, act, act,
                  pl.BlockSpec((None, rows, keys), lambda g: (g, 0, 0)), act, full((rows, d))],
        out_specs=[full((4, d, d)), vec, vec, full((rows, d))],
        out_shape=[sd((4, d, d), gdt)] + [sd((1, d), F32)] * 2 + [sd((rows, d), F32)],
        scratch_shapes=[pltpu.VMEM((rows, GW), BF)] * 4
        + [pltpu.VMEM((2, SEQ, SEQ), F32), pltpu.VMEM((2, SEQ, SEQ), BF)],
        compiler_params=pltpu.CompilerParams(vmem_limit_bytes=VMEM_MAX),
        name="attn_bwd",
    )(x, db, wall, wall, wall, wall, q, k, v, p, c, dsum)


def far_layer(me, n, random_blocks, tokens, segment_ids, cot, weights, vecs, inner_weight, inner_bias, outer_weight, limit):
    d, ff = tokens.shape[1], inner_weight.shape[1]
    heads, part, wide = random_blocks.shape[0], vecs[0].shape[0], inner_bias.shape[0]
    wall = lax.all_gather(jnp.stack(weights), "dp", axis=1, tiled=True)
    wi, wu = (lax.all_gather(a, "dp", axis=0, tiled=True) for a in (inner_weight, outer_weight))
    vecs = lax.psum(vectors_part(me, n, vecs, inner_bias).astype(F32), "dp")
    q, k, v, p, c, z, hm = attn_fwd(random_blocks.reshape(-1), tokens, segment_ids.reshape(-1, SEQ),
                                    segment_ids.reshape(-1, 1), wall, vecs)
    out, dsum, db, dwi, dwu, small = ffn(z, cot, wi, wu, vecs, F32)
    dwall, dqb, dvb, dx = attn_bwd(tokens, db, wall, q, k, v, p, c, dsum, F32)
    mine = small.at[QB:QB + 1].set(dqb).at[VB:VB + 1].set(dvb).at[TOP, :hm.shape[0]].set(hm[:, 0])
    scatter = lambda a, at: lax.psum_scatter(a, "dp", scatter_dimension=at, tiled=True)
    dwu, dwi, dwall = scatter(dwu, 0), scatter(dwi, 0), scatter(dwall, 1)
    row = lax.broadcasted_iota(jnp.int32, mine.shape, 0)
    total = jnp.where(row == TOP, lax.pmax(mine, "dp"), lax.psum(mine, "dp"))
    vec8 = lax.dynamic_slice(total, (0, me * part), (8, part))
    dbi = lax.dynamic_slice(total[BI:BI + ff // d].reshape(-1), (me * wide,), (wide,))
    head_maxima = total[TOP, :heads]
    factor = jnp.sqrt(jnp.minimum(1.0, limit[0].astype(F32) / jnp.maximum(head_maxima, 1.0)))
    columns = jnp.repeat(factor, HD)[None, :]
    cq, ck = ((w.astype(F32) * columns).astype(BF) for w in weights[:2])
    return out, dx, dwall[0], dwall[1], dwall[2], dwall[3], dwi, dwu, [vec8[i] for i in range(8)], dbi, cq, ck, head_maxima


def near_layer(me, n, random_blocks, tokens, segment_ids, cot, weights, vecs, inner_weight, inner_bias, outer_weight, limit):
    d, ff = tokens.shape[1], inner_weight.shape[1]
    heads, part, wide = random_blocks.shape[0], vecs[0].shape[0], inner_bias.shape[0]
    pieces = jnp.concatenate([jnp.pad(jnp.stack(vecs), ((0, 0), (0, 128 - part))),
                              jnp.pad(inner_bias[None, :], ((0, 7), (0, 128 - wide)))]).astype(F32)
    wall, wi, wu, vec, q, k, v, p, c, z, hm = front(random_blocks, tokens, segment_ids.reshape(-1, 128), *weights, pieces,
                                                    inner_weight, outer_weight, n)
    raw = rear(n, z, cot, wi.reshape(d, ff), wu.reshape(ff, d), tokens, wall.reshape(4, d, d), q, k, v, c, p, vec, hm)
    out, dx, dwq, dwk, dwv, dwo, dwi, dwu, cq, ck, *fins = finish(n, heads, limit, weights[0], weights[1], *raw)
    fins = [a.reshape(-1) for a in fins]
    return out, dx, dwq, dwk, dwv, dwo, dwi, dwu, fins[:8], fins[8], cq, ck, fins[9]


def finish_body(n, heads, limit, wq, wk, total, *refs):
    count = 8
    srcs, dsts, refs = refs[:count], refs[count:2 * count], refs[2 * count:]
    (cq, ck), fins, held, sems = refs[:2], refs[2:12], refs[12:-1], refs[-1]
    jobs = []
    for src, dst, tmp in zip(srcs, dsts, held):
        cut = 8 if src.shape[0] >= 512 else 1
        step = src.shape[0] // cut
        for i in range(cut):
            at = pl.ds(i * step, step)
            slot = len(jobs)
            jobs.append((pltpu.make_async_copy(src.at[at], tmp.at[at], sems.at[0, slot]),
                         pltpu.make_async_copy(tmp.at[at], dst.at[at], sems.at[1, slot])))
    for get, _ in jobs:
        get.start()
    me = lax.axis_index("dp")
    d = total.shape[1]
    part, wide = d // n, held[7].shape[0]
    top = total[TOP:TOP + 1, 0:128]
    head = lax.broadcasted_iota(jnp.int32, (1, d), 1) // HD
    columns = jnp.zeros((1, d), F32)
    for h in range(heads):
        columns = jnp.where(head == h, top[:, h:h + 1], columns)
    factor = jnp.sqrt(jnp.minimum(1.0, limit[0].astype(F32) / jnp.maximum(columns, 1.0)))
    cq[...] = (wq[...].astype(F32) * factor).astype(BF)
    ck[...] = (wk[...].astype(F32) * factor).astype(BF)
    mine = pltpu.roll(total[0:8, :], d - me * part, 1)
    for i in range(8):
        fins[i][...] = mine[i:i + 1, 0:part]
    per = d // wide
    inner = jnp.broadcast_to(total[pl.ds(BI + me // per, 1), :], (8, d))
    fins[8][...] = pltpu.roll(inner, d - (me % per) * wide, 1)[0:1, 0:wide]
    fins[9][...] = top[:, 0:heads]
    for get, put in jobs:
        get.wait()
        put.start()
    for _, put in jobs:
        put.wait()


def finish(n, heads, limit, wq, wk, *raw):
    mats, total = raw[:8], raw[8]
    vm, hbm = pl.BlockSpec(memory_space=pltpu.VMEM), pl.BlockSpec(memory_space=pl.ANY)
    sd = jax.ShapeDtypeStruct
    return pl.pallas_call(
        partial(finish_body, n, heads),
        in_specs=[pl.BlockSpec(memory_space=pltpu.SMEM)] + [vm] * 3 + [hbm] * 8,
        out_specs=[hbm] * 8 + [vm] * 12,
        out_shape=[sd(a.shape, a.dtype) for a in mats] + [sd(wq.shape, BF)] * 2 + [sd((1, mats[2].shape[0]), F32)] * 8
        + [sd((1, mats[7].shape[0]), F32), sd((1, heads), F32)],
        scratch_shapes=[pltpu.VMEM(a.shape, a.dtype) for a in mats] + [pltpu.SemaphoreType.DMA((2, 24))],
        compiler_params=pltpu.CompilerParams(vmem_limit_bytes=VMEM_MAX),
        name="finish",
    )(limit, wq, wk, total, *mats)


def vectors_part(me, n, vecs, inner_bias):
    part = vecs[0].shape[0]
    d = part * n
    rows = jnp.tile(jnp.stack(vecs), (1, n))
    rows = jnp.where(lax.broadcasted_iota(jnp.int32, rows.shape, 1) // part == me, rows, 0)
    flat = jnp.tile(inner_bias, n)
    flat = jnp.where(lax.broadcasted_iota(jnp.int32, flat.shape, 0) // inner_bias.shape[0] == me, flat, 0)
    flat = flat.reshape(-1, d)
    rest = jnp.zeros((16 - rows.shape[0] - flat.shape[0], d), BF)
    return jnp.concatenate([rows, flat, rest], axis=0)


def per_device(n, tokens, segment_ids, random_blocks, clip_limit, query_weight, query_bias, key_weight, value_weight,
               value_bias, output_weight, output_bias, attn_gain, attn_shift, inner_weight, inner_bias,
               outer_weight, outer_bias, final_gain, final_shift, out_cotangent):
    rows, d = tokens.shape
    near = n == 32 and (rows, d, inner_weight.shape[1]) == (2 * SEQ, 3 * GW, 6 * SEQ)
    weights = (query_weight, key_weight, value_weight, output_weight)
    vecs = (query_bias, value_bias, output_bias, attn_gain, attn_shift, outer_bias, final_gain, final_shift)
    out, dx, dwq, dwk, dwv, dwo, dwi, dwu, vec8, dbi, cq, ck, head_maxima = (near_layer if near else far_layer)(
        lax.axis_index("dp"), n, random_blocks, tokens, segment_ids, out_cotangent, weights, vecs, inner_weight, inner_bias,
        outer_weight, clip_limit)
    dqb, dvb, dob, dag, dash, dbo, dfg, dfs = vec8
    return (out, dx, dwq, dqb, dwk, dwv, dvb, dwo, dob, dag, dash, dwi, dbi, dwu, dbo, dfg, dfs, cq, ck, head_maxima)


def solution(mesh):
    mat, vec, rep = P("dp", None), P("dp"), P()
    in_specs = (mat, vec, rep, rep, mat, vec, mat, mat, vec, mat, vec, vec, vec, mat, vec, mat, vec, vec, vec, mat)
    out_specs = (mat, mat, mat, vec, mat, mat, vec, mat, vec, vec, vec, mat, vec, mat, vec, vec, vec, mat, mat, rep)
    return jax.shard_map(partial(per_device, mesh.shape["dp"]), mesh=mesh, in_specs=in_specs, out_specs=out_specs,
                         check_vma=False)
```
